32 devices in a mesh: row: 4 (over y, core), col: 4 (over z), feat: 2 (over x).
Axes of the slice: x: 2, y: 2, z: 4, core: 2. Of those that a mesh axis runs over, the one named last changes fastest.
Arguments:
- src_feats: bfloat16 [8192, 256], P(('row', 'col'), 'feat'), may hold values from -170 to 170
- dst_feats: bfloat16 [1024, 256], P(('row', 'col'), 'feat'), may hold values from -170 to 170
- proj: bfloat16 [256, 256], P('feat'), may hold values from -0.375 to 0.375
- att_src: float32 [256], P('feat'), may hold values from -1 to 1
- att_dst: float32 [256], P('feat'), may hold values from -1 to 1
- bias: float32 [256], P('feat'), may hold values from -3 to 3
- tile_rows: int32 [4, 4, 128], P('row', 'col'), may hold values from 0 to 1, as said below
- tile_cols: int32 [4, 4, 128], P('row', 'col'), may hold values from 0 to 15
- tile_count: int32 [4, 4], P('row', 'col'), may hold values from 16 to 128, as said below
- edge_weight: bfloat16 [4, 4, 128, 128, 128], P('row', 'col'), may hold values from 0 to 3, as said below
Outputs:
- node_out: bfloat16 [1024, 256], P(('row', 'col'), 'feat')
The draws below stay inside these ranges and needn't reach their ends.
Inputs may be any that keep to these rules, and one draw needn't show every extreme that they name: `tile_count`: one device holds exactly 128 live slots in every draw; counts differ several times between devices. `tile_rows`: the slots of one device name distinct tiles as long as there are tiles left in its block, then name the same tiles again in the same order; slots beyond the count also hold valid tile numbers. `edge_weight`: about a third of the entries are edges.
All inputs are finite; a program needn't handle non-finite values.
Results may differ from the reference program's by a relative error of at most 0.001.
Values sent between devices are 32-bit elements; how exact they have to be, the bound alone decides.
No kernel may reach another device: no remote copies, remote signals or barrier semaphores. Data moves between devices by JAX's collectives and lax.ppermute only.
A program may use at most 64 MiB of HBM per device.

```python
import math
import jax
import jax.numpy as jnp
from jax import lax

HEADS = 8
D = 256
DIN = 256
TILE = 128
GROUP = 4
RDEV = 64
SPIECE = 512
TMAX = 128
RTILES = 2
CTILES = 16
NDST = 1024
NSRC = 8192
N_ROW = 4
N_COL = 4


def feature_draw(key, count):
    key_base = jax.random.fold_in(key, 0)
    values = jnp.clip(jax.random.normal(key_base, (count, DIN), jnp.float32), -4.0, 4.0)
    return values.astype(jnp.bfloat16)


def draw_src_feats(key, part):
    return feature_draw(jax.random.fold_in(key, 101), NSRC)


def draw_dst_feats(key, part):
    return feature_draw(jax.random.fold_in(key, 202), NDST)


def tile_plan(key):
    base = jax.random.fold_in(key, 4211)
    key_level, key_pick, key_perm = jax.random.split(base, 3)
    device_total = N_ROW * N_COL
    levels = jax.random.randint(key_level, (device_total,), 0, 4)
    counts = jnp.maximum(jnp.right_shift(jnp.full((device_total,), TMAX, jnp.int32), levels), 1)
    chosen = jax.random.randint(key_pick, (), 0, device_total)
    counts = jnp.where(jnp.arange(device_total) == chosen, TMAX, counts)
    perm_keys = jax.random.split(key_perm, device_total)
    slot_order = jnp.arange(TMAX, dtype=jnp.int32) % (RTILES * CTILES)
    picks = jax.vmap(lambda each_key: jax.random.permutation(each_key, RTILES * CTILES)[slot_order])(perm_keys)
    picks = picks.astype(jnp.int32)
    tile_row = (picks // CTILES).reshape(N_ROW, N_COL, TMAX)
    tile_col = (picks % CTILES).reshape(N_ROW, N_COL, TMAX)
    return (counts.reshape(N_ROW, N_COL).astype(jnp.int32), tile_row.astype(jnp.int32), tile_col.astype(jnp.int32))


def draw_tile_count(key, part):
    return tile_plan(key)[0]


def draw_tile_rows(key, part):
    return tile_plan(key)[1]


def draw_tile_cols(key, part):
    return tile_plan(key)[2]


def draw_edge_weight(key, part):
    shape = (N_ROW, N_COL, TMAX, TILE, TILE)
    key_keep, key_value = jax.random.split(jax.random.fold_in(key, 303))
    present = jax.random.uniform(key_keep, shape, jnp.float32) < 0.35
    values = jnp.exp(jax.random.uniform(key_value, shape, jnp.float32, math.log(0.3), math.log(3.0)))
    return jnp.where(present, values, 0.0).astype(jnp.bfloat16)


def block_levels(own_key, shape, shards, low, largest):
    def one(position, parts):
        steps = jax.random.uniform(jax.random.fold_in(jax.random.fold_in(own_key, 6), position), (parts,), jnp.float32, low / len(shards), largest / len(shards))
        return jnp.repeat(jnp.exp(steps), shape[position] // parts).reshape((-1,) + (1,) * (len(shape) - position - 1))

    loudness = one(*shards[0])
    for cut in shards[1:]:
        loudness = loudness * one(*cut)
    return loudness


def scatter_about(stream_key, shape, scale, bound, shards=(), kind=jnp.bfloat16):
    array = scale * jax.random.normal(stream_key, shape, jnp.float32)
    if shards:
        array = array * block_levels(stream_key, shape, shards, -0.22, 0.18)
    return jnp.clip(array, -bound, bound).astype(kind)


def setup_inputs(seed: int = 0) -> dict:
    streams_of = jax.random.split(jax.random.key(seed), 11)
    src_feats = draw_src_feats(jax.random.fold_in(streams_of[10], 71), 0)
    dst_feats = draw_dst_feats(jax.random.fold_in(streams_of[10], 71), 0)
    proj = scatter_about(streams_of[2], (DIN, D), DIN ** -0.5, 0.375, ((0, 2),))
    att_src = scatter_about(streams_of[3], (D,), (D // HEADS) ** -0.5, 1.0, ((0, 2),), jnp.float32)
    att_dst = scatter_about(streams_of[4], (D,), (D // HEADS) ** -0.5, 1.0, ((0, 2),), jnp.float32)
    bias = scatter_about(streams_of[5], (D,), 0.5, 3.0, ((0, 2),), jnp.float32)
    tile_rows = draw_tile_rows(jax.random.fold_in(streams_of[10], 71), 0)
    tile_cols = draw_tile_cols(jax.random.fold_in(streams_of[10], 71), 0)
    tile_count = draw_tile_count(jax.random.fold_in(streams_of[10], 71), 0)
    edge_weight = draw_edge_weight(jax.random.fold_in(streams_of[10], 71), 0)
    return dict(src_feats=src_feats, dst_feats=dst_feats, proj=proj, att_src=att_src, att_dst=att_dst, bias=bias, tile_rows=tile_rows, tile_cols=tile_cols, tile_count=tile_count, edge_weight=edge_weight)


def leaky_relu(values):
    return jnp.where(values > 0, values, 0.2 * values)


def head_sum(projected, vector, dims):
    return (projected * vector).reshape(projected.shape[0], -1, dims).sum(2)


def reference(src_feats, dst_feats, proj, att_src, att_dst, bias, tile_rows, tile_cols, tile_count, edge_weight):
    dims = D // HEADS
    zsrc = jnp.dot(src_feats, proj, preferred_element_type=jnp.float32)
    zdst = jnp.dot(dst_feats, proj, preferred_element_type=jnp.float32)
    s_src = head_sum(zsrc, att_src, dims)
    s_dst = head_sum(zdst, att_dst, dims)
    s_self = head_sum(zdst, att_src, dims)
    col_block = SPIECE * N_ROW
    col_tiles = col_block // TILE
    row_block = RDEV * N_COL
    row_tiles = row_block // TILE
    z_cols = zsrc.reshape(N_ROW, N_COL, SPIECE, D).transpose(1, 0, 2, 3).reshape(N_COL, col_tiles, TILE, HEADS, dims)
    s_cols = s_src.reshape(N_ROW, N_COL, SPIECE, HEADS).transpose(1, 0, 2, 3).reshape(N_COL, col_tiles, TILE, HEADS).transpose(0, 1, 3, 2)
    t_rows = s_dst.reshape(N_ROW, row_tiles, TILE, HEADS).transpose(0, 1, 3, 2)
    live_all = (jnp.arange(TMAX, dtype=jnp.int32)[None, None, :] < tile_count[:, :, None]).astype(jnp.float32)
    groups = N_COL * TMAX // GROUP
    block_of = (jnp.arange(groups, dtype=jnp.int32) * GROUP // TMAX).astype(jnp.int32)

    def per_block(block_r):
        row_ids = tile_rows[block_r].reshape(groups, GROUP)
        col_ids = tile_cols[block_r].reshape(groups, GROUP)
        weights = edge_weight[block_r].reshape(groups, GROUP, TILE, TILE)
        alive = live_all[block_r].reshape(groups, GROUP)
        target = t_rows[block_r]

        def masked_scores(row_g, col_g, col_b, weight_g, alive_g):
            weight_f = weight_g.astype(jnp.float32) * alive_g[:, None, None]
            scores = target[row_g][:, :, :, None] + s_cols[col_b][col_g][:, :, None, :]
            return jnp.where(weight_f[:, None] > 0, leaky_relu(scores), jnp.float32(-1e30)), weight_f

        def max_step(running, inputs):
            row_g, col_g, col_b, weight_g, alive_g = inputs
            masked, weight_f = masked_scores(row_g, col_g, col_b, weight_g, alive_g)
            return running.at[row_g].max(masked.max(-1)), None

        start_max = jnp.full((row_tiles, HEADS, TILE), -1e30, jnp.float32)
        row_max, _ = lax.scan(max_step, start_max, (row_ids, col_ids, block_of, weights, alive))

        def sum_step(carry, inputs):
            total, accum = carry
            row_g, col_g, col_b, weight_g, alive_g = inputs
            masked, weight_f = masked_scores(row_g, col_g, col_b, weight_g, alive_g)
            probs = weight_f[:, None] * jnp.exp(masked - row_max[row_g][:, :, :, None])
            total = total.at[row_g].add(probs.sum(-1))
            gathered = z_cols[col_b][col_g]
            contrib = jnp.einsum("ghij,gjhd->gihd", probs, gathered, precision=lax.Precision.HIGHEST)
            return (total, accum.at[row_g].add(contrib)), None

        start_sum = (jnp.zeros((row_tiles, HEADS, TILE), jnp.float32), jnp.zeros((row_tiles, TILE, HEADS, dims), jnp.float32))
        (total, accum), _ = lax.scan(sum_step, start_sum, (row_ids, col_ids, block_of, weights, alive))
        return row_max, total, accum

    row_max, total, accum = lax.map(per_block, jnp.arange(N_ROW, dtype=jnp.int32))
    row_max = row_max.transpose(0, 1, 3, 2).reshape(N_ROW * row_block, HEADS)
    total = total.transpose(0, 1, 3, 2).reshape(N_ROW * row_block, HEADS)
    accum = accum.reshape(N_ROW * row_block, HEADS, dims)
    e_self = leaky_relu(s_dst + s_self)
    final_max = jnp.maximum(row_max, e_self)
    factor = jnp.exp(row_max - final_max)
    self_factor = jnp.exp(e_self - final_max)
    denom = total * factor + self_factor
    numer = accum * factor[:, :, None] + zdst.reshape(-1, HEADS, dims) * self_factor[:, :, None]
    mixed = (numer / denom[:, :, None]).reshape(-1, D) + bias
    return jax.nn.elu(mixed).astype(jnp.bfloat16)
```

```python
import jax
import jax.numpy as jnp
from jax import lax
from jax.experimental import pallas as pl
from jax.experimental.pallas import tpu as pltpu
from jax.sharding import PartitionSpec as P

HEADS = 8
TILE = 128
SLOPE = 0.2
LOG2E = 1.4426950408889634
NEG = -1e30
F32 = jnp.float32
BF16 = jnp.bfloat16
HIGHEST = lax.Precision.HIGHEST
VMEM = pl.BlockSpec(memory_space=pltpu.VMEM)
SMEM = pl.BlockSpec(memory_space=pltpu.SMEM)


def is_pow2(n):
    return n & (n - 1) == 0


def goes_to(i, d, n):
    return i ^ d if is_pow2(n) else lax.rem(i + d, n)


def comes_from(i, d, n):
    return i ^ d if is_pow2(n) else lax.rem(i + n - d, n)


def hop(x, axis, d):
    n = lax.axis_size(axis)
    pairs = [(i, i ^ d if is_pow2(n) else (i + d) % n) for i in range(n)]
    return lax.ppermute(x, axis, pairs)


def call(kernel, out_shape, *args, in_specs=None, flops=0, bytes_accessed=0, **kw):
    return pl.pallas_call(
        kernel,
        out_shape=out_shape,
        in_specs=in_specs or [VMEM] * len(args),
        cost_estimate=pl.CostEstimate(
            flops=flops, bytes_accessed=bytes_accessed, transcendentals=0
        ),
        **kw,
    )(*args)


def up8(n):
    return -(-n // 8) * 8


def head_rows(vector, heads, width):
    dims = width // heads
    shape = (up8(heads), width)
    row = lax.broadcasted_iota(jnp.int32, shape, 0)
    lane = lax.broadcasted_iota(jnp.int32, shape, 1)
    return jnp.where(lane // dims == row, jnp.broadcast_to(vector, shape), 0.0)


def contract(lhs, rhs, dims, precision=HIGHEST):
    return lax.dot_general(
        lhs, rhs, (dims, ((), ())), preferred_element_type=F32, precision=precision
    )


def take_cols(proj_ref, which, width):
    if width % TILE == 0:
        return proj_ref[:, pl.ds(pl.multiple_of(which * width, width), width)]
    full = proj_ref[...]
    out = full[:, :width]
    for k in range(1, full.shape[1] // width):
        out = jnp.where(which == k, full[:, k * width : (k + 1) * width], out)
    return out


def project(x, w):
    return lax.dot_general(x, w, (((1,), (0,)), ((), ())), preferred_element_type=F32)


def leaky(x):
    return jnp.maximum(x, SLOPE * x)


def on_device(
    src_feats, dst_feats, proj, att_src, att_dst, bias, tile_rows, tile_cols, tile_count, edge_weight
):
    n_row, n_col, n_feat = (lax.axis_size(a) for a in ("row", "col", "feat"))
    width = proj.shape[1] // n_feat
    heads = HEADS // n_feat
    dims = width // heads
    lanes = -(-width // TILE) * TILE
    src_rows, own_rows = src_feats.shape[0], dst_feats.shape[0]
    slots = tile_rows.shape[2]
    row_tiles = own_rows * n_col // TILE
    piece_tiles = src_rows // TILE
    col_tiles = piece_tiles * n_row
    per_tile = TILE // own_rows
    hp = up8(heads)
    mdp = up8(2 * heads)
    att_src2, att_dst2, bias2 = (v.reshape(1, width) for v in (att_src, att_dst, bias))

    def send_kernel(dst_ref, src_ref, proj_ref, *outs):
        me = lax.axis_index("feat")
        for d in range(1, n_feat):
            w = take_cols(proj_ref, goes_to(me, d, n_feat), width)
            outs[2 * d - 2][...] = project(dst_ref[...], w)
            outs[2 * d - 1][...] = project(src_ref[...], w)

    sent = call(
        send_kernel,
        [
            jax.ShapeDtypeStruct((n, width), F32)
            for _ in range(1, n_feat)
            for n in (own_rows, src_rows)
        ],
        dst_feats,
        src_feats,
        proj,
    )
    dst_parts = [hop(sent[2 * d - 2], "feat", d) for d in range(1, n_feat)]
    src_parts = [hop(sent[2 * d - 1], "feat", d) for d in range(1, n_feat)]

    group = 16

    def weight_kernel(rows_ref, cols_ref, count_ref, w_ref, panel_ref):
        step = pl.program_id(0)

        @pl.when(step == 0)
        def _():
            @pl.loop(0, row_tiles * col_tiles)
            def _(t):
                panel_ref[t // col_tiles, t % col_tiles] = jnp.zeros((TILE, TILE), F32)

        base = step * group
        live = jnp.clip(count_ref[0, 0] - base, 0, group)

        @pl.loop(0, live)
        def _(t):
            r, c = rows_ref[0, 0, base + t], cols_ref[0, 0, base + t]
            panel_ref[r, c] = panel_ref[r, c] + w_ref[0, 0, t].astype(F32)

    panel = pl.pallas_call(
        weight_kernel,
        out_shape=jax.ShapeDtypeStruct((row_tiles, col_tiles, TILE, TILE), F32),
        grid=(slots // group,),
        in_specs=[
            SMEM,
            SMEM,
            SMEM,
            pl.BlockSpec((1, 1, group, TILE, TILE), lambda s: (0, 0, s, 0, 0)),
        ],
        out_specs=pl.BlockSpec(
            (row_tiles, col_tiles, TILE, TILE), lambda s: (0, 0, 0, 0)
        ),
        cost_estimate=pl.CostEstimate(
            flops=slots * TILE * TILE, bytes_accessed=slots * TILE * TILE * 2, transcendentals=0
        ),
    )(tile_rows, tile_cols, tile_count, edge_weight)

    def dst_kernel(dst_ref, proj_ref, att_ref, *rest):
        parts, (z_ref, s_ref) = rest[: n_feat - 1], rest[n_feat - 1 :]
        z = project(dst_ref[...], take_cols(proj_ref, lax.axis_index("feat"), width))
        for part in parts:
            z = z + part[...]
        z_ref[...] = z
        s_ref[...] = LOG2E * contract(head_rows(att_ref[...], heads, width), z, ((1,), (1,)))

    zdst, s_dst = call(
        dst_kernel,
        [
            jax.ShapeDtypeStruct((own_rows, width), F32),
            jax.ShapeDtypeStruct((hp, own_rows), F32),
        ],
        dst_feats,
        proj,
        att_dst2,
        *dst_parts,
    )
    targets = [s_dst] + [hop(s_dst, "col", d) for d in range(1, n_col)]

    pack_rows = src_rows + piece_tiles * hp

    def src_kernel(src_ref, proj_ref, att_ref, *rest):
        parts, out_ref = rest[: n_feat - 1], rest[n_feat - 1]
        z = project(src_ref[...], take_cols(proj_ref, lax.axis_index("feat"), width))
        for part in parts:
            z = z + part[...]
        if width < lanes:
            out_ref[...] = jnp.zeros_like(out_ref)
        out_ref[:src_rows, :width] = z
        s = LOG2E * contract(head_rows(att_ref[...], heads, width), z, ((1,), (1,)))
        for t in range(piece_tiles):
            at = src_rows + t * hp
            out_ref[at : at + hp, :TILE] = s[:, t * TILE : (t + 1) * TILE]

    own_piece = call(
        src_kernel,
        jax.ShapeDtypeStruct((pack_rows, lanes), F32),
        src_feats,
        proj,
        att_src2,
        *src_parts,
    )
    pieces = {0: own_piece}
    d = n_row // 2
    while d:
        for k in list(pieces):
            pieces[k ^ d] = hop(pieces[k], "row", d)
        d //= 2
    pieces = [pieces[k] for k in range(n_row)]

    block = 32
    chunk_rows = own_rows + mdp

    def att_kernel(*refs):
        tgt_refs, refs = refs[:n_col], refs[n_col:]
        piece_refs, refs = refs[:n_row], refs[n_row:]
        w_ref, refs = refs[0], refs[1:]
        out_refs, (tgt, z_cat, probs, den_s, m_s, done) = refs[:n_col], refs[n_col:]
        rt = pl.program_id(0)
        row, col = lax.axis_index("row"), lax.axis_index("col")

        @pl.when(rt == 0)
        def _():
            eye = (
                lax.broadcasted_iota(jnp.int32, (hp, TILE), 0)
                == lax.broadcasted_iota(jnp.int32, (hp, TILE), 1)
            ).astype(F32)
            for d in range(n_col):
                at = pl.multiple_of(comes_from(col, d, n_col) * own_rows, own_rows)
                tgt[pl.ds(at, own_rows), :] = contract(tgt_refs[d][...], eye, ((0,), (0,)))
            for k in range(n_row):
                z = piece_refs[k][:src_rows, :width]
                hi = z.astype(BF16)
                z_cat[k * src_rows : (k + 1) * src_rows, :width] = hi
                z_cat[k * src_rows : (k + 1) * src_rows, width:] = (z - hi.astype(F32)).astype(BF16)

        def score_row(q, h):
            k, t = divmod(q, piece_tiles)
            at = src_rows + t * hp + h
            return piece_refs[k][at : at + 1, :TILE]

        def weight(q, i0):
            k, t = divmod(q, piece_tiles)
            return w_ref[0, (row ^ k) * piece_tiles + t, pl.ds(i0, block), :]

        @pl.loop(0, TILE // block)
        def _(step):
            i0 = pl.multiple_of(step * block, block)
            best = [jnp.full((block, TILE), NEG, F32) for _ in range(heads)]
            for q in range(col_tiles):
                edge = weight(q, i0) > 0
                for h in range(heads):
                    b = jnp.broadcast_to(score_row(q, h), (block, TILE))
                    best[h] = jnp.maximum(best[h], jnp.where(edge, b, NEG))
            t_at = pl.multiple_of(rt * TILE + i0, block)
            t_all = tgt[pl.ds(t_at, block), :]
            for h in range(heads):
                a = t_all[:, h : h + 1]
                m = leaky(a + jnp.max(best[h], axis=1, keepdims=True))
                pos = jnp.broadcast_to(a - m, (block, TILE))
                neg = jnp.broadcast_to(SLOPE * a - m, (block, TILE))
                den = jnp.zeros((block, TILE), F32)
                for q in range(col_tiles):
                    b = score_row(q, h)
                    x = jnp.maximum(pos + b, neg + SLOPE * b)
                    p = weight(q, i0) * jnp.exp2(jnp.minimum(x, 0.0))
                    den = den + p
                    hi = p.astype(BF16)
                    at = 2 * h * TILE + i0
                    probs[pl.ds(pl.multiple_of(at, block), block), q * TILE : (q + 1) * TILE] = hi
                    lo = (p - hi.astype(F32)).astype(BF16)
                    probs[
                        pl.ds(pl.multiple_of(at + TILE, block), block), q * TILE : (q + 1) * TILE
                    ] = lo
                den_s[h, pl.ds(i0, block), :] = jnp.broadcast_to(
                    jnp.sum(den, axis=1, keepdims=True), (block, TILE)
                )
                m_s[h, pl.ds(i0, block), :] = jnp.broadcast_to(m, (block, TILE))

        both = lax.dot_general(
            probs[...], z_cat[...], (((1,), (0,)), ((), ())), preferred_element_type=F32
        )
        lane_w = lax.broadcasted_iota(jnp.int32, (TILE, width), 1) // dims
        lane_t = lax.broadcasted_iota(jnp.int32, (TILE, TILE), 1)
        num = jnp.zeros((TILE, width), F32)
        md = jnp.zeros((TILE, TILE), F32)
        for h in range(heads):
            hi = both[2 * h * TILE : (2 * h + 1) * TILE]
            lo = both[(2 * h + 1) * TILE : (2 * h + 2) * TILE]
            mine = hi[:, :width] + (hi[:, width:] + lo[:, :width])
            num = jnp.where(lane_w == h, mine, num)
            md = jnp.where(lane_t == h, den_s[h], md)
            md = jnp.where(lane_t == heads + h, m_s[h], md)
        md = md.T
        for k in range(per_tile):
            done[rt * per_tile + k, :own_rows, :width] = num[k * own_rows : (k + 1) * own_rows]
            done[rt * per_tile + k, own_rows:, :own_rows] = md[
                :mdp, k * own_rows : (k + 1) * own_rows
            ]

        @pl.when(rt == row_tiles - 1)
        def _():
            for d in range(n_col):
                out_refs[d][...] = done[goes_to(col, d, n_col)]

    full = lambda shape: pl.BlockSpec(shape, lambda s: (0,) * len(shape))
    chunk = jax.ShapeDtypeStruct((chunk_rows, lanes), F32)
    k_all = n_row * src_rows
    chunks = pl.pallas_call(
        att_kernel,
        out_shape=[chunk] * n_col,
        grid=(row_tiles,),
        in_specs=[full((hp, own_rows))] * n_col
        + [full((pack_rows, lanes))] * n_row
        + [pl.BlockSpec((1, col_tiles, TILE, TILE), lambda s: (s, 0, 0, 0))],
        out_specs=[full((chunk_rows, lanes))] * n_col,
        scratch_shapes=[
            pltpu.VMEM((row_tiles * TILE, TILE), F32),
            pltpu.VMEM((k_all, 2 * width), BF16),
            pltpu.VMEM((2 * heads * TILE, k_all), BF16),
            pltpu.VMEM((heads, TILE, TILE), F32),
            pltpu.VMEM((heads, TILE, TILE), F32),
            pltpu.VMEM((n_col, chunk_rows, lanes), F32),
        ],
        cost_estimate=pl.CostEstimate(
            flops=row_tiles * TILE * k_all * width * heads * 8,
            bytes_accessed=k_all * width * 4,
            transcendentals=row_tiles * TILE * k_all * heads,
        ),
    )(*targets, *pieces, panel)
    gathered = [chunks[0]] + [hop(chunks[d], "col", d) for d in range(1, n_col)]

    def out_kernel(zdst_ref, src_ref, dst_ref, bias_ref, *rest):
        parts, out_ref = rest[:n_col], rest[n_col]
        same = (
            lax.broadcasted_iota(jnp.int32, (width, width), 0) // dims
            == lax.broadcasted_iota(jnp.int32, (width, width), 1) // dims
        ).astype(F32)
        z = zdst_ref[...]
        pair = contract(z * (dst_ref[...] + src_ref[...]), same, ((1,), (0,)))
        e_self = leaky(LOG2E * pair)
        which = lax.broadcasted_iota(jnp.int32, (mdp, width), 0)
        head = lax.broadcasted_iota(jnp.int32, (mdp, width), 1) // dims
        den_of, m_of = (which == head).astype(F32), (which == head + heads).astype(F32)
        mds = [part[own_rows:, :own_rows] for part in parts]
        ms = [contract(md, m_of, ((0,), (0,))) for md in mds]
        dens = [contract(md, den_of, ((0,), (0,))) for md in mds]
        top = e_self
        for m in ms:
            top = jnp.maximum(top, m)
        den = jnp.exp2(e_self - top)
        num = den * z
        for part, m, own_den in zip(parts, ms, dens):
            factor = jnp.exp2(m - top)
            den = den + factor * own_den
            num = num + factor * part[:own_rows, :width]
        x = num / den + bias_ref[...]
        out_ref[...] = jnp.where(x > 0, x, jnp.exp(jnp.minimum(x, 0.0)) - 1.0).astype(BF16)

    return call(
        out_kernel,
        jax.ShapeDtypeStruct((own_rows, width), BF16),
        zdst,
        att_src2,
        att_dst2,
        bias2,
        *gathered,
    )


def solution(mesh):
    return jax.shard_map(
        on_device,
        mesh=mesh,
        in_specs=(
            P(("row", "col"), "feat"),
            P(("row", "col"), "feat"),
            P("feat", None),
            P("feat"),
            P("feat"),
            P("feat"),
            P("row", "col", None),
            P("row", "col", None),
            P("row", "col"),
            P("row", "col", None, None, None),
        ),
        out_specs=P(("row", "col"), "feat"),
        check_vma=False,
    )
```

```python
import jax
import jax.numpy as jnp
from jax import lax
from jax.experimental import pallas as pl
from jax.experimental.pallas import tpu as pltpu
from jax.sharding import PartitionSpec as P

HEADS = 8
TILE = 128
SLOPE = 0.2
LOG2E = 1.4426950408889634
NEG = -1e30
F32 = jnp.float32
BF16 = jnp.bfloat16
HIGHEST = lax.Precision.HIGHEST
VMEM = pl.BlockSpec(memory_space=pltpu.VMEM)
SMEM = pl.BlockSpec(memory_space=pltpu.SMEM)


def is_pow2(n):
    return n & (n - 1) == 0


def goes_to(i, d, n):
    return i ^ d if is_pow2(n) else lax.rem(i + d, n)


def comes_from(i, d, n):
    return i ^ d if is_pow2(n) else lax.rem(i + n - d, n)


def hop(x, axis, d):
    n = lax.axis_size(axis)
    pairs = [(i, i ^ d if is_pow2(n) else (i + d) % n) for i in range(n)]
    return lax.ppermute(x, axis, pairs)


def call(kernel, out_shape, *args, in_specs=None, flops=0, bytes_accessed=0, **kw):
    return pl.pallas_call(
        kernel,
        out_shape=out_shape,
        in_specs=in_specs or [VMEM] * len(args),
        cost_estimate=pl.CostEstimate(
            flops=flops, bytes_accessed=bytes_accessed, transcendentals=0
        ),
        compiler_params=pltpu.CompilerParams(vmem_limit_bytes=limit(8, 0)),
        **kw,
    )(*args)


def limit(mib, least):
    return min(max(mib << 20, least), 60 << 20)


def up8(n):
    return -(-n // 8) * 8


def head_rows(vector, heads, width, height):
    dims = width // heads
    shape = (height, width)
    row = lax.broadcasted_iota(jnp.int32, shape, 0) % heads
    lane = lax.broadcasted_iota(jnp.int32, shape, 1)
    return jnp.where(lane // dims == row, jnp.broadcast_to(vector, shape), 0.0)


def contract(lhs, rhs, dims, precision=HIGHEST):
    return lax.dot_general(
        lhs, rhs, (dims, ((), ())), preferred_element_type=F32, precision=precision
    )


def take_cols(proj_ref, which, width):
    if width % TILE == 0:
        return proj_ref[:, pl.ds(pl.multiple_of(which * width, width), width)]
    full = proj_ref[...]
    out = full[:, :width]
    for k in range(1, full.shape[1] // width):
        out = jnp.where(which == k, full[:, k * width : (k + 1) * width], out)
    return out


def project(x, w):
    return lax.dot_general(x, w, (((1,), (0,)), ((), ())), preferred_element_type=F32)


def leaky(x):
    return jnp.maximum(x, SLOPE * x)


def on_device(
    src_feats, dst_feats, proj, att_src, att_dst, bias, tile_rows, tile_cols, tile_count, edge_weight
):
    n_row, n_col, n_feat = (lax.axis_size(a) for a in ("row", "col", "feat"))
    width = proj.shape[1] // n_feat
    heads = HEADS // n_feat
    dims = width // heads
    lanes = -(-width // TILE) * TILE
    src_rows, own_rows = src_feats.shape[0], dst_feats.shape[0]
    slots = tile_rows.shape[2]
    row_tiles = own_rows * n_col // TILE
    piece_tiles = src_rows // TILE
    col_tiles = piece_tiles * n_row
    per_tile = TILE // own_rows
    hp = up8(2 * heads)
    mdp = up8(2 * heads)
    att_src2, att_dst2, bias2 = (v.reshape(1, width) for v in (att_src, att_dst, bias))

    rows = src_rows + own_rows

    def send_kernel(src_ref, dst_ref, proj_ref, *outs):
        me = lax.axis_index("feat")
        for d in range(1, n_feat):
            w = take_cols(proj_ref, goes_to(me, d, n_feat), width)
            outs[d - 1][:src_rows] = project(src_ref[...], w)
            outs[d - 1][src_rows:] = project(dst_ref[...], w)

    sent = call(
        send_kernel,
        [jax.ShapeDtypeStruct((rows, width), F32)] * (n_feat - 1),
        src_feats,
        dst_feats,
        proj,
    )
    parts = [hop(sent[d - 1], "feat", d) for d in range(1, n_feat)]

    half = col_tiles // 2
    tiles = row_tiles * col_tiles
    period = min(slots, tiles) if slots % min(slots, tiles) == 0 else slots
    reps = slots // period
    group = 8

    def weight_kernel(rows_ref, cols_ref, count_ref, w_ref, near_ref, far_ref):
        step = pl.program_id(0)
        row = lax.axis_index("row")
        count = count_ref[0, 0]

        @pl.when(step == 0)
        def _():
            @pl.loop(0, row_tiles * half)
            def _(t):
                near_ref[t // half, t % half] = jnp.zeros((TILE, TILE), F32)
                far_ref[t // half, t % half] = jnp.zeros((TILE, TILE), F32)

        base = step * group

        @pl.loop(0, jnp.clip(count - base, 0, group))
        def _(u):
            r, c = rows_ref[0, 0, base + u], cols_ref[0, 0, base + u]
            q = ((c // piece_tiles) ^ row) * piece_tiles + c % piece_tiles
            total = w_ref[0, u].astype(F32)
            for k in range(1, reps):
                live = (base + u + k * period < count).astype(F32)
                total = total + w_ref[k, u].astype(F32) * live

            @pl.when(q < half)
            def _():
                near_ref[r, q] = near_ref[r, q] + total

            @pl.when(q >= half)
            def _():
                far_ref[r, q - half] = far_ref[r, q - half] + total

    panel_shape = (row_tiles, half, TILE, TILE)
    whole = lambda shape: pl.BlockSpec(shape, lambda s: (0,) * len(shape))
    panels = pl.pallas_call(
        weight_kernel,
        out_shape=[jax.ShapeDtypeStruct(panel_shape, F32)] * 2,
        grid=(period // group,),
        in_specs=[
            SMEM,
            SMEM,
            SMEM,
            pl.BlockSpec((reps, group, TILE, TILE), lambda s: (0, s, 0, 0)),
        ],
        out_specs=[whole(panel_shape)] * 2,
        compiler_params=pltpu.CompilerParams(vmem_limit_bytes=limit(32, 8 * tiles * TILE * TILE)),
        cost_estimate=pl.CostEstimate(
            flops=slots * TILE * TILE, bytes_accessed=slots * TILE * TILE * 2, transcendentals=0
        ),
    )(tile_rows, tile_cols, tile_count, edge_weight.reshape(reps, period, TILE, TILE))
    tied = lax.optimization_barrier((*parts, *panels))
    parts, panels = tied[: n_feat - 1], tied[n_feat - 1 :]

    pack_rows = src_rows + piece_tiles * hp

    def z_kernel(src_ref, dst_ref, proj_ref, att_src_ref, att_dst_ref, *rest):
        got, (out_ref, z_ref, s_ref) = rest[: n_feat - 1], rest[n_feat - 1 :]
        w = take_cols(proj_ref, lax.axis_index("feat"), width)
        z = project(src_ref[...], w)
        zdst = project(dst_ref[...], w)
        for part in got:
            z = z + part[:src_rows]
            zdst = zdst + part[src_rows:]
        if width < lanes:
            out_ref[...] = jnp.zeros_like(out_ref)
        out_ref[:src_rows, :width] = z
        s = LOG2E * contract(head_rows(att_src_ref[...], heads, width, hp), z, ((1,), (1,)))
        low = lax.broadcasted_iota(jnp.int32, s.shape, 0) < heads
        s = jnp.where(low, s, SLOPE * s)
        for t in range(piece_tiles):
            at = src_rows + t * hp
            out_ref[at : at + hp, :TILE] = s[:, t * TILE : (t + 1) * TILE]
        z_ref[...] = zdst
        s_ref[...] = LOG2E * contract(
            head_rows(att_dst_ref[...], heads, width, up8(heads)), zdst, ((1,), (1,))
        )

    own_piece, zdst, s_dst = call(
        z_kernel,
        [
            jax.ShapeDtypeStruct((pack_rows, lanes), F32),
            jax.ShapeDtypeStruct((own_rows, width), F32),
            jax.ShapeDtypeStruct((up8(heads), own_rows), F32),
        ],
        src_feats,
        dst_feats,
        proj,
        att_src2,
        att_dst2,
        *parts,
    )
    far0 = hop(own_piece, "row", n_row // 2)

    def spread(piece):
        pieces = {0: piece}
        d = n_row // 4
        while d:
            for k in list(pieces):
                pieces[k ^ d] = hop(pieces[k], "row", d)
            d //= 2
        return [pieces[k] for k in range(n_row // 2)]

    near_pieces = spread(own_piece)
    targets = [s_dst] + [hop(s_dst, "col", d) for d in range(1, n_col)]
    far_pieces = spread(far0)

    block = 64
    blocks = TILE // block
    unroll = 2 if row_tiles % 2 == 0 else 1
    chunk_rows = own_rows + mdp
    n_piece = n_row // 2
    k_all = n_piece * src_rows
    group_rows = unroll * TILE
    all_rows = row_tiles * TILE
    tiny = 2.0**-60

    def attend(refs, tgt, piece_refs, w_ref, z_cat, probs, num_ref, md_ref):
        step = pl.program_id(0)

        def score_rows(q, h):
            k, t = divmod(q, piece_tiles)
            at = src_rows + t * hp + h
            return piece_refs[k][at : at + 1, :TILE], piece_refs[k][at + heads : at + heads + 1, :TILE]

        tops = []
        for h in range(heads):
            top = score_rows(0, h)[0]
            for q in range(1, half):
                top = jnp.maximum(top, score_rows(q, h)[0])
            tops.append(jnp.max(top, axis=1, keepdims=True))

        lane_w = lax.broadcasted_iota(jnp.int32, (block, width), 1) // dims
        lane_t = lax.broadcasted_iota(jnp.int32, (block, TILE), 1)

        def put(at, h, q, p, slot):
            cols = slice(q * TILE, (q + 1) * TILE)
            hi = p.astype(BF16)
            lo = (p - hi.astype(F32)).astype(BF16)
            probs[slot, 2 * h * block : (2 * h + 1) * block, cols] = hi
            probs[slot, (2 * h + 1) * block : (2 * h + 2) * block, cols] = lo

        def finish(at, slot, dens, ms):
            both = lax.dot_general(
                probs[slot], z_cat[...], (((1,), (0,)), ((), ())), preferred_element_type=F32
            )
            num = jnp.zeros((block, width), F32)
            md = jnp.zeros((block, TILE), F32)
            for h in range(heads):
                hi = both[2 * h * block : (2 * h + 1) * block]
                lo = both[(2 * h + 1) * block : (2 * h + 2) * block]
                num = jnp.where(lane_w == h, hi[:, :width] + (hi[:, width:] + lo[:, :width]), num)
                md = jnp.where(lane_t == h, dens[h], md)
                md = jnp.where(lane_t == heads + h, ms[h], md)
            num_ref[pl.ds(at, block), :] = num
            md_ref[pl.ds(at, block), :] = md

        base = step * group_rows
        worst = None
        for b in range(unroll * blocks):
            at = pl.multiple_of(base + b * block, block)
            rt, i0 = divmod(b * block, TILE)
            t_all = tgt[pl.ds(at, block), :]
            dens, ms = [], []
            for h in range(heads):
                a = t_all[:, h : h + 1]
                m = leaky(a + tops[h])
                pos = jnp.broadcast_to(a - m, (block, TILE))
                neg = jnp.broadcast_to(SLOPE * a - m, (block, TILE))
                den = jnp.zeros((block, TILE), F32)
                for q in range(half):
                    s, s_low = score_rows(q, h)
                    p = w_ref[rt, q, i0 : i0 + block, :] * jnp.exp2(
                        jnp.maximum(pos + s, neg + s_low)
                    )
                    den = den + p
                    put(at, h, q, p, b % 2)
                den = jnp.sum(den, axis=1, keepdims=True)
                worst = den if worst is None else jnp.minimum(worst, den)
                dens.append(den)
                ms.append(m)
            finish(at, b % 2, dens, ms)

        @pl.when(jnp.logical_not(jnp.min(worst) >= tiny))
        def _():
            @pl.loop(0, unroll * blocks)
            def _(b):
                at = pl.multiple_of(base + b * block, block)
                rt = b // blocks
                i0 = pl.multiple_of((b % blocks) * block, block)
                t_all = tgt[pl.ds(at, block), :]
                dens, ms = [], []
                for h in range(heads):
                    best = jnp.full((block, TILE), NEG, F32)
                    for q in range(half):
                        s, _ = score_rows(q, h)
                        edge = w_ref[rt, q, pl.ds(i0, block), :] > 0
                        best = jnp.maximum(best, jnp.where(edge, s, NEG))
                    a = t_all[:, h : h + 1]
                    m = leaky(a + jnp.max(best, axis=1, keepdims=True))
                    pos, neg = a - m, SLOPE * a - m
                    den = jnp.zeros((block, TILE), F32)
                    for q in range(half):
                        s, s_low = score_rows(q, h)
                        x = jnp.maximum(pos + s, neg + s_low)
                        p = w_ref[rt, q, pl.ds(i0, block), :] * jnp.exp2(jnp.minimum(x, 0.0))
                        den = den + p
                        put(at, h, q, p, 0)
                    dens.append(jnp.sum(den, axis=1, keepdims=True))
                    ms.append(m)
                finish(at, 0, dens, ms)

    def split_z(piece_refs, z_cat):
        for k in range(n_piece):
            z = piece_refs[k][:src_rows, :width]
            hi = z.astype(BF16)
            z_cat[k * src_rows : (k + 1) * src_rows, :width] = hi
            z_cat[k * src_rows : (k + 1) * src_rows, width:] = (z - hi.astype(F32)).astype(BF16)

    def near_kernel(*refs):
        tgt_refs, refs = refs[:n_col], refs[n_col:]
        piece_refs, refs = refs[:n_piece], refs[n_piece:]
        w_ref, tgt, num_ref, md_ref, z_cat, probs = refs
        col = lax.axis_index("col")

        @pl.when(pl.program_id(0) == 0)
        def _():
            shape = (up8(heads), TILE)
            eye = (
                lax.broadcasted_iota(jnp.int32, shape, 0)
                == lax.broadcasted_iota(jnp.int32, shape, 1)
            ).astype(F32)
            for d in range(n_col):
                at = pl.multiple_of(comes_from(col, d, n_col) * own_rows, own_rows)
                tgt[pl.ds(at, own_rows), :] = contract(tgt_refs[d][...], eye, ((0,), (0,)))
            split_z(piece_refs, z_cat)

        attend(refs, tgt, piece_refs, w_ref, z_cat, probs, num_ref, md_ref)

    def far_kernel(*refs):
        tgt, near_num, near_md, refs = refs[0], refs[1], refs[2], refs[3:]
        piece_refs, refs = refs[:n_piece], refs[n_piece:]
        w_ref, refs = refs[0], refs[1:]
        out_refs, (num_ref, md_ref, z_cat, probs) = refs[:n_col], refs[n_col:]
        col = lax.axis_index("col")
        step = pl.program_id(0)

        @pl.when(step == 0)
        def _():
            split_z(piece_refs, z_cat)

        attend(refs, tgt, piece_refs, w_ref, z_cat, probs, num_ref, md_ref)

        base = step * group_rows
        lane_w = lax.broadcasted_iota(jnp.int32, (TILE, width), 1) // dims
        lane_t = lax.broadcasted_iota(jnp.int32, (TILE, TILE), 1)
        for rt in range(unroll):
            at = pl.ds(pl.multiple_of(base + rt * TILE, TILE), TILE)
            near, far = near_md[at, :], md_ref[at, :]
            md = jnp.zeros((TILE, TILE), F32)
            f_near = jnp.zeros((TILE, width), F32)
            f_far = jnp.zeros((TILE, width), F32)
            for h in range(heads):
                m0, m1 = near[:, heads + h : heads + h + 1], far[:, heads + h : heads + h + 1]
                m = jnp.maximum(m0, m1)
                f0, f1 = jnp.exp2(m0 - m), jnp.exp2(m1 - m)
                den = near[:, h : h + 1] * f0 + far[:, h : h + 1] * f1
                md = jnp.where(lane_t == h, den, md)
                md = jnp.where(lane_t == heads + h, m, md)
                f_near = jnp.where(lane_w == h, f0, f_near)
                f_far = jnp.where(lane_w == h, f1, f_far)
            num = near_num[at, :] * f_near + num_ref[at, :] * f_far
            num_ref[at, :] = num
            md_ref[at, :] = md

        @pl.when(step == row_tiles // unroll - 1)
        def _():
            for d in range(n_col):
                at = pl.multiple_of(goes_to(col, d, n_col) * own_rows, own_rows)
                if width < lanes:
                    out_refs[d][...] = jnp.zeros_like(out_refs[d])
                out_refs[d][:own_rows, :width] = num_ref[pl.ds(at, own_rows), :]
                out_refs[d][own_rows:, :own_rows] = md_ref[pl.ds(at, own_rows), :].T[:mdp]

    scratch = [
        pltpu.VMEM((k_all, 2 * width), BF16),
        pltpu.VMEM((2, 2 * heads * block, k_all), BF16),
    ]
    cost = pl.CostEstimate(
        flops=all_rows * k_all * width * heads * 8,
        bytes_accessed=k_all * width * 4,
        transcendentals=all_rows * k_all * heads,
    )
    w_spec = pl.BlockSpec((unroll, half, TILE, TILE), lambda s: (s, 0, 0, 0))
    rows_shape = [(all_rows, TILE), (all_rows, width), (all_rows, TILE)]
    params = pltpu.CompilerParams(vmem_limit_bytes=limit(32, 8 * tiles * TILE * TILE))
    tgt, near_num, near_md = pl.pallas_call(
        near_kernel,
        out_shape=[jax.ShapeDtypeStruct(s, F32) for s in rows_shape],
        grid=(row_tiles // unroll,),
        in_specs=[whole((up8(heads), own_rows))] * n_col
        + [whole((pack_rows, lanes))] * n_piece
        + [w_spec],
        out_specs=[whole(s) for s in rows_shape],
        scratch_shapes=scratch,
        cost_estimate=cost,
        compiler_params=params,
    )(*targets, *near_pieces, panels[0])
    chunk = (chunk_rows, lanes)
    chunks = pl.pallas_call(
        far_kernel,
        out_shape=[jax.ShapeDtypeStruct(chunk, F32)] * n_col,
        grid=(row_tiles // unroll,),
        in_specs=[whole(s) for s in rows_shape]
        + [whole((pack_rows, lanes))] * n_piece
        + [w_spec],
        out_specs=[whole(chunk)] * n_col,
        scratch_shapes=[pltpu.VMEM(s, F32) for s in rows_shape[1:]] + scratch,
        cost_estimate=cost,
        compiler_params=params,
    )(tgt, near_num, near_md, *far_pieces, panels[1])
    gathered = [chunks[0]] + [hop(chunks[d], "col", d) for d in range(1, n_col)]

    def out_kernel(zdst_ref, src_ref, dst_ref, bias_ref, *rest):
        parts, out_ref = rest[:n_col], rest[n_col]
        same = (
            lax.broadcasted_iota(jnp.int32, (width, width), 0) // dims
            == lax.broadcasted_iota(jnp.int32, (width, width), 1) // dims
        ).astype(F32)
        z = zdst_ref[...]
        pair = contract(z * (dst_ref[...] + src_ref[...]), same, ((1,), (0,)))
        e_self = leaky(LOG2E * pair)
        which = lax.broadcasted_iota(jnp.int32, (mdp, width), 0)
        head = lax.broadcasted_iota(jnp.int32, (mdp, width), 1) // dims
        den_of, m_of = (which == head).astype(F32), (which == head + heads).astype(F32)
        mds = [part[own_rows:, :own_rows] for part in parts]
        ms = [contract(md, m_of, ((0,), (0,))) for md in mds]
        dens = [contract(md, den_of, ((0,), (0,))) for md in mds]
        top = e_self
        for m in ms:
            top = jnp.maximum(top, m)
        den = jnp.exp2(e_self - top)
        num = den * z
        for part, m, own_den in zip(parts, ms, dens):
            factor = jnp.exp2(m - top)
            den = den + factor * own_den
            num = num + factor * part[:own_rows, :width]
        x = num / den + bias_ref[...]
        out_ref[...] = jnp.where(x > 0, x, jnp.exp(jnp.minimum(x, 0.0)) - 1.0).astype(BF16)

    return call(
        out_kernel,
        jax.ShapeDtypeStruct((own_rows, width), BF16),
        zdst,
        att_src2,
        att_dst2,
        bias2,
        *gathered,
    )


def solution(mesh):
    return jax.shard_map(
        on_device,
        mesh=mesh,
        in_specs=(
            P(("row", "col"), "feat"),
            P(("row", "col"), "feat"),
            P("feat", None),
            P("feat"),
            P("feat"),
            P("feat"),
            P("row", "col", None),
            P("row", "col", None),
            P("row", "col"),
            P("row", "col", None, None, None),
        ),
        out_specs=P(("row", "col"), "feat"),
        check_vma=False,
    )
```

```python
import jax
import jax.numpy as jnp
from jax import lax
from jax.experimental import pallas as pl
from jax.experimental.pallas import tpu as pltpu
from jax.sharding import PartitionSpec as P

HEADS = 8
TILE = 128
SLOPE = 0.2
LOG2E = 1.4426950408889634
NEG = -1e30
F32 = jnp.float32
BF16 = jnp.bfloat16
ALL_VMEM = 67043328
HIGHEST = lax.Precision.HIGHEST
VMEM = pl.BlockSpec(memory_space=pltpu.VMEM)
SMEM = pl.BlockSpec(memory_space=pltpu.SMEM)
HBM = pl.BlockSpec(memory_space=pltpu.HBM)


def is_pow2(n):
    return n & (n - 1) == 0


def goes_to(i, d, n):
    return i ^ d if is_pow2(n) else lax.rem(i + d, n)


def comes_from(i, d, n):
    return i ^ d if is_pow2(n) else lax.rem(i + n - d, n)


def hop(x, axis, d):
    n = lax.axis_size(axis)
    pairs = [(i, i ^ d if is_pow2(n) else (i + d) % n) for i in range(n)]
    return lax.ppermute(x, axis, pairs)


def call(kernel, out_shape, *args, in_specs=None, flops=0, bytes_accessed=0, grant=8 << 20, **kw):
    return pl.pallas_call(
        kernel,
        out_shape=out_shape,
        in_specs=in_specs or [VMEM] * len(args),
        cost_estimate=pl.CostEstimate(
            flops=flops, bytes_accessed=bytes_accessed, transcendentals=0
        ),
        compiler_params=pltpu.CompilerParams(vmem_limit_bytes=grant),
        **kw,
    )(*args)


def limit(mib, least):
    return min(max(mib << 20, least), 60 << 20)


def up8(n):
    return -(-n // 8) * 8


def head_rows(vector, heads, width, height):
    dims = width // heads
    shape = (height, width)
    row = lax.broadcasted_iota(jnp.int32, shape, 0) % heads
    lane = lax.broadcasted_iota(jnp.int32, shape, 1)
    return jnp.where(lane // dims == row, jnp.broadcast_to(vector, shape), 0.0)


def contract(lhs, rhs, dims, precision=HIGHEST):
    return lax.dot_general(
        lhs, rhs, (dims, ((), ())), preferred_element_type=F32, precision=precision
    )


def take_cols(proj_ref, which, width):
    if width % TILE == 0:
        return proj_ref[:, pl.ds(pl.multiple_of(which * width, width), width)]
    full = proj_ref[...]
    out = full[:, :width]
    for k in range(1, full.shape[1] // width):
        out = jnp.where(which == k, full[:, k * width : (k + 1) * width], out)
    return out


def project(x, w):
    return lax.dot_general(x, w, (((1,), (0,)), ((), ())), preferred_element_type=F32)


def leaky(x):
    return jnp.maximum(x, SLOPE * x)


def on_device(
    src_feats, dst_feats, proj, att_src, att_dst, bias, tile_rows, tile_cols, tile_count, edge_weight
):
    n_row, n_col, n_feat = (lax.axis_size(a) for a in ("row", "col", "feat"))
    width = proj.shape[1] // n_feat
    heads = HEADS // n_feat
    dims = width // heads
    lanes = -(-width // TILE) * TILE
    src_rows, own_rows = src_feats.shape[0], dst_feats.shape[0]
    slots = tile_rows.shape[2]
    row_tiles = own_rows * n_col // TILE
    piece_tiles = src_rows // TILE
    col_tiles = piece_tiles * n_row
    hp = up8(2 * heads)
    mdp = up8(2 * heads)
    att_src2, att_dst2, bias2 = (v.reshape(1, width) for v in (att_src, att_dst, bias))

    def send_kernel(*refs):
        hbm, outs, refs = refs[:4], refs[4:-5], refs[-5:]
        sems, refs = refs[4], refs[:4]
        copies = [pltpu.make_async_copy(h, v, sems.at[k]) for k, (h, v) in enumerate(zip(hbm, refs))]
        for copy in copies:
            copy.start()
        for copy in copies:
            copy.wait()
        src_ref, dst_ref, proj_ref, att_ref = refs
        me = lax.axis_index("feat")
        outs[0][...] = project(dst_ref[...], take_cols(proj_ref, me, width))
        outs[1][...] = LOG2E * head_rows(att_ref[...], heads, width, up8(heads))
        for d in range(1, n_feat):
            w = take_cols(proj_ref, goes_to(me, d, n_feat), width)
            outs[2 * d][...] = project(dst_ref[...], w)
            outs[2 * d + 1][...] = project(src_ref[...], w)

    inputs = (src_feats, dst_feats, proj, att_dst2)
    dst_own, att_rows, *sent = call(
        send_kernel,
        [
            jax.ShapeDtypeStruct((own_rows, width), F32),
            jax.ShapeDtypeStruct((up8(heads), width), F32),
        ]
        + [
            jax.ShapeDtypeStruct((n, width), F32)
            for _ in range(1, n_feat)
            for n in (own_rows, src_rows)
        ],
        *inputs,
        in_specs=[HBM] * len(inputs),
        scratch_shapes=[
            *(pltpu.VMEM(v.shape, v.dtype) for v in inputs),
            pltpu.SemaphoreType.DMA((len(inputs),)),
        ],
        grant=ALL_VMEM,
    )
    dst_parts = [hop(sent[2 * d - 2], "feat", d) for d in range(1, n_feat)]
    src_parts = [hop(sent[2 * d - 1], "feat", d) for d in range(1, n_feat)]

    half = col_tiles // 2
    tiles = row_tiles * col_tiles
    period = min(slots, tiles) if slots % min(slots, tiles) == 0 else slots
    reps = slots // period
    group = 8

    def weight_kernel(rows_ref, cols_ref, count_ref, w_ref, near_ref, far_ref):
        step = pl.program_id(0)
        row = lax.axis_index("row")
        count = count_ref[0, 0]

        @pl.when(step == 0)
        def _():
            @pl.loop(0, row_tiles * half)
            def _(t):
                near_ref[t // half, t % half] = jnp.zeros((TILE, TILE), F32)
                far_ref[t // half, t % half] = jnp.zeros((TILE, TILE), F32)

        base = step * group

        @pl.loop(0, jnp.clip(count - base, 0, group))
        def _(u):
            r, c = rows_ref[0, 0, base + u], cols_ref[0, 0, base + u]
            q = ((c // piece_tiles) ^ row) * piece_tiles + c % piece_tiles
            total = w_ref[0, u].astype(F32)
            for k in range(1, reps):
                live = (base + u + k * period < count).astype(F32)
                total = total + w_ref[k, u].astype(F32) * live

            @pl.when(q < half)
            def _():
                near_ref[r, q] = near_ref[r, q] + total

            @pl.when(q >= half)
            def _():
                far_ref[r, q - half] = far_ref[r, q - half] + total

    panel_shape = (row_tiles, half, TILE, TILE)
    whole = lambda shape: pl.BlockSpec(shape, lambda s, *_: (0,) * len(shape))
    panels = pl.pallas_call(
        weight_kernel,
        out_shape=[jax.ShapeDtypeStruct(panel_shape, F32)] * 2,
        grid_spec=pltpu.PrefetchScalarGridSpec(
            num_scalar_prefetch=3,
            grid=(period // group,),
            in_specs=[pl.BlockSpec((reps, group, TILE, TILE), lambda s, *_: (0, s, 0, 0))],
            out_specs=[whole(panel_shape)] * 2,
        ),
        compiler_params=pltpu.CompilerParams(vmem_limit_bytes=60 << 20),
        cost_estimate=pl.CostEstimate(
            flops=slots * TILE * TILE, bytes_accessed=slots * TILE * TILE * 2, transcendentals=0
        ),
    )(tile_rows, tile_cols, tile_count, edge_weight.reshape(reps, period, TILE, TILE))
    dst_parts, panels = lax.optimization_barrier((dst_parts, panels))

    def dst_kernel(own_ref, att_ref, *rest):
        got, (z_ref, s_ref) = rest[: n_feat - 1], rest[n_feat - 1 :]
        z = own_ref[...]
        for part in got:
            z = z + part[...]
        z_ref[...] = z
        s_ref[...] = contract(att_ref[...], z, ((1,), (1,)))

    zdst, s_dst = call(
        dst_kernel,
        [
            jax.ShapeDtypeStruct((own_rows, width), F32),
            jax.ShapeDtypeStruct((up8(heads), own_rows), F32),
        ],
        dst_own,
        att_rows,
        *dst_parts,
    )
    targets = [hop(s_dst, "col", d) for d in range(n_col - 1, 0, -1)]
    targets = [s_dst] + targets[::-1]
    src_parts, targets = lax.optimization_barrier((src_parts, targets))

    pack_rows = src_rows + piece_tiles * hp

    def z_kernel(src_ref, proj_ref, att_ref, *rest):
        got, out_ref = rest[: n_feat - 1], rest[n_feat - 1]
        z = project(src_ref[...], take_cols(proj_ref, lax.axis_index("feat"), width))
        for part in got:
            z = z + part[...]
        if width < lanes:
            out_ref[...] = jnp.zeros_like(out_ref)
        out_ref[:src_rows, :width] = z
        s = LOG2E * contract(head_rows(att_ref[...], heads, width, hp), z, ((1,), (1,)))
        low = lax.broadcasted_iota(jnp.int32, s.shape, 0) < heads
        s = jnp.where(low, s, SLOPE * s)
        for t in range(piece_tiles):
            at = src_rows + t * hp
            out_ref[at : at + hp, :TILE] = s[:, t * TILE : (t + 1) * TILE]

    own_piece = call(
        z_kernel,
        jax.ShapeDtypeStruct((pack_rows, lanes), F32),
        src_feats,
        proj,
        att_src2,
        *src_parts,
    )
    far0 = hop(own_piece, "row", n_row // 2)

    def spread(piece):
        pieces = {0: piece}
        d = n_row // 4
        while d:
            for k in list(pieces):
                pieces[k ^ d] = hop(pieces[k], "row", d)
            d //= 2
        return [pieces[k] for k in range(n_row // 2)]

    near_pieces = spread(own_piece)

    block = 64
    blocks = TILE // block
    unroll = 2 if row_tiles % 2 == 0 else 1
    chunk_rows = own_rows + mdp
    n_piece = n_row // 2
    k_all = n_piece * src_rows
    group_rows = unroll * TILE
    all_rows = row_tiles * TILE
    tiny = 2.0**-60

    def attend(tgt, piece_refs, w_ref, z_cat, probs, num_ref, md_ref):
        step = pl.program_id(0)

        def score_rows(q, h):
            k, t = divmod(q, piece_tiles)
            at = src_rows + t * hp + h
            return piece_refs[k][at : at + 1, :TILE], piece_refs[k][at + heads : at + heads + 1, :TILE]

        tops = []
        for h in range(heads):
            top = score_rows(0, h)[0]
            for q in range(1, half):
                top = jnp.maximum(top, score_rows(q, h)[0])
            tops.append(jnp.max(top, axis=1, keepdims=True))

        lane_w = lax.broadcasted_iota(jnp.int32, (block, width), 1) // dims
        lane_t = lax.broadcasted_iota(jnp.int32, (block, TILE), 1)

        def put(h, q, p, slot):
            cols = slice(q * TILE, (q + 1) * TILE)
            hi = p.astype(BF16)
            lo = (p - hi.astype(F32)).astype(BF16)
            probs[slot, 2 * h * block : (2 * h + 1) * block, cols] = hi
            probs[slot, (2 * h + 1) * block : (2 * h + 2) * block, cols] = lo

        def finish(at, slot, dens, ms):
            both = lax.dot_general(
                probs[slot], z_cat[...], (((1,), (0,)), ((), ())), preferred_element_type=F32
            )
            num = jnp.zeros((block, width), F32)
            md = jnp.zeros((block, TILE), F32)
            for h in range(heads):
                hi = both[2 * h * block : (2 * h + 1) * block]
                lo = both[(2 * h + 1) * block : (2 * h + 2) * block]
                num = jnp.where(lane_w == h, hi[:, :width] + (hi[:, width:] + lo[:, :width]), num)
                md = jnp.where(lane_t == h, dens[h], md)
                md = jnp.where(lane_t == heads + h, ms[h], md)
            num_ref[pl.ds(at, block), :] = num
            md_ref[pl.ds(at, block), :] = md

        base = step * group_rows
        worst = None
        for b in range(unroll * blocks):
            at = pl.multiple_of(base + b * block, block)
            rt, i0 = divmod(b * block, TILE)
            t_all = tgt[pl.ds(at, block), :]
            dens, ms = [], []
            for h in range(heads):
                a = t_all[:, h : h + 1]
                m = leaky(a + tops[h])
                pos = jnp.broadcast_to(a - m, (block, TILE))
                neg = jnp.broadcast_to(SLOPE * a - m, (block, TILE))
                den = jnp.zeros((block, TILE), F32)
                for q in range(half):
                    s, s_low = score_rows(q, h)
                    p = w_ref[rt, q, i0 : i0 + block, :] * jnp.exp2(
                        jnp.maximum(pos + s, neg + s_low)
                    )
                    den = den + p
                    put(h, q, p, b % 2)
                den = jnp.sum(den, axis=1, keepdims=True)
                worst = den if worst is None else jnp.minimum(worst, den)
                dens.append(den)
                ms.append(m)
            finish(at, b % 2, dens, ms)

        @pl.when(jnp.logical_not(jnp.min(worst) >= tiny))
        def _():
            @pl.loop(0, unroll * blocks)
            def _(b):
                at = pl.multiple_of(base + b * block, block)
                rt = b // blocks
                i0 = pl.multiple_of((b % blocks) * block, block)
                t_all = tgt[pl.ds(at, block), :]
                dens, ms = [], []
                for h in range(heads):
                    best = jnp.full((block, TILE), NEG, F32)
                    for q in range(half):
                        s, _ = score_rows(q, h)
                        edge = w_ref[rt, q, pl.ds(i0, block), :] > 0
                        best = jnp.maximum(best, jnp.where(edge, s, NEG))
                    a = t_all[:, h : h + 1]
                    m = leaky(a + jnp.max(best, axis=1, keepdims=True))
                    pos, neg = a - m, SLOPE * a - m
                    den = jnp.zeros((block, TILE), F32)
                    for q in range(half):
                        s, s_low = score_rows(q, h)
                        x = jnp.maximum(pos + s, neg + s_low)
                        p = w_ref[rt, q, pl.ds(i0, block), :] * jnp.exp2(jnp.minimum(x, 0.0))
                        den = den + p
                        put(h, q, p, 0)
                    dens.append(jnp.sum(den, axis=1, keepdims=True))
                    ms.append(m)
                finish(at, 0, dens, ms)

    def split_z(piece_refs, z_cat):
        for k in range(n_piece):
            z = piece_refs[k][:src_rows, :width]
            hi = z.astype(BF16)
            z_cat[k * src_rows : (k + 1) * src_rows, :width] = hi
            z_cat[k * src_rows : (k + 1) * src_rows, width:] = (z - hi.astype(F32)).astype(BF16)

    def near_kernel(*refs):
        tgt_refs, refs = refs[:n_col], refs[n_col:]
        piece_refs, refs = refs[:n_piece], refs[n_piece:]
        w_ref, tgt, num_ref, md_ref, z_cat, probs = refs
        col = lax.axis_index("col")

        @pl.when(pl.program_id(0) == 0)
        def _():
            shape = (up8(heads), TILE)
            eye = (
                lax.broadcasted_iota(jnp.int32, shape, 0)
                == lax.broadcasted_iota(jnp.int32, shape, 1)
            ).astype(F32)
            for d in range(n_col):
                at = pl.multiple_of(comes_from(col, d, n_col) * own_rows, own_rows)
                tgt[pl.ds(at, own_rows), :] = contract(tgt_refs[d][...], eye, ((0,), (0,)))
            split_z(piece_refs, z_cat)

        attend(tgt, piece_refs, w_ref, z_cat, probs, num_ref, md_ref)

    def far_kernel(*refs):
        tgt, near_num, near_md, refs = refs[0], refs[1], refs[2], refs[3:]
        piece_refs, refs = refs[:n_piece], refs[n_piece:]
        w_ref, refs = refs[0], refs[1:]
        out_refs, (num_ref, md_ref, z_cat, probs) = refs[:n_col], refs[n_col:]
        col = lax.axis_index("col")
        step = pl.program_id(0)

        @pl.when(step == 0)
        def _():
            split_z(piece_refs, z_cat)

        attend(tgt, piece_refs, w_ref, z_cat, probs, num_ref, md_ref)

        base = step * group_rows
        lane_w = lax.broadcasted_iota(jnp.int32, (TILE, width), 1) // dims
        lane_t = lax.broadcasted_iota(jnp.int32, (TILE, TILE), 1)
        for rt in range(unroll):
            at = pl.ds(pl.multiple_of(base + rt * TILE, TILE), TILE)
            near, far = near_md[at, :], md_ref[at, :]
            md = jnp.zeros((TILE, TILE), F32)
            f_near = jnp.zeros((TILE, width), F32)
            f_far = jnp.zeros((TILE, width), F32)
            for h in range(heads):
                m0, m1 = near[:, heads + h : heads + h + 1], far[:, heads + h : heads + h + 1]
                m = jnp.maximum(m0, m1)
                f0, f1 = jnp.exp2(m0 - m), jnp.exp2(m1 - m)
                den = near[:, h : h + 1] * f0 + far[:, h : h + 1] * f1
                md = jnp.where(lane_t == h, den, md)
                md = jnp.where(lane_t == heads + h, m, md)
                f_near = jnp.where(lane_w == h, f0, f_near)
                f_far = jnp.where(lane_w == h, f1, f_far)
            num = near_num[at, :] * f_near + num_ref[at, :] * f_far
            num_ref[at, :] = num
            md_ref[at, :] = md

        @pl.when(step == row_tiles // unroll - 1)
        def _():
            for d in range(n_col):
                at = pl.multiple_of(goes_to(col, d, n_col) * own_rows, own_rows)
                if width < lanes:
                    out_refs[d][...] = jnp.zeros_like(out_refs[d])
                out_refs[d][:own_rows, :width] = num_ref[pl.ds(at, own_rows), :]
                out_refs[d][own_rows:, :own_rows] = md_ref[pl.ds(at, own_rows), :].T[:mdp]

    scratch = [
        pltpu.VMEM((k_all, 2 * width), BF16),
        pltpu.VMEM((2, 2 * heads * block, k_all), BF16),
    ]
    cost = pl.CostEstimate(
        flops=all_rows * k_all * width * heads * 8,
        bytes_accessed=k_all * width * 4,
        transcendentals=all_rows * k_all * heads,
    )
    w_spec = pl.BlockSpec((unroll, half, TILE, TILE), lambda s: (s, 0, 0, 0))
    rows_shape = [(all_rows, TILE), (all_rows, width), (all_rows, TILE)]
    params = pltpu.CompilerParams(vmem_limit_bytes=limit(32, 8 * tiles * TILE * TILE))
    tgt, near_num, near_md = pl.pallas_call(
        near_kernel,
        out_shape=[jax.ShapeDtypeStruct(s, F32) for s in rows_shape],
        grid=(row_tiles // unroll,),
        in_specs=[whole((up8(heads), own_rows))] * n_col
        + [whole((pack_rows, lanes))] * n_piece
        + [w_spec],
        out_specs=[whole(s) for s in rows_shape],
        scratch_shapes=scratch,
        cost_estimate=cost,
        compiler_params=params,
    )(*targets, *near_pieces, panels[0])
    far0, tgt, near_num, near_md = lax.optimization_barrier((far0, tgt, near_num, near_md))
    far_pieces = spread(far0)
    chunk = (chunk_rows, lanes)
    chunks = pl.pallas_call(
        far_kernel,
        out_shape=[jax.ShapeDtypeStruct(chunk, F32)] * n_col,
        grid=(row_tiles // unroll,),
        in_specs=[whole(s) for s in rows_shape]
        + [whole((pack_rows, lanes))] * n_piece
        + [w_spec],
        out_specs=[whole(chunk)] * n_col,
        scratch_shapes=[pltpu.VMEM(s, F32) for s in rows_shape[1:]] + scratch,
        cost_estimate=cost,
        compiler_params=params,
    )(tgt, near_num, near_md, *far_pieces, panels[1])
    gathered = [hop(chunks[d], "col", d) for d in range(n_col - 1, 0, -1)]
    gathered = [chunks[0]] + gathered[::-1]

    def out_kernel(zdst_ref, src_ref, dst_ref, bias_ref, *rest):
        parts, out_ref = rest[:n_col], rest[n_col]
        same = (
            lax.broadcasted_iota(jnp.int32, (width, width), 0) // dims
            == lax.broadcasted_iota(jnp.int32, (width, width), 1) // dims
        ).astype(F32)
        z = zdst_ref[...]
        pair = contract(z * (dst_ref[...] + src_ref[...]), same, ((1,), (0,)))
        e_self = leaky(LOG2E * pair)
        which = lax.broadcasted_iota(jnp.int32, (mdp, width), 0)
        head = lax.broadcasted_iota(jnp.int32, (mdp, width), 1) // dims
        den_of, m_of = (which == head).astype(F32), (which == head + heads).astype(F32)
        mds = [part[own_rows:, :own_rows] for part in parts]
        ms = [contract(md, m_of, ((0,), (0,))) for md in mds]
        dens = [contract(md, den_of, ((0,), (0,))) for md in mds]
        top = e_self
        for m in ms:
            top = jnp.maximum(top, m)
        den = jnp.exp2(e_self - top)
        num = den * z
        for part, m, own_den in zip(parts, ms, dens):
            factor = jnp.exp2(m - top)
            den = den + factor * own_den
            num = num + factor * part[:own_rows, :width]
        x = num / den + bias_ref[...]
        out_ref[...] = jnp.where(x > 0, x, jnp.exp(jnp.minimum(x, 0.0)) - 1.0).astype(BF16)

    return call(
        out_kernel,
        jax.ShapeDtypeStruct((own_rows, width), BF16),
        zdst,
        att_src2,
        att_dst2,
        bias2,
        *gathered,
    )


def solution(mesh):
    return jax.shard_map(
        on_device,
        mesh=mesh,
        in_specs=(
            P(("row", "col"), "feat"),
            P(("row", "col"), "feat"),
            P("feat", None),
            P("feat"),
            P("feat"),
            P("feat"),
            P("row", "col", None),
            P("row", "col", None),
            P("row", "col"),
            P("row", "col", None, None, None),
        ),
        out_specs=P(("row", "col"), "feat"),
        check_vma=False,
    )
```

```python
import jax
import jax.numpy as jnp
from jax import lax
from jax.experimental import pallas as pl
from jax.experimental.pallas import tpu as pltpu
from jax.sharding import PartitionSpec as P

HEADS = 8
TILE = 128
SLOPE = 0.2
LOG2E = 1.4426950408889634
NEG = -1e30
F32 = jnp.float32
BF16 = jnp.bfloat16
HIGHEST = lax.Precision.HIGHEST
VMEM = pl.BlockSpec(memory_space=pltpu.VMEM)
SMEM = pl.BlockSpec(memory_space=pltpu.SMEM)
HBM = pl.BlockSpec(memory_space=pltpu.HBM)


def is_pow2(n):
    return n & (n - 1) == 0


def goes_to(i, d, n):
    return i ^ d if is_pow2(n) else lax.rem(i + d, n)


def comes_from(i, d, n):
    return i ^ d if is_pow2(n) else lax.rem(i + n - d, n)


def hop(x, axis, d):
    n = lax.axis_size(axis)
    pairs = [(i, i ^ d if is_pow2(n) else (i + d) % n) for i in range(n)]
    return lax.ppermute(x, axis, pairs)


def call(kernel, out_shape, *args, in_specs=None, flops=0, bytes_accessed=0, grant=8 << 20, **kw):
    return pl.pallas_call(
        kernel,
        out_shape=out_shape,
        in_specs=in_specs or [VMEM] * len(args),
        cost_estimate=pl.CostEstimate(
            flops=flops, bytes_accessed=bytes_accessed, transcendentals=0
        ),
        compiler_params=pltpu.CompilerParams(vmem_limit_bytes=grant),
        **kw,
    )(*args)


def limit(mib, least):
    return min(max(mib << 20, least), 60 << 20)


def in_hbm(x):
    return pltpu.with_memory_space_constraint(x, pltpu.HBM)


def up8(n):
    return -(-n // 8) * 8


def head_rows(vector, heads, width, height):
    dims = width // heads
    shape = (height, width)
    row = lax.broadcasted_iota(jnp.int32, shape, 0) % heads
    lane = lax.broadcasted_iota(jnp.int32, shape, 1)
    return jnp.where(lane // dims == row, jnp.broadcast_to(vector, shape), 0.0)


def contract(lhs, rhs, dims, precision=HIGHEST):
    return lax.dot_general(
        lhs, rhs, (dims, ((), ())), preferred_element_type=F32, precision=precision
    )


def take_cols(proj_ref, which, width):
    if width % TILE == 0:
        return proj_ref[:, pl.ds(pl.multiple_of(which * width, width), width)]
    full = proj_ref[...]
    out = full[:, :width]
    for k in range(1, full.shape[1] // width):
        out = jnp.where(which == k, full[:, k * width : (k + 1) * width], out)
    return out


def project(x, w):
    return lax.dot_general(x, w, (((1,), (0,)), ((), ())), preferred_element_type=F32)


def leaky(x):
    return jnp.maximum(x, SLOPE * x)


def on_device(
    src_feats, dst_feats, proj, att_src, att_dst, bias, tile_rows, tile_cols, tile_count, edge_weight
):
    n_row, n_col, n_feat = (lax.axis_size(a) for a in ("row", "col", "feat"))
    width = proj.shape[1] // n_feat
    heads = HEADS // n_feat
    dims = width // heads
    lanes = -(-width // TILE) * TILE
    src_rows, own_rows = src_feats.shape[0], dst_feats.shape[0]
    slots = tile_rows.shape[2]
    row_tiles = own_rows * n_col // TILE
    piece_tiles = src_rows // TILE
    col_tiles = piece_tiles * n_row
    hp = up8(2 * heads)
    mdp = up8(2 * heads)
    att_src2, att_dst2, bias2 = (v.reshape(1, width) for v in (att_src, att_dst, bias))

    def fetch(hbm, vmem, sems):
        copies = [pltpu.make_async_copy(h, v, sems.at[k]) for k, (h, v) in enumerate(zip(hbm, vmem))]
        for copy in copies:
            copy.start()
        for copy in copies:
            copy.wait()

    def fetching(kernel, outs, *args):
        return call(
            kernel,
            outs,
            *map(in_hbm, args),
            in_specs=[HBM] * len(args),
            scratch_shapes=[
                *(pltpu.VMEM(v.shape, v.dtype) for v in args),
                pltpu.SemaphoreType.DMA((len(args),)),
            ],
        )

    def send_kernel(*refs):
        hbm, outs, (src_ref, dst_ref, proj_ref, sems) = refs[:3], refs[3:-4], refs[-4:]
        fetch(hbm, (src_ref, dst_ref, proj_ref), sems)
        me = lax.axis_index("feat")
        for d in range(1, n_feat):
            w = take_cols(proj_ref, goes_to(me, d, n_feat), width)
            outs[2 * d - 2][...] = project(dst_ref[...], w)
            outs[2 * d - 1][...] = project(src_ref[...], w)

    sent = fetching(
        send_kernel,
        [pltpu.VMEM((n, width), F32) for _ in range(1, n_feat) for n in (own_rows, src_rows)],
        src_feats,
        dst_feats,
        proj,
    )
    dst_parts = [hop(sent[2 * d - 2], "feat", d) for d in range(1, n_feat)]
    src_parts = [hop(sent[2 * d - 1], "feat", d) for d in range(1, n_feat)]

    def own_kernel(*refs):
        hbm, outs, refs = refs[:5], refs[5:9], refs[9:]
        fetch(hbm, refs[:5], refs[5])
        src_ref, dst_ref, proj_ref, att_src_ref, att_dst_ref = refs[:5]
        w = take_cols(proj_ref, lax.axis_index("feat"), width)
        outs[0][...] = project(src_ref[...], w)
        outs[1][...] = project(dst_ref[...], w)
        outs[2][...] = LOG2E * head_rows(att_src_ref[...], heads, width, hp)
        outs[3][...] = LOG2E * head_rows(att_dst_ref[...], heads, width, up8(heads))

    src_own, dst_own, src_att, dst_att = fetching(
        own_kernel,
        [
            pltpu.VMEM((src_rows, width), F32),
            pltpu.VMEM((own_rows, width), F32),
            pltpu.VMEM((hp, width), F32),
            pltpu.VMEM((up8(heads), width), F32),
        ],
        src_feats,
        dst_feats,
        proj,
        att_src2,
        att_dst2,
    )
    dst_parts, src_own = lax.optimization_barrier((dst_parts, src_own))

    half = col_tiles // 2
    tiles = row_tiles * col_tiles
    whole = lambda shape: pl.BlockSpec(shape, lambda s: (0,) * len(shape))

    def dst_kernel(own_ref, att_ref, *rest):
        got, (z_ref, s_ref) = rest[: n_feat - 1], rest[n_feat - 1 :]
        z = own_ref[...]
        for part in got:
            z = z + part[...]
        z_ref[...] = z
        s_ref[...] = contract(att_ref[...], z, ((1,), (1,)))

    zdst, s_dst = call(
        dst_kernel,
        [
            jax.ShapeDtypeStruct((own_rows, width), F32),
            jax.ShapeDtypeStruct((up8(heads), own_rows), F32),
        ],
        dst_own,
        dst_att,
        *dst_parts,
    )
    targets = [hop(s_dst, "col", d) for d in range(n_col - 1, 0, -1)]
    targets = [s_dst] + targets[::-1]
    src_parts, targets = lax.optimization_barrier((src_parts, targets))

    pack_rows = src_rows + piece_tiles * hp

    def z_kernel(own_ref, att_ref, *rest):
        got, out_ref = rest[: n_feat - 1], rest[n_feat - 1]
        z = own_ref[...]
        for part in got:
            z = z + part[...]
        if width < lanes:
            out_ref[...] = jnp.zeros_like(out_ref)
        out_ref[:src_rows, :width] = z
        s = contract(att_ref[...], z, ((1,), (1,)))
        low = lax.broadcasted_iota(jnp.int32, s.shape, 0) < heads
        s = jnp.where(low, s, SLOPE * s)
        for t in range(piece_tiles):
            at = src_rows + t * hp
            out_ref[at : at + hp, :TILE] = s[:, t * TILE : (t + 1) * TILE]

    own_piece = call(
        z_kernel,
        pltpu.VMEM((pack_rows, lanes), F32),
        src_own,
        src_att,
        *src_parts,
    )
    far0 = hop(own_piece, "row", n_row // 2)
    own_piece, tile_count = lax.optimization_barrier((own_piece, tile_count))

    period = min(slots, tiles) if slots % min(slots, tiles) == 0 else slots
    reps = slots // period
    group = 8
    groups = period // group

    def weight_kernel(rows_hbm, cols_hbm, count_ref, w_hbm, near_ref, far_ref, *scratch):
        rows_ref, cols_ref, w_ref, index_sems, w_sems = scratch
        row = lax.axis_index("row")
        count = count_ref[0, 0]
        indices = [
            pltpu.make_async_copy(rows_hbm, rows_ref, index_sems.at[0]),
            pltpu.make_async_copy(cols_hbm, cols_ref, index_sems.at[1]),
        ]
        blocks = [
            pltpu.make_async_copy(
                w_hbm.at[k, pl.ds(g * group, group)],
                w_ref.at[k, pl.ds(g * group, group)],
                w_sems.at[g, k],
            )
            for g in range(groups)
            for k in range(reps)
        ]
        for copy in indices + blocks:
            copy.start()

        @pl.loop(0, row_tiles * half)
        def _(t):
            near_ref[t // half, t % half] = jnp.zeros((TILE, TILE), F32)
            far_ref[t // half, t % half] = jnp.zeros((TILE, TILE), F32)

        for copy in indices:
            copy.wait()
        for g in range(groups):
            for copy in blocks[g * reps : (g + 1) * reps]:
                copy.wait()
            base = g * group

            @pl.loop(base, jnp.clip(count, base, base + group))
            def _(u):
                r, c = rows_ref[0, 0, u], cols_ref[0, 0, u]
                q = ((c // piece_tiles) ^ row) * piece_tiles + c % piece_tiles
                total = w_ref[0, u].astype(F32)
                for k in range(1, reps):
                    live = (u + k * period < count).astype(F32)
                    total = total + w_ref[k, u].astype(F32) * live

                @pl.when(q < half)
                def _():
                    near_ref[r, q] = near_ref[r, q] + total

                @pl.when(q >= half)
                def _():
                    far_ref[r, q - half] = far_ref[r, q - half] + total

    panel_shape = (row_tiles, half, TILE, TILE)
    panels = call(
        weight_kernel,
        [pltpu.VMEM(panel_shape, F32)] * 2,
        in_hbm(tile_rows),
        in_hbm(tile_cols),
        tile_count,
        in_hbm(edge_weight.reshape(reps, period, TILE, TILE)),
        in_specs=[HBM, HBM, SMEM, HBM],
        scratch_shapes=[
            pltpu.SMEM(tile_rows.shape, jnp.int32),
            pltpu.SMEM(tile_cols.shape, jnp.int32),
            pltpu.VMEM((reps, period, TILE, TILE), edge_weight.dtype),
            pltpu.SemaphoreType.DMA((2,)),
            pltpu.SemaphoreType.DMA((groups, reps)),
        ],
        flops=slots * TILE * TILE,
        bytes_accessed=slots * TILE * TILE * 2,
        grant=12 << 20,
    )

    def spread(piece):
        pieces = {0: piece}
        d = n_row // 4
        while d:
            for k in list(pieces):
                pieces[k ^ d] = hop(pieces[k], "row", d)
            d //= 2
        return [pieces[k] for k in range(n_row // 2)]

    near_pieces = spread(own_piece)

    block = 64
    blocks = TILE // block
    unroll = 2 if row_tiles % 2 == 0 else 1
    chunk_rows = own_rows + mdp
    n_piece = n_row // 2
    k_all = n_piece * src_rows
    group_rows = unroll * TILE
    all_rows = row_tiles * TILE
    tiny = 2.0**-60

    def attend(tgt, piece_refs, w_ref, z_cat, probs, num_ref, md_ref):
        step = pl.program_id(0)

        def score_rows(q, h):
            k, t = divmod(q, piece_tiles)
            at = src_rows + t * hp + h
            return piece_refs[k][at : at + 1, :TILE], piece_refs[k][at + heads : at + heads + 1, :TILE]

        tops = []
        for h in range(heads):
            top = score_rows(0, h)[0]
            for q in range(1, half):
                top = jnp.maximum(top, score_rows(q, h)[0])
            tops.append(jnp.max(top, axis=1, keepdims=True))

        lane_w = lax.broadcasted_iota(jnp.int32, (block, width), 1) // dims
        lane_t = lax.broadcasted_iota(jnp.int32, (block, TILE), 1)

        def put(h, q, p, slot):
            cols = slice(q * TILE, (q + 1) * TILE)
            hi = p.astype(BF16)
            lo = (p - hi.astype(F32)).astype(BF16)
            probs[slot, 2 * h * block : (2 * h + 1) * block, cols] = hi
            probs[slot, (2 * h + 1) * block : (2 * h + 2) * block, cols] = lo

        def finish(at, slot, dens, ms):
            both = lax.dot_general(
                probs[slot], z_cat[...], (((1,), (0,)), ((), ())), preferred_element_type=F32
            )
            num = jnp.zeros((block, width), F32)
            md = jnp.zeros((block, TILE), F32)
            for h in range(heads):
                hi = both[2 * h * block : (2 * h + 1) * block]
                lo = both[(2 * h + 1) * block : (2 * h + 2) * block]
                num = jnp.where(lane_w == h, hi[:, :width] + (hi[:, width:] + lo[:, :width]), num)
                md = jnp.where(lane_t == h, dens[h], md)
                md = jnp.where(lane_t == heads + h, ms[h], md)
            num_ref[pl.ds(at, block), :] = num
            md_ref[pl.ds(at, block), :] = md

        base = step * group_rows
        worst = None
        for b in range(unroll * blocks):
            at = pl.multiple_of(base + b * block, block)
            rt, i0 = divmod(b * block, TILE)
            t_all = tgt[pl.ds(at, block), :]
            dens, ms = [], []
            for h in range(heads):
                a = t_all[:, h : h + 1]
                m = leaky(a + tops[h])
                pos = jnp.broadcast_to(a - m, (block, TILE))
                neg = jnp.broadcast_to(SLOPE * a - m, (block, TILE))
                den = jnp.zeros((block, TILE), F32)
                for q in range(half):
                    s, s_low = score_rows(q, h)
                    p = w_ref[rt, q, i0 : i0 + block, :] * jnp.exp2(
                        jnp.maximum(pos + s, neg + s_low)
                    )
                    den = den + p
                    put(h, q, p, b % 2)
                den = jnp.sum(den, axis=1, keepdims=True)
                worst = den if worst is None else jnp.minimum(worst, den)
                dens.append(den)
                ms.append(m)
            finish(at, b % 2, dens, ms)

        @pl.when(jnp.logical_not(jnp.min(worst) >= tiny))
        def _():
            @pl.loop(0, unroll * blocks)
            def _(b):
                at = pl.multiple_of(base + b * block, block)
                rt = b // blocks
                i0 = pl.multiple_of((b % blocks) * block, block)
                t_all = tgt[pl.ds(at, block), :]
                dens, ms = [], []
                for h in range(heads):
                    best = jnp.full((block, TILE), NEG, F32)
                    for q in range(half):
                        s, _ = score_rows(q, h)
                        edge = w_ref[rt, q, pl.ds(i0, block), :] > 0
                        best = jnp.maximum(best, jnp.where(edge, s, NEG))
                    a = t_all[:, h : h + 1]
                    m = leaky(a + jnp.max(best, axis=1, keepdims=True))
                    pos, neg = a - m, SLOPE * a - m
                    den = jnp.zeros((block, TILE), F32)
                    for q in range(half):
                        s, s_low = score_rows(q, h)
                        x = jnp.maximum(pos + s, neg + s_low)
                        p = w_ref[rt, q, pl.ds(i0, block), :] * jnp.exp2(jnp.minimum(x, 0.0))
                        den = den + p
                        put(h, q, p, 0)
                    dens.append(jnp.sum(den, axis=1, keepdims=True))
                    ms.append(m)
                finish(at, 0, dens, ms)

    def split_z(piece_refs, z_cat):
        for k in range(n_piece):
            z = piece_refs[k][:src_rows, :width]
            hi = z.astype(BF16)
            z_cat[k * src_rows : (k + 1) * src_rows, :width] = hi
            z_cat[k * src_rows : (k + 1) * src_rows, width:] = (z - hi.astype(F32)).astype(BF16)

    def near_kernel(*refs):
        tgt_refs, refs = refs[:n_col], refs[n_col:]
        piece_refs, refs = refs[:n_piece], refs[n_piece:]
        w_ref, tgt, num_ref, md_ref, z_cat, probs = refs
        col = lax.axis_index("col")

        @pl.when(pl.program_id(0) == 0)
        def _():
            shape = (up8(heads), TILE)
            eye = (
                lax.broadcasted_iota(jnp.int32, shape, 0)
                == lax.broadcasted_iota(jnp.int32, shape, 1)
            ).astype(F32)
            for d in range(n_col):
                at = pl.multiple_of(comes_from(col, d, n_col) * own_rows, own_rows)
                tgt[pl.ds(at, own_rows), :] = contract(tgt_refs[d][...], eye, ((0,), (0,)))
            split_z(piece_refs, z_cat)

        attend(tgt, piece_refs, w_ref, z_cat, probs, num_ref, md_ref)

    def far_kernel(*refs):
        tgt, near_num, near_md, refs = refs[0], refs[1], refs[2], refs[3:]
        piece_refs, refs = refs[:n_piece], refs[n_piece:]
        w_ref, refs = refs[0], refs[1:]
        out_refs, (num_ref, md_ref, z_cat, probs) = refs[:n_col], refs[n_col:]
        col = lax.axis_index("col")
        step = pl.program_id(0)

        @pl.when(step == 0)
        def _():
            split_z(piece_refs, z_cat)

        attend(tgt, piece_refs, w_ref, z_cat, probs, num_ref, md_ref)

        base = step * group_rows
        lane_w = lax.broadcasted_iota(jnp.int32, (TILE, width), 1) // dims
        lane_t = lax.broadcasted_iota(jnp.int32, (TILE, TILE), 1)
        for rt in range(unroll):
            at = pl.ds(pl.multiple_of(base + rt * TILE, TILE), TILE)
            near, far = near_md[at, :], md_ref[at, :]
            md = jnp.zeros((TILE, TILE), F32)
            f_near = jnp.zeros((TILE, width), F32)
            f_far = jnp.zeros((TILE, width), F32)
            for h in range(heads):
                m0, m1 = near[:, heads + h : heads + h + 1], far[:, heads + h : heads + h + 1]
                m = jnp.maximum(m0, m1)
                f0, f1 = jnp.exp2(m0 - m), jnp.exp2(m1 - m)
                den = near[:, h : h + 1] * f0 + far[:, h : h + 1] * f1
                md = jnp.where(lane_t == h, den, md)
                md = jnp.where(lane_t == heads + h, m, md)
                f_near = jnp.where(lane_w == h, f0, f_near)
                f_far = jnp.where(lane_w == h, f1, f_far)
            num = near_num[at, :] * f_near + num_ref[at, :] * f_far
            num_ref[at, :] = num
            md_ref[at, :] = md

        @pl.when(step == row_tiles // unroll - 1)
        def _():
            for d in range(n_col):
                at = pl.multiple_of(goes_to(col, d, n_col) * own_rows, own_rows)
                if width < lanes:
                    out_refs[d][...] = jnp.zeros_like(out_refs[d])
                out_refs[d][:own_rows, :width] = num_ref[pl.ds(at, own_rows), :]
                out_refs[d][own_rows:, :own_rows] = md_ref[pl.ds(at, own_rows), :].T[:mdp]

    scratch = [
        pltpu.VMEM((k_all, 2 * width), BF16),
        pltpu.VMEM((2, 2 * heads * block, k_all), BF16),
    ]
    cost = pl.CostEstimate(
        flops=all_rows * k_all * width * heads * 8,
        bytes_accessed=k_all * width * 4,
        transcendentals=all_rows * k_all * heads,
    )
    w_spec = pl.BlockSpec((unroll, half, TILE, TILE), lambda s: (s, 0, 0, 0))
    rows_shape = [(all_rows, TILE), (all_rows, width), (all_rows, TILE)]
    params = pltpu.CompilerParams(vmem_limit_bytes=limit(32, 8 * tiles * TILE * TILE))
    tgt, near_num, near_md = pl.pallas_call(
        near_kernel,
        out_shape=[jax.ShapeDtypeStruct(s, F32) for s in rows_shape],
        grid=(row_tiles // unroll,),
        in_specs=[whole((up8(heads), own_rows))] * n_col
        + [whole((pack_rows, lanes))] * n_piece
        + [w_spec],
        out_specs=[whole(s) for s in rows_shape],
        scratch_shapes=scratch,
        cost_estimate=cost,
        compiler_params=params,
    )(*targets, *near_pieces, panels[0])
    far0, tgt, near_num, near_md = lax.optimization_barrier((far0, tgt, near_num, near_md))
    far_pieces = spread(far0)
    chunk = (chunk_rows, lanes)
    chunks = pl.pallas_call(
        far_kernel,
        out_shape=[jax.ShapeDtypeStruct(chunk, F32)] * n_col,
        grid=(row_tiles // unroll,),
        in_specs=[whole(s) for s in rows_shape]
        + [whole((pack_rows, lanes))] * n_piece
        + [w_spec],
        out_specs=[whole(chunk)] * n_col,
        scratch_shapes=[pltpu.VMEM(s, F32) for s in rows_shape[1:]] + scratch,
        cost_estimate=cost,
        compiler_params=params,
    )(tgt, near_num, near_md, *far_pieces, panels[1])
    gathered = [hop(chunks[d], "col", d) for d in range(n_col - 1, 0, -1)]
    gathered = [chunks[0]] + gathered[::-1]

    def out_kernel(zdst_ref, src_ref, dst_ref, bias_ref, *rest):
        parts, out_ref = rest[:n_col], rest[n_col]
        same = (
            lax.broadcasted_iota(jnp.int32, (width, width), 0) // dims
            == lax.broadcasted_iota(jnp.int32, (width, width), 1) // dims
        ).astype(F32)
        z = zdst_ref[...]
        pair = contract(z * (dst_ref[...] + src_ref[...]), same, ((1,), (0,)))
        e_self = leaky(LOG2E * pair)
        which = lax.broadcasted_iota(jnp.int32, (mdp, width), 0)
        head = lax.broadcasted_iota(jnp.int32, (mdp, width), 1) // dims
        den_of, m_of = (which == head).astype(F32), (which == head + heads).astype(F32)
        mds = [part[own_rows:, :own_rows] for part in parts]
        ms = [contract(md, m_of, ((0,), (0,))) for md in mds]
        dens = [contract(md, den_of, ((0,), (0,))) for md in mds]
        top = e_self
        for m in ms:
            top = jnp.maximum(top, m)
        den = jnp.exp2(e_self - top)
        num = den * z
        for part, m, own_den in zip(parts, ms, dens):
            factor = jnp.exp2(m - top)
            den = den + factor * own_den
            num = num + factor * part[:own_rows, :width]
        x = num / den + bias_ref[...]
        out_ref[...] = jnp.where(x > 0, x, jnp.exp(jnp.minimum(x, 0.0)) - 1.0).astype(BF16)

    return call(
        out_kernel,
        jax.ShapeDtypeStruct((own_rows, width), BF16),
        zdst,
        att_src2,
        att_dst2,
        bias2,
        *gathered,
    )


def solution(mesh):
    return jax.shard_map(
        on_device,
        mesh=mesh,
        in_specs=(
            P(("row", "col"), "feat"),
            P(("row", "col"), "feat"),
            P("feat", None),
            P("feat"),
            P("feat"),
            P("feat"),
            P("row", "col", None),
            P("row", "col", None),
            P("row", "col"),
            P("row", "col", None, None, None),
        ),
        out_specs=P(("row", "col"), "feat"),
        check_vma=False,
    )
```

```python
import jax
import jax.numpy as jnp
from jax import lax
from jax.experimental import pallas as pl
from jax.experimental.pallas import tpu as pltpu
from jax.sharding import PartitionSpec as P

HEADS = 8
TILE = 128
SLOPE = 0.2
LOG2E = 1.4426950408889634
NEG = -1e30
F32 = jnp.float32
BF16 = jnp.bfloat16
HIGHEST = lax.Precision.HIGHEST
VMEM = pl.BlockSpec(memory_space=pltpu.VMEM)
SMEM = pl.BlockSpec(memory_space=pltpu.SMEM)
HBM = pl.BlockSpec(memory_space=pltpu.HBM)


def is_pow2(n):
    return n & (n - 1) == 0


def goes_to(i, d, n):
    return i ^ d if is_pow2(n) else lax.rem(i + d, n)


def comes_from(i, d, n):
    return i ^ d if is_pow2(n) else lax.rem(i + n - d, n)


def hop(x, axis, d):
    n = lax.axis_size(axis)
    pairs = [(i, i ^ d if is_pow2(n) else (i + d) % n) for i in range(n)]
    return lax.ppermute(x, axis, pairs)


def call(kernel, out_shape, *args, in_specs=None, flops=0, bytes_accessed=0, grant=8 << 20, **kw):
    return pl.pallas_call(
        kernel,
        out_shape=out_shape,
        in_specs=in_specs or [VMEM] * len(args),
        cost_estimate=pl.CostEstimate(
            flops=flops, bytes_accessed=bytes_accessed, transcendentals=0
        ),
        compiler_params=pltpu.CompilerParams(vmem_limit_bytes=grant),
        **kw,
    )(*args)


def limit(mib, least):
    return min(max(mib << 20, least), 60 << 20)


def in_hbm(x):
    return pltpu.with_memory_space_constraint(x, pltpu.HBM)


def up8(n):
    return -(-n // 8) * 8


def head_rows(vector, heads, width, height):
    dims = width // heads
    shape = (height, width)
    row = lax.broadcasted_iota(jnp.int32, shape, 0) % heads
    lane = lax.broadcasted_iota(jnp.int32, shape, 1)
    return jnp.where(lane // dims == row, jnp.broadcast_to(vector, shape), 0.0)


def contract(lhs, rhs, dims, precision=HIGHEST):
    return lax.dot_general(
        lhs, rhs, (dims, ((), ())), preferred_element_type=F32, precision=precision
    )


def take_cols(proj_ref, which, width):
    if width % TILE == 0:
        return proj_ref[:, pl.ds(pl.multiple_of(which * width, width), width)]
    full = proj_ref[...]
    out = full[:, :width]
    for k in range(1, full.shape[1] // width):
        out = jnp.where(which == k, full[:, k * width : (k + 1) * width], out)
    return out


def project(x, w):
    return lax.dot_general(x, w, (((1,), (0,)), ((), ())), preferred_element_type=F32)


def leaky(x):
    return jnp.maximum(x, SLOPE * x)


def on_device(
    src_feats, dst_feats, proj, att_src, att_dst, bias, tile_rows, tile_cols, tile_count, edge_weight
):
    n_row, n_col, n_feat = (lax.axis_size(a) for a in ("row", "col", "feat"))
    width = proj.shape[1] // n_feat
    heads = HEADS // n_feat
    dims = width // heads
    lanes = -(-width // TILE) * TILE
    src_rows, own_rows = src_feats.shape[0], dst_feats.shape[0]
    slots = tile_rows.shape[2]
    row_tiles = own_rows * n_col // TILE
    piece_tiles = src_rows // TILE
    n_chunk = 2 if piece_tiles % 2 == 0 else 1
    chunk_tiles = piece_tiles // n_chunk
    part_rows = src_rows // n_chunk
    col_tiles = piece_tiles * n_row
    hp = up8(2 * heads)
    mdp = up8(2 * heads)
    att_src2, att_dst2, bias2 = (v.reshape(1, width) for v in (att_src, att_dst, bias))

    def fetch(hbm, vmem, sems):
        copies = [pltpu.make_async_copy(h, v, sems.at[k]) for k, (h, v) in enumerate(zip(hbm, vmem))]
        for copy in copies:
            copy.start()
        for copy in copies:
            copy.wait()

    def fetching(kernel, outs, *args):
        return call(
            kernel,
            outs,
            *map(in_hbm, args),
            in_specs=[HBM] * len(args),
            scratch_shapes=[
                *(pltpu.VMEM(v.shape, v.dtype) for v in args),
                pltpu.SemaphoreType.DMA((len(args),)),
            ],
        )

    def send_kernel(*refs):
        hbm, outs, (src_ref, dst_ref, proj_ref, sems) = refs[:3], refs[3:-4], refs[-4:]
        fetch(hbm, (src_ref, dst_ref, proj_ref), sems)
        me = lax.axis_index("feat")
        for d in range(1, n_feat):
            w = take_cols(proj_ref, goes_to(me, d, n_feat), width)
            own_outs = outs[(d - 1) * (n_chunk + 1) : d * (n_chunk + 1)]
            own_outs[0][...] = project(dst_ref[...], w)
            for ch in range(n_chunk):
                own_outs[ch + 1][...] = project(src_ref[ch * part_rows : (ch + 1) * part_rows], w)

    sent = fetching(
        send_kernel,
        [
            pltpu.VMEM((n, width), F32)
            for _ in range(1, n_feat)
            for n in [own_rows] + [part_rows] * n_chunk
        ],
        src_feats,
        dst_feats,
        proj,
    )
    sent = [sent[k :: n_chunk + 1] for k in range(n_chunk + 1)]
    dst_parts = [hop(sent[0][d - 1], "feat", d) for d in range(1, n_feat)]
    src_parts = [[hop(part[d - 1], "feat", d) for d in range(1, n_feat)] for part in sent[1:]]

    def own_kernel(*refs):
        hbm, outs, refs = refs[:5], refs[5 : 8 + n_chunk], refs[8 + n_chunk :]
        fetch(hbm, refs[:5], refs[5])
        src_ref, dst_ref, proj_ref, att_src_ref, att_dst_ref = refs[:5]
        w = take_cols(proj_ref, lax.axis_index("feat"), width)
        outs[0][...] = project(dst_ref[...], w)
        outs[1][...] = LOG2E * head_rows(att_dst_ref[...], heads, width, up8(heads))
        outs[2][...] = LOG2E * head_rows(att_src_ref[...], heads, width, hp)
        for ch in range(n_chunk):
            outs[3 + ch][...] = project(src_ref[ch * part_rows : (ch + 1) * part_rows], w)

    dst_own, dst_att, src_att, *src_own = fetching(
        own_kernel,
        [
            pltpu.VMEM((own_rows, width), F32),
            pltpu.VMEM((up8(heads), width), F32),
            pltpu.VMEM((hp, width), F32),
        ]
        + [pltpu.VMEM((part_rows, width), F32)] * n_chunk,
        src_feats,
        dst_feats,
        proj,
        att_src2,
        att_dst2,
    )
    dst_parts, src_own = lax.optimization_barrier((dst_parts, src_own))

    tiles = row_tiles * col_tiles
    whole = lambda shape: pl.BlockSpec(shape, lambda s: (0,) * len(shape))

    def dst_kernel(own_ref, att_ref, *rest):
        got, (z_ref, s_ref) = rest[: n_feat - 1], rest[n_feat - 1 :]
        z = own_ref[...]
        for part in got:
            z = z + part[...]
        z_ref[...] = z
        s_ref[...] = contract(att_ref[...], z, ((1,), (1,)))

    zdst, s_dst = call(
        dst_kernel,
        [
            jax.ShapeDtypeStruct((own_rows, width), F32),
            jax.ShapeDtypeStruct((up8(heads), own_rows), F32),
        ],
        dst_own,
        dst_att,
        *dst_parts,
    )
    targets = [hop(s_dst, "col", d) for d in range(n_col - 1, 0, -1)]
    targets = [s_dst] + targets[::-1]


    pack_rows = part_rows + chunk_tiles * hp

    def z_kernel(own_ref, att_ref, *rest):
        got, out_ref = rest[: n_feat - 1], rest[n_feat - 1]
        z = own_ref[...]
        for part in got:
            z = z + part[...]
        if width < lanes:
            out_ref[...] = jnp.zeros_like(out_ref)
        out_ref[:part_rows, :width] = z
        s = contract(att_ref[...], z, ((1,), (1,)))
        low = lax.broadcasted_iota(jnp.int32, s.shape, 0) < heads
        s = jnp.where(low, s, SLOPE * s)
        for t in range(chunk_tiles):
            at = part_rows + t * hp
            out_ref[at : at + hp, :TILE] = s[:, t * TILE : (t + 1) * TILE]

    parts, far_first = {}, n_row // 2
    for ch in range(n_chunk):
        own = call(z_kernel, pltpu.VMEM((pack_rows, lanes), F32), src_own[ch], src_att, *src_parts[ch])
        parts[far_first, ch] = hop(own, "row", far_first)
        parts[0, ch] = own
    last = n_chunk - 1
    parts[0, last], tile_rows = lax.optimization_barrier((parts[0, last], tile_rows))

    def spread(first, ch):
        d = n_row // 4
        while d:
            for k in [k for k, c in parts if c == ch and k ^ first < far_first]:
                parts[k ^ d, ch] = hop(parts[k, ch], "row", d)
            d //= 2

    for ch in range(n_chunk):
        spread(0, ch)

    units = n_row * n_chunk
    period = min(slots, tiles) if slots % min(slots, tiles) == 0 else slots
    reps = slots // period
    group = 8
    groups = period // group

    def weight_kernel(rows_hbm, cols_hbm, count_ref, w_hbm, panel_ref, *scratch):
        rows_ref, cols_ref, w_ref, index_sems, w_sems = scratch
        row = lax.axis_index("row")
        indices = [
            pltpu.make_async_copy(rows_hbm, rows_ref, index_sems.at[0]),
            pltpu.make_async_copy(cols_hbm, cols_ref, index_sems.at[1]),
        ]
        blocks = [
            pltpu.make_async_copy(
                w_hbm.at[k, pl.ds(g * group, group)],
                w_ref.at[k, pl.ds(g * group, group)],
                w_sems.at[g, k],
            )
            for g in range(groups)
            for k in range(reps)
        ]
        for copy in indices + blocks:
            copy.start()

        @pl.loop(0, units)
        def _(u):
            @pl.loop(0, row_tiles)
            def _(r):
                panel_ref[u, r] = jnp.zeros((chunk_tiles, TILE, TILE), F32)

        for copy in indices:
            copy.wait()
        count = count_ref[0, 0]
        for g in range(groups):
            for copy in blocks[g * reps : (g + 1) * reps]:
                copy.wait()
            base = g * group

            @pl.loop(base, jnp.clip(count, base, base + group))
            def _(u):
                r, c = rows_ref[0, 0, u], cols_ref[0, 0, u]
                unit = ((c // piece_tiles) ^ row) * n_chunk + c % piece_tiles // chunk_tiles
                t = c % chunk_tiles
                total = w_ref[0, u].astype(F32)
                for k in range(1, reps):
                    live = (u + k * period < count).astype(F32)
                    total = total + w_ref[k, u].astype(F32) * live
                panel_ref[unit, r, t] = panel_ref[unit, r, t] + total

    panel = call(
        weight_kernel,
        pltpu.VMEM((units, row_tiles, chunk_tiles, TILE, TILE), F32),
        in_hbm(tile_rows),
        in_hbm(tile_cols),
        tile_count,
        in_hbm(edge_weight.reshape(reps, period, TILE, TILE)),
        in_specs=[HBM, HBM, SMEM, HBM],
        scratch_shapes=[
            pltpu.SMEM(tile_rows.shape, jnp.int32),
            pltpu.SMEM(tile_cols.shape, jnp.int32),
            pltpu.VMEM((reps, period, TILE, TILE), edge_weight.dtype),
            pltpu.SemaphoreType.DMA((2,)),
            pltpu.SemaphoreType.DMA((groups, reps)),
        ],
        flops=slots * TILE * TILE,
        bytes_accessed=slots * TILE * TILE * 2,
        grant=12 << 20,
    )

    block = 64
    blocks = TILE // block
    unroll = 2 if row_tiles % 2 == 0 else 1
    steps = row_tiles // unroll
    chunk_rows = own_rows + mdp
    group_rows = unroll * TILE
    all_rows = row_tiles * TILE
    tiny, huge = 2.0**-60, 2.0**60
    lane_w = lambda: lax.broadcasted_iota(jnp.int32, (block, width), 1) // dims
    lane_t = lambda: lax.broadcasted_iota(jnp.int32, (block, TILE), 1)

    def score_rows(part_ref, t, h):
        at = part_rows + t * hp + h
        return part_ref[at : at + 1, :TILE], part_ref[at + heads : at + heads + 1, :TILE]

    def split_z(part_ref, z_cat, k):
        z = part_ref[:part_rows, :width]
        hi = z.astype(BF16)
        z_cat[k * part_rows : (k + 1) * part_rows, :width] = hi
        z_cat[k * part_rows : (k + 1) * part_rows, width:] = (z - hi.astype(F32)).astype(BF16)

    def put(probs, slot, h, q, p):
        cols = slice(q * TILE, (q + 1) * TILE)
        hi = p.astype(BF16)
        probs[slot, 2 * h * block : (2 * h + 1) * block, cols] = hi
        probs[slot, (2 * h + 1) * block : (2 * h + 2) * block, cols] = (
            p - hi.astype(F32)
        ).astype(BF16)

    def weighted(probs, z):
        both = lax.dot_general(probs, z, (((1,), (0,)), ((), ())), preferred_element_type=F32)
        num = jnp.zeros((block, width), F32)
        for h in range(heads):
            hi = both[2 * h * block : (2 * h + 1) * block]
            lo = both[(2 * h + 1) * block : (2 * h + 2) * block]
            num = jnp.where(lane_w() == h, hi[:, :width] + (hi[:, width:] + lo[:, :width]), num)
        return num

    def attend(part_refs, w_refs, posneg, den_in, num_in, den_out, num_out, z_cat, probs):
        base = pl.program_id(0) * group_rows
        for b in range(unroll * blocks):
            at = pl.ds(pl.multiple_of(base + b * block, block), block)
            rt, i0 = divmod(b * block, TILE)
            for h in range(heads):
                pn = posneg[at, :]
                pos = jnp.broadcast_to(pn[:, h : h + 1], (block, TILE))
                neg = jnp.broadcast_to(pn[:, heads + h : heads + h + 1], (block, TILE))
                den = jnp.zeros((block, TILE), F32) if den_in is None else den_in[h, at, :]
                for k, part_ref in enumerate(part_refs):
                    for t in range(chunk_tiles):
                        s, s_low = score_rows(part_ref, t, h)
                        x = jnp.maximum(pos + s, neg + s_low)
                        p = w_refs[k][0, rt, t, i0 : i0 + block, :] * jnp.exp2(x)
                        den = den + p
                        put(probs, b % 2, h, k * chunk_tiles + t, p)
                den_out[h, at, :] = den
            num = weighted(probs[b % 2], z_cat[...])
            num_out[at, :] = num if num_in is None else num_in[at, :] + num

    shape_t, shape_w, shape_d = (all_rows, TILE), (all_rows, width), (heads, all_rows, TILE)
    part_spec = whole((pack_rows, lanes))

    def unit_spec(k, ch):
        return pl.BlockSpec(
            (1, unroll, chunk_tiles, TILE, TILE), lambda s: (k * n_chunk + ch, s, 0, 0, 0)
        )

    def stage(kernel, keys, before, before_shapes, outs, extra=(), scratch=()):
        n = len(keys)
        return pl.pallas_call(
            kernel,
            out_shape=[pltpu.VMEM(s, F32) for s in outs],
            grid=(steps,),
            in_specs=[whole(s) for s in before_shapes]
            + [part_spec] * (n + len(extra))
            + [unit_spec(*key) for key in (*keys, *extra)],
            out_specs=[whole(s) for s in outs],
            scratch_shapes=[
                pltpu.VMEM((n * part_rows, 2 * width), BF16),
                pltpu.VMEM((2, 2 * heads * block, n * part_rows), BF16),
                *scratch,
            ],
            cost_estimate=pl.CostEstimate(
                flops=all_rows * n * part_rows * width * heads * 8,
                bytes_accessed=n * part_rows * width * 4,
                transcendentals=all_rows * n * part_rows * heads,
            ),
            compiler_params=pltpu.CompilerParams(vmem_limit_bytes=limit(16, 4 * tiles * TILE * TILE)),
        )(*before, *(parts[key] for key in (*keys, *extra)), *[panel] * (n + len(extra)))

    near_keys = [(k, ch) for ch in range(n_chunk) for k in range(far_first)]

    def near_kernel(*refs):
        n = len(near_keys)
        tgt_refs, part_refs, w_refs = refs[:n_col], refs[n_col : n_col + n], refs[n_col + n :][:n]
        posneg, tgt_m, den_out, num_out, z_cat, probs, tgt = refs[n_col + 2 * n :]
        col = lax.axis_index("col")

        @pl.when(pl.program_id(0) == 0)
        def _():
            shape = (up8(heads), TILE)
            eye = (
                lax.broadcasted_iota(jnp.int32, shape, 0)
                == lax.broadcasted_iota(jnp.int32, shape, 1) % heads
            ).astype(F32)
            lane = lax.broadcasted_iota(jnp.int32, (1, TILE), 1)
            bound = jnp.zeros((1, TILE), F32)
            for h in range(heads):
                rows = [score_rows(r, t, h)[0] for r in part_refs for t in range(chunk_tiles)]
                top = rows[0]
                for other in rows[1:]:
                    top = jnp.maximum(top, other)
                top = jnp.max(top, axis=1, keepdims=True)
                bound = jnp.where(lane % heads == h, top, bound)
            for d in range(n_col):
                at = pl.ds(
                    pl.multiple_of(comes_from(col, d, n_col) * own_rows, own_rows), own_rows
                )
                a = contract(tgt_refs[d][...], eye, ((0,), (0,)))
                m = leaky(a + bound)
                tgt[at, :] = a
                tgt_m[at, :] = jnp.where(lane < heads, a, m)
                posneg[at, :] = jnp.where(lane < heads, a, SLOPE * a) - m
            for k, part_ref in enumerate(part_refs):
                split_z(part_ref, z_cat, k)

        attend(part_refs, w_refs, posneg, None, None, den_out, num_out, z_cat, probs)

    def middle_kernel(*refs):
        n = len(middle_keys)
        (posneg, den_in, num_in), refs = refs[:3], refs[3:]
        part_refs, w_refs, (den_out, num_out, z_cat, probs) = refs[:n], refs[n : 2 * n], refs[2 * n :]

        @pl.when(pl.program_id(0) == 0)
        def _():
            for k, part_ref in enumerate(part_refs):
                split_z(part_ref, z_cat, k)

        attend(part_refs, w_refs, posneg, den_in, num_in, den_out, num_out, z_cat, probs)

    def last_kernel(*refs):
        n, n_all = len(last_keys), len(last_keys) + len(other_keys)
        (posneg, den_in, num_in, tgt_m), refs = refs[:4], refs[4:]
        part_refs, w_refs, refs = refs[:n_all], refs[n_all : 2 * n_all], refs[2 * n_all :]
        out_refs, (z_cat, probs, den_s, num_s, md_s, z_one) = refs[:n_col], refs[n_col:]
        col = lax.axis_index("col")
        step = pl.program_id(0)

        @pl.when(step == 0)
        def _():
            for k in range(n):
                split_z(part_refs[k], z_cat, k)

        attend(part_refs[:n], w_refs[:n], posneg, den_in, num_in, den_s, num_s, z_cat, probs)
        base = step * group_rows
        low = high = None
        for b in range(unroll * blocks):
            at = pl.ds(pl.multiple_of(base + b * block, block), block)
            md = tgt_m[at, :]
            for h in range(heads):
                den = jnp.sum(den_s[h, at, :], axis=1, keepdims=True)
                low = den if low is None else jnp.minimum(low, den)
                high = den if high is None else jnp.maximum(high, den)
                md = jnp.where(lane_t() == h, den, md)
            md_s[at, :] = md
        fine = jnp.logical_and(jnp.min(low) >= tiny, jnp.max(high) <= huge)

        @pl.when(jnp.logical_not(fine))
        def _():
            @pl.loop(0, unroll * blocks)
            def _(b):
                at = pl.ds(pl.multiple_of(base + b * block, block), block)
                rt = b // blocks
                rows = pl.ds(pl.multiple_of((b % blocks) * block, block), block)
                md = tgt_m[at, :]
                posnegs, dens = [], []
                for h in range(heads):
                    best = jnp.full((block, TILE), NEG, F32)
                    for part_ref, w_ref in zip(part_refs, w_refs):
                        for t in range(chunk_tiles):
                            edge = w_ref[0, rt, t, rows, :] > 0
                            s = score_rows(part_ref, t, h)[0]
                            best = jnp.maximum(best, jnp.where(edge, s, NEG))
                    a = tgt_m[at, :][:, h : h + 1]
                    m = leaky(a + jnp.max(best, axis=1, keepdims=True))
                    md = jnp.where(lane_t() == heads + h, m, md)
                    posnegs.append((a - m, SLOPE * a - m))
                    dens.append(jnp.zeros((block, TILE), F32))
                num_s[at, :] = jnp.zeros((block, width), F32)
                for part_ref, w_ref in zip(part_refs, w_refs):
                    for h in range(heads):
                        pos, neg = posnegs[h]
                        for t in range(chunk_tiles):
                            s, s_low = score_rows(part_ref, t, h)
                            x = jnp.minimum(jnp.maximum(pos + s, neg + s_low), 0.0)
                            p = w_ref[0, rt, t, rows, :] * jnp.exp2(x)
                            dens[h] = dens[h] + p
                            put(probs, 0, h, t, p)
                    split_z(part_ref, z_one, 0)
                    num_s[at, :] = num_s[at, :] + weighted(probs[0, :, :part_rows], z_one[...])
                for h in range(heads):
                    md = jnp.where(lane_t() == h, jnp.sum(dens[h], axis=1, keepdims=True), md)
                md_s[at, :] = md

        @pl.when(step == steps - 1)
        def _():
            for d in range(n_col):
                at = pl.ds(
                    pl.multiple_of(goes_to(col, d, n_col) * own_rows, own_rows), own_rows
                )
                if width < lanes:
                    out_refs[d][...] = jnp.zeros_like(out_refs[d])
                out_refs[d][:own_rows, :width] = num_s[at, :]
                out_refs[d][own_rows:, :own_rows] = md_s[at, :].T[:mdp]

    if n_chunk > 1:
        parts[far_first, 0], targets = lax.optimization_barrier((parts[far_first, 0], targets))
        spread(far_first, 0)
    posneg, tgt_m, den, num = stage(
        near_kernel,
        near_keys,
        targets,
        [(up8(heads), own_rows)] * n_col,
        [shape_t, shape_t, shape_d, shape_w],
        scratch=[pltpu.VMEM(shape_t, F32)],
    )
    parts[far_first, last], den = lax.optimization_barrier((parts[far_first, last], den))
    spread(far_first, last)
    middle_keys = [(k, ch) for ch in range(last) for k in range(far_first, n_row)]
    if middle_keys:
        den, num = stage(
            middle_kernel,
            middle_keys,
            (posneg, den, num),
            [shape_t, shape_d, shape_w],
            [shape_d, shape_w],
        )
    last_keys = [(k, last) for k in range(far_first, n_row)]
    other_keys = near_keys + middle_keys
    chunks = stage(
        last_kernel,
        last_keys,
        (posneg, den, num, tgt_m),
        [shape_t, shape_d, shape_w, shape_t],
        [(chunk_rows, lanes)] * n_col,
        extra=other_keys,
        scratch=[
            pltpu.VMEM(shape_d, F32),
            pltpu.VMEM(shape_w, F32),
            pltpu.VMEM(shape_t, F32),
            pltpu.VMEM((part_rows, 2 * width), BF16),
        ],
    )
    gathered = [hop(chunks[d], "col", d) for d in range(n_col - 1, 0, -1)]
    gathered = [chunks[0]] + gathered[::-1]

    def out_kernel(zdst_ref, src_ref, dst_ref, bias_ref, *rest):
        parts, out_ref = rest[:n_col], rest[n_col]
        same = (
            lax.broadcasted_iota(jnp.int32, (width, width), 0) // dims
            == lax.broadcasted_iota(jnp.int32, (width, width), 1) // dims
        ).astype(F32)
        z = zdst_ref[...]
        pair = contract(z * (dst_ref[...] + src_ref[...]), same, ((1,), (0,)))
        e_self = leaky(LOG2E * pair)
        which = lax.broadcasted_iota(jnp.int32, (mdp, width), 0)
        head = lax.broadcasted_iota(jnp.int32, (mdp, width), 1) // dims
        den_of, m_of = (which == head).astype(F32), (which == head + heads).astype(F32)
        mds = [part[own_rows:, :own_rows] for part in parts]
        ms = [contract(md, m_of, ((0,), (0,))) for md in mds]
        dens = [contract(md, den_of, ((0,), (0,))) for md in mds]
        top = e_self
        for m in ms:
            top = jnp.maximum(top, m)
        den = jnp.exp2(e_self - top)
        num = den * z
        for part, m, own_den in zip(parts, ms, dens):
            factor = jnp.exp2(m - top)
            den = den + factor * own_den
            num = num + factor * part[:own_rows, :width]
        x = num / den + bias_ref[...]
        out_ref[...] = jnp.where(x > 0, x, jnp.exp(jnp.minimum(x, 0.0)) - 1.0).astype(BF16)

    return call(
        out_kernel,
        jax.ShapeDtypeStruct((own_rows, width), BF16),
        zdst,
        att_src2,
        att_dst2,
        bias2,
        *gathered,
    )


def solution(mesh):
    return jax.shard_map(
        on_device,
        mesh=mesh,
        in_specs=(
            P(("row", "col"), "feat"),
            P(("row", "col"), "feat"),
            P("feat", None),
            P("feat"),
            P("feat"),
            P("feat"),
            P("row", "col", None),
            P("row", "col", None),
            P("row", "col"),
            P("row", "col", None, None, None),
        ),
        out_specs=P(("row", "col"), "feat"),
        check_vma=False,
    )
```

```python
import jax
import jax.numpy as jnp
from jax import lax
from jax.experimental import pallas as pl
from jax.experimental.pallas import tpu as pltpu
from jax.sharding import PartitionSpec as P

HEADS = 8
TILE = 128
SLOPE = 0.2
LOG2E = 1.4426950408889634
NEG = -1e30
F32 = jnp.float32
BF16 = jnp.bfloat16
HIGHEST = lax.Precision.HIGHEST
VMEM = pl.BlockSpec(memory_space=pltpu.VMEM)
SMEM = pl.BlockSpec(memory_space=pltpu.SMEM)
HBM = pl.BlockSpec(memory_space=pltpu.HBM)


def is_pow2(n):
    return n & (n - 1) == 0


def goes_to(i, d, n):
    return i ^ d if is_pow2(n) else lax.rem(i + d, n)


def comes_from(i, d, n):
    return i ^ d if is_pow2(n) else lax.rem(i + n - d, n)


def hop(x, axis, d):
    n = lax.axis_size(axis)
    pairs = [(i, i ^ d if is_pow2(n) else (i + d) % n) for i in range(n)]
    return lax.ppermute(x, axis, pairs)


def call(kernel, out_shape, *args, in_specs=None, flops=0, bytes_accessed=0, grant=8 << 20, **kw):
    return pl.pallas_call(
        kernel,
        out_shape=out_shape,
        in_specs=in_specs or [VMEM] * len(args),
        cost_estimate=pl.CostEstimate(
            flops=flops, bytes_accessed=bytes_accessed, transcendentals=0
        ),
        compiler_params=pltpu.CompilerParams(vmem_limit_bytes=grant),
        **kw,
    )(*args)


def limit(mib, least):
    return min(max(mib << 20, least), 60 << 20)


def in_hbm(x):
    return pltpu.with_memory_space_constraint(x, pltpu.HBM)


def up8(n):
    return -(-n // 8) * 8


def head_rows(vector, heads, width, height):
    dims = width // heads
    shape = (height, width)
    row = lax.broadcasted_iota(jnp.int32, shape, 0) % heads
    lane = lax.broadcasted_iota(jnp.int32, shape, 1)
    return jnp.where(lane // dims == row, jnp.broadcast_to(vector, shape), 0.0)


def contract(lhs, rhs, dims, precision=HIGHEST):
    return lax.dot_general(
        lhs, rhs, (dims, ((), ())), preferred_element_type=F32, precision=precision
    )


def take_cols(proj_ref, which, width):
    if width % TILE == 0:
        return proj_ref[:, pl.ds(pl.multiple_of(which * width, width), width)]
    full = proj_ref[...]
    out = full[:, :width]
    for k in range(1, full.shape[1] // width):
        out = jnp.where(which == k, full[:, k * width : (k + 1) * width], out)
    return out


def project(x, w):
    return lax.dot_general(x, w, (((1,), (0,)), ((), ())), preferred_element_type=F32)


def leaky(x):
    return jnp.maximum(x, SLOPE * x)


def on_device(
    src_feats, dst_feats, proj, att_src, att_dst, bias, tile_rows, tile_cols, tile_count, edge_weight
):
    n_row, n_col, n_feat = (lax.axis_size(a) for a in ("row", "col", "feat"))
    width = proj.shape[1] // n_feat
    heads = HEADS // n_feat
    dims = width // heads
    lanes = -(-width // TILE) * TILE
    src_rows, own_rows = src_feats.shape[0], dst_feats.shape[0]
    slots = tile_rows.shape[2]
    row_tiles = own_rows * n_col // TILE
    piece_tiles = src_rows // TILE
    n_chunk = 2 if piece_tiles % 2 == 0 else 1
    chunk_tiles = piece_tiles // n_chunk
    part_rows = src_rows // n_chunk
    col_tiles = piece_tiles * n_row
    hp = up8(2 * heads)
    mdp = up8(2 * heads)
    att_src2, att_dst2, bias2 = (v.reshape(1, width) for v in (att_src, att_dst, bias))

    def fetch(hbm, vmem, sems):
        copies = [pltpu.make_async_copy(h, v, sems.at[k]) for k, (h, v) in enumerate(zip(hbm, vmem))]
        for copy in copies:
            copy.start()
        for copy in copies:
            copy.wait()

    def fetching(kernel, outs, *args):
        return call(
            kernel,
            outs,
            *map(in_hbm, args),
            in_specs=[HBM] * len(args),
            scratch_shapes=[
                *(pltpu.VMEM(v.shape, v.dtype) for v in args),
                pltpu.SemaphoreType.DMA((len(args),)),
            ],
        )

    def send_kernel(*refs):
        hbm, outs, (src_ref, dst_ref, proj_ref, sems) = refs[:3], refs[3:-4], refs[-4:]
        fetch(hbm, (src_ref, dst_ref, proj_ref), sems)
        me = lax.axis_index("feat")
        for d in range(1, n_feat):
            w = take_cols(proj_ref, goes_to(me, d, n_feat), width)
            own_outs = outs[(d - 1) * (n_chunk + 1) : d * (n_chunk + 1)]
            own_outs[0][...] = project(dst_ref[...], w)
            for ch in range(n_chunk):
                own_outs[ch + 1][...] = project(src_ref[ch * part_rows : (ch + 1) * part_rows], w)

    sent = fetching(
        send_kernel,
        [
            pltpu.VMEM((n, width), F32)
            for _ in range(1, n_feat)
            for n in [own_rows] + [part_rows] * n_chunk
        ],
        src_feats,
        dst_feats,
        proj,
    )
    sent = [sent[k :: n_chunk + 1] for k in range(n_chunk + 1)]
    dst_parts = [hop(sent[0][d - 1], "feat", d) for d in range(1, n_feat)]
    src_parts = [[hop(part[d - 1], "feat", d) for d in range(1, n_feat)] for part in sent[1:]]

    units = n_row * n_chunk
    tiles = row_tiles * col_tiles
    period = min(slots, tiles) if slots % min(slots, tiles) == 0 else slots
    reps = slots // period
    group = 8
    groups = period // group

    def local_kernel(*refs):
        hbm, count_ref, refs = refs[:8], refs[8], refs[9:]
        outs, panel_ref, refs = refs[: 3 + n_chunk], refs[3 + n_chunk], refs[4 + n_chunk :]
        src_ref, dst_ref, proj_ref, att_src_ref, att_dst_ref, rows_ref, cols_ref, w_ref = refs[:8]
        sems, w_sems = refs[8:]
        small = [
            pltpu.make_async_copy(h, v, sems.at[k]) for k, (h, v) in enumerate(zip(hbm[:7], refs[:7]))
        ]
        large = [
            pltpu.make_async_copy(
                hbm[7].at[k, pl.ds(g * group, group)],
                w_ref.at[k, pl.ds(g * group, group)],
                w_sems.at[g, k],
            )
            for g in range(groups)
            for k in range(reps)
        ]
        for copy in small + large:
            copy.start()

        @pl.loop(0, units)
        def _(u):
            @pl.loop(0, row_tiles)
            def _(r):
                panel_ref[u, r] = jnp.zeros((chunk_tiles, TILE, TILE), F32)

        for copy in small:
            copy.wait()
        w = take_cols(proj_ref, lax.axis_index("feat"), width)
        outs[0][...] = project(dst_ref[...], w)
        outs[1][...] = LOG2E * head_rows(att_dst_ref[...], heads, width, up8(heads))
        outs[2][...] = LOG2E * head_rows(att_src_ref[...], heads, width, hp)
        for ch in range(n_chunk):
            outs[3 + ch][...] = project(src_ref[ch * part_rows : (ch + 1) * part_rows], w)

        row = lax.axis_index("row")
        count = count_ref[0, 0]
        for g in range(groups):
            for copy in large[g * reps : (g + 1) * reps]:
                copy.wait()
            base = g * group

            @pl.loop(base, jnp.clip(count, base, base + group))
            def _(u):
                r, c = rows_ref[0, 0, u], cols_ref[0, 0, u]
                unit = ((c // piece_tiles) ^ row) * n_chunk + c % piece_tiles // chunk_tiles
                t = c % chunk_tiles
                total = w_ref[0, u].astype(F32)
                for k in range(1, reps):
                    live = (u + k * period < count).astype(F32)
                    total = total + w_ref[k, u].astype(F32) * live
                panel_ref[unit, r, t] = panel_ref[unit, r, t] + total

    slot_weights = edge_weight.reshape(reps, period, TILE, TILE)
    inputs = (src_feats, dst_feats, proj, att_src2, att_dst2, tile_rows, tile_cols, slot_weights)
    dst_own, dst_att, src_att, *src_own, panel = call(
        local_kernel,
        [
            pltpu.VMEM((own_rows, width), F32),
            pltpu.VMEM((up8(heads), width), F32),
            pltpu.VMEM((hp, width), F32),
        ]
        + [pltpu.VMEM((part_rows, width), F32)] * n_chunk
        + [pltpu.VMEM((units, row_tiles, chunk_tiles, TILE, TILE), F32)],
        *map(in_hbm, inputs),
        tile_count,
        in_specs=[HBM] * len(inputs) + [SMEM],
        scratch_shapes=[
            *(
                (pltpu.SMEM if v.dtype == jnp.int32 else pltpu.VMEM)(v.shape, v.dtype)
                for v in inputs
            ),
            pltpu.SemaphoreType.DMA((7,)),
            pltpu.SemaphoreType.DMA((groups, reps)),
        ],
        grant=12 << 20,
    )
    dst_parts, src_own = lax.optimization_barrier((dst_parts, src_own))

    whole = lambda shape: pl.BlockSpec(shape, lambda s: (0,) * len(shape))

    def dst_kernel(own_ref, att_ref, *rest):
        got, (z_ref, s_ref) = rest[: n_feat - 1], rest[n_feat - 1 :]
        z = own_ref[...]
        for part in got:
            z = z + part[...]
        z_ref[...] = z
        s_ref[...] = contract(att_ref[...], z, ((1,), (1,)))

    zdst, s_dst = call(
        dst_kernel,
        [
            jax.ShapeDtypeStruct((own_rows, width), F32),
            jax.ShapeDtypeStruct((up8(heads), own_rows), F32),
        ],
        dst_own,
        dst_att,
        *dst_parts,
    )
    targets = [hop(s_dst, "col", d) for d in range(n_col - 1, 0, -1)]
    targets = [s_dst] + targets[::-1]


    pack_rows = part_rows + chunk_tiles * hp

    def z_kernel(own_ref, att_ref, *rest):
        got, out_ref = rest[: n_feat - 1], rest[n_feat - 1]
        z = own_ref[...]
        for part in got:
            z = z + part[...]
        if width < lanes:
            out_ref[...] = jnp.zeros_like(out_ref)
        out_ref[:part_rows, :width] = z
        s = contract(att_ref[...], z, ((1,), (1,)))
        low = lax.broadcasted_iota(jnp.int32, s.shape, 0) < heads
        s = jnp.where(low, s, SLOPE * s)
        for t in range(chunk_tiles):
            at = part_rows + t * hp
            out_ref[at : at + hp, :TILE] = s[:, t * TILE : (t + 1) * TILE]

    parts, far_first = {}, n_row // 2
    for ch in range(n_chunk):
        own = call(z_kernel, pltpu.VMEM((pack_rows, lanes), F32), src_own[ch], src_att, *src_parts[ch])
        parts[far_first, ch] = hop(own, "row", far_first)
        parts[0, ch] = own
    last = n_chunk - 1

    def spread(first, ch):
        d = n_row // 4
        while d:
            for k in [k for k, c in parts if c == ch and k ^ first < far_first]:
                parts[k ^ d, ch] = hop(parts[k, ch], "row", d)
            d //= 2

    for ch in range(n_chunk):
        spread(0, ch)

    block = 64
    blocks = TILE // block
    unroll = 2 if row_tiles % 2 == 0 else 1
    steps = row_tiles // unroll
    chunk_rows = own_rows + mdp
    group_rows = unroll * TILE
    all_rows = row_tiles * TILE
    tiny, huge = 2.0**-60, 2.0**60
    lane_w = lambda: lax.broadcasted_iota(jnp.int32, (block, width), 1) // dims
    lane_t = lambda: lax.broadcasted_iota(jnp.int32, (block, TILE), 1)

    def score_rows(part_ref, t, h):
        at = part_rows + t * hp + h
        return part_ref[at : at + 1, :TILE], part_ref[at + heads : at + heads + 1, :TILE]

    def split(x):
        hi = x.astype(BF16)
        return hi, (x - hi.astype(F32)).astype(BF16)

    def split_z(part_refs):
        return jnp.concatenate(
            [jnp.concatenate(split(p[:part_rows, :width]), axis=1) for p in part_refs], axis=0
        )

    def stack(pairs):
        return jnp.concatenate(
            [jnp.concatenate([p[k] for p in row], axis=1) for row in pairs for k in range(2)], axis=0
        )

    def weighted(probs, z):
        both = lax.dot_general(probs, z, (((1,), (0,)), ((), ())), preferred_element_type=F32)
        num = jnp.zeros((block, width), F32)
        for h in range(heads):
            hi = both[2 * h * block : (2 * h + 1) * block]
            lo = both[(2 * h + 1) * block : (2 * h + 2) * block]
            num = jnp.where(lane_w() == h, hi[:, :width] + (hi[:, width:] + lo[:, :width]), num)
        return num

    def attend(part_refs, w_refs, posneg, den_in, num_in, den_out, num_out):
        base = pl.program_id(0) * group_rows
        z_cat = split_z(part_refs)
        for b in range(unroll * blocks):
            at = pl.ds(pl.multiple_of(base + b * block, block), block)
            rt, i0 = divmod(b * block, TILE)
            pairs = []
            for h in range(heads):
                pairs.append([])
                pn = posneg[at, :]
                pos = jnp.broadcast_to(pn[:, h : h + 1], (block, TILE))
                neg = jnp.broadcast_to(pn[:, heads + h : heads + h + 1], (block, TILE))
                den = jnp.zeros((block, TILE), F32) if den_in is None else den_in[h, at, :]
                for k, part_ref in enumerate(part_refs):
                    for t in range(chunk_tiles):
                        s, s_low = score_rows(part_ref, t, h)
                        x = jnp.maximum(pos + s, neg + s_low)
                        p = w_refs[k][0, rt, t, i0 : i0 + block, :] * jnp.exp2(x)
                        den = den + p
                        pairs[h].append(split(p))
                den_out[h, at, :] = den
            num = weighted(stack(pairs), z_cat)
            num_out[at, :] = num if num_in is None else num_in[at, :] + num

    shape_t, shape_w, shape_d = (all_rows, TILE), (all_rows, width), (heads, all_rows, TILE)
    part_spec = whole((pack_rows, lanes))

    def unit_spec(k, ch):
        return pl.BlockSpec(
            (1, unroll, chunk_tiles, TILE, TILE), lambda s: (k * n_chunk + ch, s, 0, 0, 0)
        )

    def stage(kernel, keys, before, before_shapes, outs, extra=(), scratch=()):
        n = len(keys)
        return pl.pallas_call(
            kernel,
            out_shape=[pltpu.VMEM(s, F32) for s in outs],
            grid=(steps,),
            in_specs=[whole(s) for s in before_shapes]
            + [part_spec] * (n + len(extra))
            + [unit_spec(*key) for key in (*keys, *extra)],
            out_specs=[whole(s) for s in outs],
            scratch_shapes=scratch,
            cost_estimate=pl.CostEstimate(
                flops=all_rows * n * part_rows * width * heads * 8,
                bytes_accessed=n * part_rows * width * 4,
                transcendentals=all_rows * n * part_rows * heads,
            ),
            compiler_params=pltpu.CompilerParams(vmem_limit_bytes=limit(16, 4 * tiles * TILE * TILE)),
        )(*before, *(parts[key] for key in (*keys, *extra)), *[panel] * (n + len(extra)))

    near_keys = [(k, ch) for ch in range(n_chunk) for k in range(far_first)]

    def near_kernel(*refs):
        n = len(near_keys)
        tgt_refs, part_refs, w_refs = refs[:n_col], refs[n_col : n_col + n], refs[n_col + n :][:n]
        posneg, tgt_m, den_out, num_out = refs[n_col + 2 * n :]
        col = lax.axis_index("col")

        @pl.when(pl.program_id(0) == 0)
        def _():
            shape = (up8(heads), TILE)
            eye = (
                lax.broadcasted_iota(jnp.int32, shape, 0)
                == lax.broadcasted_iota(jnp.int32, shape, 1) % heads
            ).astype(F32)
            lane = lax.broadcasted_iota(jnp.int32, (1, TILE), 1)
            bound = jnp.zeros((1, TILE), F32)
            for h in range(heads):
                rows = [score_rows(r, t, h)[0] for r in part_refs for t in range(chunk_tiles)]
                top = rows[0]
                for other in rows[1:]:
                    top = jnp.maximum(top, other)
                top = jnp.max(top, axis=1, keepdims=True)
                bound = jnp.where(lane % heads == h, top, bound)
            for d in range(n_col):
                at = pl.ds(
                    pl.multiple_of(comes_from(col, d, n_col) * own_rows, own_rows), own_rows
                )
                a = contract(tgt_refs[d][...], eye, ((0,), (0,)))
                m = leaky(a + bound)
                tgt_m[at, :] = jnp.where(lane < heads, a, m)
                posneg[at, :] = jnp.where(lane < heads, a, SLOPE * a) - m

        attend(part_refs, w_refs, posneg, None, None, den_out, num_out)

    def middle_kernel(*refs):
        n = len(middle_keys)
        (posneg, den_in, num_in), refs = refs[:3], refs[3:]
        part_refs, w_refs, (den_out, num_out) = refs[:n], refs[n : 2 * n], refs[2 * n :]
        attend(part_refs, w_refs, posneg, den_in, num_in, den_out, num_out)

    def last_kernel(*refs):
        n, n_all = len(last_keys), len(last_keys) + len(other_keys)
        (posneg, den_in, num_in, tgt_m), refs = refs[:4], refs[4:]
        part_refs, w_refs, refs = refs[:n_all], refs[n_all : 2 * n_all], refs[2 * n_all :]
        out_refs, (den_s, num_s, md_s) = refs[:n_col], refs[n_col:]
        col = lax.axis_index("col")
        step = pl.program_id(0)

        attend(part_refs[:n], w_refs[:n], posneg, den_in, num_in, den_s, num_s)
        base = step * group_rows
        low = high = None
        for b in range(unroll * blocks):
            at = pl.ds(pl.multiple_of(base + b * block, block), block)
            md = tgt_m[at, :]
            for h in range(heads):
                den = jnp.sum(den_s[h, at, :], axis=1, keepdims=True)
                low = den if low is None else jnp.minimum(low, den)
                high = den if high is None else jnp.maximum(high, den)
                md = jnp.where(lane_t() == h, den, md)
            md_s[at, :] = md
        fine = jnp.logical_and(jnp.min(low) >= tiny, jnp.max(high) <= huge)

        @pl.when(jnp.logical_not(fine))
        def _():
            @pl.loop(0, unroll * blocks)
            def _(b):
                at = pl.ds(pl.multiple_of(base + b * block, block), block)
                rt = b // blocks
                rows = pl.ds(pl.multiple_of((b % blocks) * block, block), block)
                md = tgt_m[at, :]
                posnegs, dens = [], []
                for h in range(heads):
                    best = jnp.full((block, TILE), NEG, F32)
                    for part_ref, w_ref in zip(part_refs, w_refs):
                        for t in range(chunk_tiles):
                            edge = w_ref[0, rt, t, rows, :] > 0
                            s = score_rows(part_ref, t, h)[0]
                            best = jnp.maximum(best, jnp.where(edge, s, NEG))
                    a = tgt_m[at, :][:, h : h + 1]
                    m = leaky(a + jnp.max(best, axis=1, keepdims=True))
                    md = jnp.where(lane_t() == heads + h, m, md)
                    posnegs.append((a - m, SLOPE * a - m))
                    dens.append(jnp.zeros((block, TILE), F32))
                num_s[at, :] = jnp.zeros((block, width), F32)
                for part_ref, w_ref in zip(part_refs, w_refs):
                    pairs = []
                    for h in range(heads):
                        pairs.append([])
                        pos, neg = posnegs[h]
                        for t in range(chunk_tiles):
                            s, s_low = score_rows(part_ref, t, h)
                            x = jnp.minimum(jnp.maximum(pos + s, neg + s_low), 0.0)
                            p = w_ref[0, rt, t, rows, :] * jnp.exp2(x)
                            dens[h] = dens[h] + p
                            pairs[h].append(split(p))
                    num_s[at, :] = num_s[at, :] + weighted(stack(pairs), split_z([part_ref]))
                for h in range(heads):
                    md = jnp.where(lane_t() == h, jnp.sum(dens[h], axis=1, keepdims=True), md)
                md_s[at, :] = md

        @pl.when(step == steps - 1)
        def _():
            for d in range(n_col):
                at = pl.ds(
                    pl.multiple_of(goes_to(col, d, n_col) * own_rows, own_rows), own_rows
                )
                if width < lanes:
                    out_refs[d][...] = jnp.zeros_like(out_refs[d])
                out_refs[d][:own_rows, :width] = num_s[at, :]
                out_refs[d][own_rows:, :own_rows] = md_s[at, :].T[:mdp]

    if n_chunk > 1:
        parts[far_first, 0], targets = lax.optimization_barrier((parts[far_first, 0], targets))
        spread(far_first, 0)
    posneg, tgt_m, den, num = stage(
        near_kernel,
        near_keys,
        targets,
        [(up8(heads), own_rows)] * n_col,
        [shape_t, shape_t, shape_d, shape_w],
    )
    parts[far_first, last], den = lax.optimization_barrier((parts[far_first, last], den))
    spread(far_first, last)
    middle_keys = [(k, ch) for ch in range(last) for k in range(far_first, n_row)]
    if middle_keys:
        den, num = stage(
            middle_kernel,
            middle_keys,
            (posneg, den, num),
            [shape_t, shape_d, shape_w],
            [shape_d, shape_w],
        )
    last_keys = [(k, last) for k in range(far_first, n_row)]
    other_keys = near_keys + middle_keys
    chunks = stage(
        last_kernel,
        last_keys,
        (posneg, den, num, tgt_m),
        [shape_t, shape_d, shape_w, shape_t],
        [(chunk_rows, lanes)] * n_col,
        extra=other_keys,
        scratch=[
            pltpu.VMEM(shape_d, F32),
            pltpu.VMEM(shape_w, F32),
            pltpu.VMEM(shape_t, F32),
        ],
    )
    gathered = [hop(chunks[d], "col", d) for d in range(n_col - 1, 0, -1)]
    gathered = [chunks[0]] + gathered[::-1]

    def out_kernel(zdst_ref, src_ref, dst_ref, bias_ref, *rest):
        parts, out_ref = rest[:n_col], rest[n_col]
        same = (
            lax.broadcasted_iota(jnp.int32, (width, width), 0) // dims
            == lax.broadcasted_iota(jnp.int32, (width, width), 1) // dims
        ).astype(F32)
        z = zdst_ref[...]
        pair = contract(z * (dst_ref[...] + src_ref[...]), same, ((1,), (0,)))
        e_self = leaky(LOG2E * pair)
        which = lax.broadcasted_iota(jnp.int32, (mdp, width), 0)
        head = lax.broadcasted_iota(jnp.int32, (mdp, width), 1) // dims
        den_of, m_of = (which == head).astype(F32), (which == head + heads).astype(F32)
        mds = [part[own_rows:, :own_rows] for part in parts]
        ms = [contract(md, m_of, ((0,), (0,))) for md in mds]
        dens = [contract(md, den_of, ((0,), (0,))) for md in mds]
        top = e_self
        for m in ms:
            top = jnp.maximum(top, m)
        den = jnp.exp2(e_self - top)
        num = den * z
        for part, m, own_den in zip(parts, ms, dens):
            factor = jnp.exp2(m - top)
            den = den + factor * own_den
            num = num + factor * part[:own_rows, :width]
        x = num / den + bias_ref[...]
        out_ref[...] = jnp.where(x > 0, x, jnp.exp(jnp.minimum(x, 0.0)) - 1.0).astype(BF16)

    return call(
        out_kernel,
        jax.ShapeDtypeStruct((own_rows, width), BF16),
        zdst,
        att_src2,
        att_dst2,
        bias2,
        *gathered,
    )


def solution(mesh):
    return jax.shard_map(
        on_device,
        mesh=mesh,
        in_specs=(
            P(("row", "col"), "feat"),
            P(("row", "col"), "feat"),
            P("feat", None),
            P("feat"),
            P("feat"),
            P("feat"),
            P("row", "col", None),
            P("row", "col", None),
            P("row", "col"),
            P("row", "col", None, None, None),
        ),
        out_specs=P(("row", "col"), "feat"),
        check_vma=False,
    )
```

```python
import jax
import jax.numpy as jnp
from jax import lax
from jax.experimental import pallas as pl
from jax.experimental.pallas import tpu as pltpu
from jax.sharding import PartitionSpec as P

HEADS = 8
TILE = 128
SLOPE = 0.2
LOG2E = 1.4426950408889634
NEG = -1e30
F32 = jnp.float32
BF16 = jnp.bfloat16
HIGHEST = lax.Precision.HIGHEST
VMEM = pl.BlockSpec(memory_space=pltpu.VMEM)
SMEM = pl.BlockSpec(memory_space=pltpu.SMEM)
HBM = pl.BlockSpec(memory_space=pltpu.HBM)


def is_pow2(n):
    return n & (n - 1) == 0


def goes_to(i, d, n):
    return i ^ d if is_pow2(n) else lax.rem(i + d, n)


def comes_from(i, d, n):
    return i ^ d if is_pow2(n) else lax.rem(i + n - d, n)


def hop(x, axis, d):
    n = lax.axis_size(axis)
    pairs = [(i, i ^ d if is_pow2(n) else (i + d) % n) for i in range(n)]
    return lax.ppermute(x, axis, pairs)


def call(kernel, out_shape, *args, in_specs=None, flops=0, bytes_accessed=0, grant=8 << 20, **kw):
    return pl.pallas_call(
        kernel,
        out_shape=out_shape,
        in_specs=in_specs or [VMEM] * len(args),
        cost_estimate=pl.CostEstimate(
            flops=flops, bytes_accessed=bytes_accessed, transcendentals=0
        ),
        compiler_params=pltpu.CompilerParams(vmem_limit_bytes=grant),
        **kw,
    )(*args)


def limit(mib, least):
    return min(max(mib << 20, least), 60 << 20)


def in_hbm(x):
    return pltpu.with_memory_space_constraint(x, pltpu.HBM)


def up8(n):
    return -(-n // 8) * 8


def head_rows(vector, heads, width, height):
    dims = width // heads
    shape = (height, width)
    row = lax.broadcasted_iota(jnp.int32, shape, 0) % heads
    lane = lax.broadcasted_iota(jnp.int32, shape, 1)
    return jnp.where(lane // dims == row, jnp.broadcast_to(vector, shape), 0.0)


def contract(lhs, rhs, dims, precision=HIGHEST):
    return lax.dot_general(
        lhs, rhs, (dims, ((), ())), preferred_element_type=F32, precision=precision
    )


def take_cols(proj_ref, which, width):
    if width % TILE == 0:
        return proj_ref[:, pl.ds(pl.multiple_of(which * width, width), width)]
    full = proj_ref[...]
    out = full[:, :width]
    for k in range(1, full.shape[1] // width):
        out = jnp.where(which == k, full[:, k * width : (k + 1) * width], out)
    return out


def project(x, w):
    return lax.dot_general(x, w, (((1,), (0,)), ((), ())), preferred_element_type=F32)


def leaky(x):
    return jnp.maximum(x, SLOPE * x)


def on_device(
    src_feats, dst_feats, proj, att_src, att_dst, bias, tile_rows, tile_cols, tile_count, edge_weight
):
    n_row, n_col, n_feat = (lax.axis_size(a) for a in ("row", "col", "feat"))
    width = proj.shape[1] // n_feat
    heads = HEADS // n_feat
    dims = width // heads
    lanes = -(-width // TILE) * TILE
    src_rows, own_rows = src_feats.shape[0], dst_feats.shape[0]
    slots = tile_rows.shape[2]
    row_tiles = own_rows * n_col // TILE
    piece_tiles = src_rows // TILE
    n_chunk = 2 if piece_tiles % 2 == 0 else 1
    chunk_tiles = piece_tiles // n_chunk
    part_rows = src_rows // n_chunk
    col_tiles = piece_tiles * n_row
    hp = up8(2 * heads)
    mdp = up8(2 * heads)
    att_src2, att_dst2, bias2 = (v.reshape(1, width) for v in (att_src, att_dst, bias))

    def fetch(hbm, vmem, sems):
        copies = [pltpu.make_async_copy(h, v, sems.at[k]) for k, (h, v) in enumerate(zip(hbm, vmem))]
        for copy in copies:
            copy.start()
        for copy in copies:
            copy.wait()

    def fetching(kernel, outs, *args):
        return call(
            kernel,
            outs,
            *map(in_hbm, args),
            in_specs=[HBM] * len(args),
            scratch_shapes=[
                *(pltpu.VMEM(v.shape, v.dtype) for v in args),
                pltpu.SemaphoreType.DMA((len(args),)),
            ],
        )

    def send_kernel(*refs):
        hbm, outs, (src_ref, dst_ref, proj_ref, sems) = refs[:3], refs[3:-4], refs[-4:]
        fetch(hbm, (src_ref, dst_ref, proj_ref), sems)
        me = lax.axis_index("feat")
        for d in range(1, n_feat):
            w = take_cols(proj_ref, goes_to(me, d, n_feat), width)
            own_outs = outs[(d - 1) * (n_chunk + 1) : d * (n_chunk + 1)]
            own_outs[0][...] = project(dst_ref[...], w)
            for ch in range(n_chunk):
                own_outs[ch + 1][...] = project(src_ref[ch * part_rows : (ch + 1) * part_rows], w)

    sent = fetching(
        send_kernel,
        [
            pltpu.VMEM((n, width), F32)
            for _ in range(1, n_feat)
            for n in [own_rows] + [part_rows] * n_chunk
        ],
        src_feats,
        dst_feats,
        proj,
    )
    sent = [sent[k :: n_chunk + 1] for k in range(n_chunk + 1)]
    dst_parts = [hop(sent[0][d - 1], "feat", d) for d in range(1, n_feat)]
    src_parts = [[hop(part[d - 1], "feat", d) for d in range(1, n_feat)] for part in sent[1:]]

    def own_kernel(*refs):
        hbm, outs, refs = refs[:5], refs[5 : 8 + n_chunk], refs[8 + n_chunk :]
        fetch(hbm, refs[:5], refs[5])
        src_ref, dst_ref, proj_ref, att_src_ref, att_dst_ref = refs[:5]
        w = take_cols(proj_ref, lax.axis_index("feat"), width)
        outs[0][...] = project(dst_ref[...], w)
        outs[1][...] = LOG2E * head_rows(att_dst_ref[...], heads, width, up8(heads))
        outs[2][...] = LOG2E * head_rows(att_src_ref[...], heads, width, hp)
        for ch in range(n_chunk):
            outs[3 + ch][...] = project(src_ref[ch * part_rows : (ch + 1) * part_rows], w)

    dst_own, dst_att, src_att, *src_own = fetching(
        own_kernel,
        [
            pltpu.VMEM((own_rows, width), F32),
            pltpu.VMEM((up8(heads), width), F32),
            pltpu.VMEM((hp, width), F32),
        ]
        + [pltpu.VMEM((part_rows, width), F32)] * n_chunk,
        src_feats,
        dst_feats,
        proj,
        att_src2,
        att_dst2,
    )
    dst_parts, src_own = lax.optimization_barrier((dst_parts, src_own))

    tiles = row_tiles * col_tiles
    whole = lambda shape: pl.BlockSpec(shape, lambda s: (0,) * len(shape))

    def dst_kernel(own_ref, att_ref, *rest):
        got, (z_ref, s_ref) = rest[: n_feat - 1], rest[n_feat - 1 :]
        z = own_ref[...]
        for part in got:
            z = z + part[...]
        z_ref[...] = z
        s_ref[...] = contract(att_ref[...], z, ((1,), (1,)))

    zdst, s_dst = call(
        dst_kernel,
        [
            jax.ShapeDtypeStruct((own_rows, width), F32),
            jax.ShapeDtypeStruct((up8(heads), own_rows), F32),
        ],
        dst_own,
        dst_att,
        *dst_parts,
    )
    rows_of = up8(heads)
    if is_pow2(n_col) and n_col > 1:
        targets, d = [s_dst], 1
        while d < n_col:
            targets = [targets[0], hop(targets[0], "col", d)]
            d *= 2
            if d < n_col:

                def join_kernel(low_ref, high_ref, out_ref):
                    out_ref[...] = jnp.concatenate([low_ref[...], high_ref[...]], axis=0)

                shape = (d * rows_of, own_rows)
                targets = [call(join_kernel, pltpu.VMEM(shape, F32), *targets)]
    else:
        targets = [s_dst] + [hop(s_dst, "col", d) for d in range(1, n_col)]
    size = n_col // len(targets)

    pack_rows = part_rows + chunk_tiles * hp

    def z_kernel(own_ref, att_ref, *rest):
        got, out_ref = rest[: n_feat - 1], rest[n_feat - 1]
        z = own_ref[...]
        for part in got:
            z = z + part[...]
        if width < lanes:
            out_ref[...] = jnp.zeros_like(out_ref)
        out_ref[:part_rows, :width] = z
        s = contract(att_ref[...], z, ((1,), (1,)))
        low = lax.broadcasted_iota(jnp.int32, s.shape, 0) < heads
        s = jnp.where(low, s, SLOPE * s)
        for t in range(chunk_tiles):
            at = part_rows + t * hp
            out_ref[at : at + hp, :TILE] = s[:, t * TILE : (t + 1) * TILE]

    parts, far_first = {}, n_row // 2
    for ch in range(n_chunk):
        own = call(z_kernel, pltpu.VMEM((pack_rows, lanes), F32), src_own[ch], src_att, *src_parts[ch])
        parts[far_first, ch] = hop(own, "row", far_first)
        parts[0, ch] = own
    last = n_chunk - 1

    def spread(first, ch):
        d = n_row // 4
        while d:
            for k in [k for k, c in parts if c == ch and k ^ first < far_first]:
                parts[k ^ d, ch] = hop(parts[k, ch], "row", d)
            d //= 2

    for ch in range(n_chunk):
        spread(0, ch)

    units = n_row * n_chunk
    period = min(slots, tiles) if slots % min(slots, tiles) == 0 else slots
    reps = slots // period
    group = 8
    groups = period // group

    def weight_kernel(rows_hbm, cols_hbm, count_ref, w_hbm, panel_ref, *scratch):
        rows_ref, cols_ref, w_ref, index_sems, w_sems = scratch
        row = lax.axis_index("row")
        indices = [
            pltpu.make_async_copy(rows_hbm, rows_ref, index_sems.at[0]),
            pltpu.make_async_copy(cols_hbm, cols_ref, index_sems.at[1]),
        ]
        blocks = [
            pltpu.make_async_copy(
                w_hbm.at[k, pl.ds(g * group, group)],
                w_ref.at[k, pl.ds(g * group, group)],
                w_sems.at[g, k],
            )
            for g in range(groups)
            for k in range(reps)
        ]
        for copy in indices + blocks:
            copy.start()

        @pl.loop(0, units)
        def _(u):
            @pl.loop(0, row_tiles)
            def _(r):
                panel_ref[u, r] = jnp.zeros((chunk_tiles, TILE, TILE), F32)

        for copy in indices:
            copy.wait()
        count = count_ref[0, 0]
        for g in range(groups):
            for copy in blocks[g * reps : (g + 1) * reps]:
                copy.wait()
            base = g * group

            @pl.loop(base, jnp.clip(count, base, base + group))
            def _(u):
                r, c = rows_ref[0, 0, u], cols_ref[0, 0, u]
                unit = ((c // piece_tiles) ^ row) * n_chunk + c % piece_tiles // chunk_tiles
                t = c % chunk_tiles
                total = w_ref[0, u].astype(F32)
                for k in range(1, reps):
                    live = (u + k * period < count).astype(F32)
                    total = total + w_ref[k, u].astype(F32) * live
                panel_ref[unit, r, t] = panel_ref[unit, r, t] + total

    panel = call(
        weight_kernel,
        pltpu.VMEM((units, row_tiles, chunk_tiles, TILE, TILE), F32),
        in_hbm(tile_rows),
        in_hbm(tile_cols),
        tile_count,
        in_hbm(edge_weight.reshape(reps, period, TILE, TILE)),
        in_specs=[HBM, HBM, SMEM, HBM],
        scratch_shapes=[
            pltpu.SMEM(tile_rows.shape, jnp.int32),
            pltpu.SMEM(tile_cols.shape, jnp.int32),
            pltpu.VMEM((reps, period, TILE, TILE), edge_weight.dtype),
            pltpu.SemaphoreType.DMA((2,)),
            pltpu.SemaphoreType.DMA((groups, reps)),
        ],
        flops=slots * TILE * TILE,
        bytes_accessed=slots * TILE * TILE * 2,
        grant=12 << 20,
    )

    block = 64
    blocks = TILE // block
    unroll = 2 if row_tiles % 2 == 0 else 1
    steps = row_tiles // unroll
    chunk_rows = own_rows + mdp
    group_rows = unroll * TILE
    all_rows = row_tiles * TILE
    tiny, huge = 2.0**-60, 2.0**60
    lane_w = lambda: lax.broadcasted_iota(jnp.int32, (block, width), 1) // dims
    lane_t = lambda: lax.broadcasted_iota(jnp.int32, (block, TILE), 1)

    def score_rows(part_ref, t, h):
        at = part_rows + t * hp + h
        return part_ref[at : at + 1, :TILE], part_ref[at + heads : at + heads + 1, :TILE]

    def split(x):
        hi = x.astype(BF16)
        return hi, (x - hi.astype(F32)).astype(BF16)

    def split_z(part_refs):
        return jnp.concatenate(
            [jnp.concatenate(split(p[:part_rows, :width]), axis=1) for p in part_refs], axis=0
        )

    def stack(pairs):
        return jnp.concatenate(
            [jnp.concatenate([p[k] for p in row], axis=1) for row in pairs for k in range(2)], axis=0
        )

    def weighted(probs, z):
        both = lax.dot_general(probs, z, (((1,), (0,)), ((), ())), preferred_element_type=F32)
        num = jnp.zeros((block, width), F32)
        for h in range(heads):
            hi = both[2 * h * block : (2 * h + 1) * block]
            lo = both[(2 * h + 1) * block : (2 * h + 2) * block]
            num = jnp.where(lane_w() == h, hi[:, :width] + (hi[:, width:] + lo[:, :width]), num)
        return num

    def attend(part_refs, w_refs, posneg, den_in, num_in, den_out, num_out):
        base = pl.program_id(0) * group_rows
        z_cat = split_z(part_refs)
        for b in range(unroll * blocks):
            at = pl.ds(pl.multiple_of(base + b * block, block), block)
            rt, i0 = divmod(b * block, TILE)
            pairs = []
            for h in range(heads):
                pairs.append([])
                pn = posneg[at, :]
                pos = jnp.broadcast_to(pn[:, h : h + 1], (block, TILE))
                neg = jnp.broadcast_to(pn[:, heads + h : heads + h + 1], (block, TILE))
                den = jnp.zeros((block, TILE), F32) if den_in is None else den_in[h, at, :]
                for k, part_ref in enumerate(part_refs):
                    for t in range(chunk_tiles):
                        s, s_low = score_rows(part_ref, t, h)
                        x = jnp.maximum(pos + s, neg + s_low)
                        p = w_refs[k][0, rt, t, i0 : i0 + block, :] * jnp.exp2(x)
                        den = den + p
                        pairs[h].append(split(p))
                den_out[h, at, :] = den
            num = weighted(stack(pairs), z_cat)
            num_out[at, :] = num if num_in is None else num_in[at, :] + num

    shape_t, shape_w, shape_d = (all_rows, TILE), (all_rows, width), (heads, all_rows, TILE)
    part_spec = whole((pack_rows, lanes))

    def unit_spec(k, ch):
        return pl.BlockSpec(
            (1, unroll, chunk_tiles, TILE, TILE), lambda s: (k * n_chunk + ch, s, 0, 0, 0)
        )

    def stage(kernel, keys, before, before_shapes, outs, extra=(), scratch=()):
        n = len(keys)
        return pl.pallas_call(
            kernel,
            out_shape=[pltpu.VMEM(s, F32) for s in outs],
            grid=(steps,),
            in_specs=[whole(s) for s in before_shapes]
            + [part_spec] * (n + len(extra))
            + [unit_spec(*key) for key in (*keys, *extra)],
            out_specs=[whole(s) for s in outs],
            scratch_shapes=scratch,
            cost_estimate=pl.CostEstimate(
                flops=all_rows * n * part_rows * width * heads * 8,
                bytes_accessed=n * part_rows * width * 4,
                transcendentals=all_rows * n * part_rows * heads,
            ),
            compiler_params=pltpu.CompilerParams(vmem_limit_bytes=limit(16, 4 * tiles * TILE * TILE)),
        )(*before, *(parts[key] for key in (*keys, *extra)), *[panel] * (n + len(extra)))

    near_keys = [(k, ch) for ch in range(n_chunk) for k in range(far_first)]

    def near_kernel(*refs):
        n = len(near_keys)
        n_tgt = len(targets)
        tgt_refs, part_refs, w_refs = refs[:n_tgt], refs[n_tgt : n_tgt + n], refs[n_tgt + n :][:n]
        posneg, tgt_m, den_out, num_out = refs[n_tgt + 2 * n :]
        col = lax.axis_index("col")

        @pl.when(pl.program_id(0) == 0)
        def _():
            shape = (up8(heads), TILE)
            eye = (
                lax.broadcasted_iota(jnp.int32, shape, 0)
                == lax.broadcasted_iota(jnp.int32, shape, 1) % heads
            ).astype(F32)
            lane = lax.broadcasted_iota(jnp.int32, (1, TILE), 1)
            bound = jnp.zeros((1, TILE), F32)
            for h in range(heads):
                rows = [score_rows(r, t, h)[0] for r in part_refs for t in range(chunk_tiles)]
                top = rows[0]
                for other in rows[1:]:
                    top = jnp.maximum(top, other)
                top = jnp.max(top, axis=1, keepdims=True)
                bound = jnp.where(lane % heads == h, top, bound)
            for d in range(n_col):
                at = pl.ds(
                    pl.multiple_of(comes_from(col, d, n_col) * own_rows, own_rows), own_rows
                )
                k, g = divmod(d, size)
                a = contract(tgt_refs[k][g * rows_of : (g + 1) * rows_of], eye, ((0,), (0,)))
                m = leaky(a + bound)
                tgt_m[at, :] = jnp.where(lane < heads, a, m)
                posneg[at, :] = jnp.where(lane < heads, a, SLOPE * a) - m

        attend(part_refs, w_refs, posneg, None, None, den_out, num_out)

    def middle_kernel(*refs):
        n = len(middle_keys)
        (posneg, den_in, num_in), refs = refs[:3], refs[3:]
        part_refs, w_refs, (den_out, num_out) = refs[:n], refs[n : 2 * n], refs[2 * n :]
        attend(part_refs, w_refs, posneg, den_in, num_in, den_out, num_out)

    def last_kernel(*refs):
        n, n_all = len(last_keys), len(last_keys) + len(other_keys)
        (posneg, den_in, num_in, tgt_m), refs = refs[:4], refs[4:]
        part_refs, w_refs, refs = refs[:n_all], refs[n_all : 2 * n_all], refs[2 * n_all :]
        out_refs, (den_s, num_s, md_s) = refs[:n_col], refs[n_col:]
        col = lax.axis_index("col")
        step = pl.program_id(0)

        attend(part_refs[:n], w_refs[:n], posneg, den_in, num_in, den_s, num_s)
        base = step * group_rows
        low = high = None
        for b in range(unroll * blocks):
            at = pl.ds(pl.multiple_of(base + b * block, block), block)
            md = tgt_m[at, :]
            for h in range(heads):
                den = jnp.sum(den_s[h, at, :], axis=1, keepdims=True)
                low = den if low is None else jnp.minimum(low, den)
                high = den if high is None else jnp.maximum(high, den)
                md = jnp.where(lane_t() == h, den, md)
            md_s[at, :] = md
        fine = jnp.logical_and(jnp.min(low) >= tiny, jnp.max(high) <= huge)

        @pl.when(jnp.logical_not(fine))
        def _():
            @pl.loop(0, unroll * blocks)
            def _(b):
                at = pl.ds(pl.multiple_of(base + b * block, block), block)
                rt = b // blocks
                rows = pl.ds(pl.multiple_of((b % blocks) * block, block), block)
                md = tgt_m[at, :]
                posnegs, dens = [], []
                for h in range(heads):
                    best = jnp.full((block, TILE), NEG, F32)
                    for part_ref, w_ref in zip(part_refs, w_refs):
                        for t in range(chunk_tiles):
                            edge = w_ref[0, rt, t, rows, :] > 0
                            s = score_rows(part_ref, t, h)[0]
                            best = jnp.maximum(best, jnp.where(edge, s, NEG))
                    a = tgt_m[at, :][:, h : h + 1]
                    m = leaky(a + jnp.max(best, axis=1, keepdims=True))
                    md = jnp.where(lane_t() == heads + h, m, md)
                    posnegs.append((a - m, SLOPE * a - m))
                    dens.append(jnp.zeros((block, TILE), F32))
                num_s[at, :] = jnp.zeros((block, width), F32)
                for part_ref, w_ref in zip(part_refs, w_refs):
                    pairs = []
                    for h in range(heads):
                        pairs.append([])
                        pos, neg = posnegs[h]
                        for t in range(chunk_tiles):
                            s, s_low = score_rows(part_ref, t, h)
                            x = jnp.minimum(jnp.maximum(pos + s, neg + s_low), 0.0)
                            p = w_ref[0, rt, t, rows, :] * jnp.exp2(x)
                            dens[h] = dens[h] + p
                            pairs[h].append(split(p))
                    num_s[at, :] = num_s[at, :] + weighted(stack(pairs), split_z([part_ref]))
                for h in range(heads):
                    md = jnp.where(lane_t() == h, jnp.sum(dens[h], axis=1, keepdims=True), md)
                md_s[at, :] = md

        @pl.when(step == steps - 1)
        def _():
            for d in range(n_col):
                at = pl.ds(
                    pl.multiple_of(goes_to(col, d, n_col) * own_rows, own_rows), own_rows
                )
                if width < lanes:
                    out_refs[d][...] = jnp.zeros_like(out_refs[d])
                out_refs[d][:own_rows, :width] = num_s[at, :]
                out_refs[d][own_rows:, :own_rows] = md_s[at, :].T[:mdp]

    if n_chunk > 1:
        parts[far_first, 0], targets = lax.optimization_barrier((parts[far_first, 0], targets))
        spread(far_first, 0)
    posneg, tgt_m, den, num = stage(
        near_kernel,
        near_keys,
        targets,
        [(size * rows_of, own_rows)] * len(targets),
        [shape_t, shape_t, shape_d, shape_w],
    )
    parts[far_first, last], den = lax.optimization_barrier((parts[far_first, last], den))
    spread(far_first, last)
    middle_keys = [(k, ch) for ch in range(last) for k in range(far_first, n_row)]
    if middle_keys:
        den, num = stage(
            middle_kernel,
            middle_keys,
            (posneg, den, num),
            [shape_t, shape_d, shape_w],
            [shape_d, shape_w],
        )
    last_keys = [(k, last) for k in range(far_first, n_row)]
    other_keys = near_keys + middle_keys
    chunks = stage(
        last_kernel,
        last_keys,
        (posneg, den, num, tgt_m),
        [shape_t, shape_d, shape_w, shape_t],
        [(chunk_rows, lanes)] * n_col,
        extra=other_keys,
        scratch=[
            pltpu.VMEM(shape_d, F32),
            pltpu.VMEM(shape_w, F32),
            pltpu.VMEM(shape_t, F32),
        ],
    )
    gathered = [hop(chunks[d], "col", d) for d in range(n_col - 1, 0, -1)]
    gathered = [chunks[0]] + gathered[::-1]

    def out_kernel(zdst_ref, src_ref, dst_ref, bias_ref, *rest):
        parts, out_ref = rest[:n_col], rest[n_col]
        same = (
            lax.broadcasted_iota(jnp.int32, (width, width), 0) // dims
            == lax.broadcasted_iota(jnp.int32, (width, width), 1) // dims
        ).astype(F32)
        z = zdst_ref[...]
        pair = contract(z * (dst_ref[...] + src_ref[...]), same, ((1,), (0,)))
        e_self = leaky(LOG2E * pair)
        which = lax.broadcasted_iota(jnp.int32, (mdp, width), 0)
        head = lax.broadcasted_iota(jnp.int32, (mdp, width), 1) // dims
        den_of, m_of = (which == head).astype(F32), (which == head + heads).astype(F32)
        mds = [part[own_rows:, :own_rows] for part in parts]
        ms = [contract(md, m_of, ((0,), (0,))) for md in mds]
        dens = [contract(md, den_of, ((0,), (0,))) for md in mds]
        top = e_self
        for m in ms:
            top = jnp.maximum(top, m)
        den = jnp.exp2(e_self - top)
        num = den * z
        for part, m, own_den in zip(parts, ms, dens):
            factor = jnp.exp2(m - top)
            den = den + factor * own_den
            num = num + factor * part[:own_rows, :width]
        x = num / den + bias_ref[...]
        out_ref[...] = jnp.where(x > 0, x, jnp.exp(jnp.minimum(x, 0.0)) - 1.0).astype(BF16)

    return call(
        out_kernel,
        jax.ShapeDtypeStruct((own_rows, width), BF16),
        zdst,
        att_src2,
        att_dst2,
        bias2,
        *gathered,
    )


def solution(mesh):
    return jax.shard_map(
        on_device,
        mesh=mesh,
        in_specs=(
            P(("row", "col"), "feat"),
            P(("row", "col"), "feat"),
            P("feat", None),
            P("feat"),
            P("feat"),
            P("feat"),
            P("row", "col", None),
            P("row", "col", None),
            P("row", "col"),
            P("row", "col", None, None, None),
        ),
        out_specs=P(("row", "col"), "feat"),
        check_vma=False,
    )
```

```python
import jax
import jax.numpy as jnp
from jax import lax
from jax.experimental import pallas as pl
from jax.experimental.pallas import tpu as pltpu
from jax.sharding import PartitionSpec as P

HEADS = 8
TILE = 128
SLOPE = 0.2
LOG2E = 1.4426950408889634
NEG = -1e30
F32 = jnp.float32
BF16 = jnp.bfloat16
HIGHEST = lax.Precision.HIGHEST
VMEM = pl.BlockSpec(memory_space=pltpu.VMEM)
SMEM = pl.BlockSpec(memory_space=pltpu.SMEM)
HBM = pl.BlockSpec(memory_space=pltpu.HBM)


def is_pow2(n):
    return n & (n - 1) == 0


def goes_to(i, d, n):
    return i ^ d if is_pow2(n) else lax.rem(i + d, n)


def comes_from(i, d, n):
    return i ^ d if is_pow2(n) else lax.rem(i + n - d, n)


def hop(x, axis, d):
    n = lax.axis_size(axis)
    pairs = [(i, i ^ d if is_pow2(n) else (i + d) % n) for i in range(n)]
    return lax.ppermute(x, axis, pairs)


def call(kernel, out_shape, *args, in_specs=None, flops=0, bytes_accessed=0, grant=8 << 20, **kw):
    return pl.pallas_call(
        kernel,
        out_shape=out_shape,
        in_specs=in_specs or [VMEM] * len(args),
        cost_estimate=pl.CostEstimate(
            flops=flops, bytes_accessed=bytes_accessed, transcendentals=0
        ),
        compiler_params=pltpu.CompilerParams(vmem_limit_bytes=grant),
        **kw,
    )(*args)


def limit(mib, least):
    return min(max(mib << 20, least), 60 << 20)


def in_hbm(x):
    return pltpu.with_memory_space_constraint(x, pltpu.HBM)


def up8(n):
    return -(-n // 8) * 8


def head_rows(vector, heads, width, height):
    dims = width // heads
    shape = (height, width)
    row = lax.broadcasted_iota(jnp.int32, shape, 0) % heads
    lane = lax.broadcasted_iota(jnp.int32, shape, 1)
    return jnp.where(lane // dims == row, jnp.broadcast_to(vector, shape), 0.0)


def contract(lhs, rhs, dims, precision=HIGHEST):
    return lax.dot_general(
        lhs, rhs, (dims, ((), ())), preferred_element_type=F32, precision=precision
    )


def take_cols(proj_ref, which, width):
    if width % TILE == 0:
        return proj_ref[:, pl.ds(pl.multiple_of(which * width, width), width)]
    full = proj_ref[...]
    out = full[:, :width]
    for k in range(1, full.shape[1] // width):
        out = jnp.where(which == k, full[:, k * width : (k + 1) * width], out)
    return out


def project(x, w):
    return lax.dot_general(x, w, (((1,), (0,)), ((), ())), preferred_element_type=F32)


def leaky(x):
    return jnp.maximum(x, SLOPE * x)


def on_device(
    src_feats, dst_feats, proj, att_src, att_dst, bias, tile_rows, tile_cols, tile_count, edge_weight
):
    n_row, n_col, n_feat = (lax.axis_size(a) for a in ("row", "col", "feat"))
    width = proj.shape[1] // n_feat
    heads = HEADS // n_feat
    dims = width // heads
    lanes = -(-width // TILE) * TILE
    src_rows, own_rows = src_feats.shape[0], dst_feats.shape[0]
    slots = tile_rows.shape[2]
    row_tiles = own_rows * n_col // TILE
    piece_tiles = src_rows // TILE
    n_chunk = 2 if piece_tiles % 2 == 0 else 1
    chunk_tiles = piece_tiles // n_chunk
    part_rows = src_rows // n_chunk
    col_tiles = piece_tiles * n_row
    hp = up8(2 * heads)
    mdp = up8(2 * heads)
    att_src2, att_dst2, bias2 = (v.reshape(1, width) for v in (att_src, att_dst, bias))

    def fetch(hbm, vmem, sems):
        copies = [pltpu.make_async_copy(h, v, sems.at[k]) for k, (h, v) in enumerate(zip(hbm, vmem))]
        for copy in copies:
            copy.start()
        for copy in copies:
            copy.wait()

    def fetching(kernel, outs, *args):
        return call(
            kernel,
            outs,
            *map(in_hbm, args),
            in_specs=[HBM] * len(args),
            scratch_shapes=[
                *(pltpu.VMEM(v.shape, v.dtype) for v in args),
                pltpu.SemaphoreType.DMA((len(args),)),
            ],
        )

    def send_kernel(*refs):
        hbm, outs, (src_ref, dst_ref, proj_ref, sems) = refs[:3], refs[3:-4], refs[-4:]
        fetch(hbm, (src_ref, dst_ref, proj_ref), sems)
        me = lax.axis_index("feat")
        for d in range(1, n_feat):
            w = take_cols(proj_ref, goes_to(me, d, n_feat), width)
            own_outs = outs[(d - 1) * (n_chunk + 1) : d * (n_chunk + 1)]
            own_outs[0][...] = project(dst_ref[...], w)
            for ch in range(n_chunk):
                own_outs[ch + 1][...] = project(src_ref[ch * part_rows : (ch + 1) * part_rows], w)

    sent = fetching(
        send_kernel,
        [
            pltpu.VMEM((n, width), F32)
            for _ in range(1, n_feat)
            for n in [own_rows] + [part_rows] * n_chunk
        ],
        src_feats,
        dst_feats,
        proj,
    )
    sent = [sent[k :: n_chunk + 1] for k in range(n_chunk + 1)]
    dst_parts = [hop(sent[0][d - 1], "feat", d) for d in range(1, n_feat)]
    src_parts = [[hop(part[d - 1], "feat", d) for d in range(1, n_feat)] for part in sent[1:]]

    def own_kernel(*refs):
        hbm, outs, refs = refs[:5], refs[5 : 8 + n_chunk], refs[8 + n_chunk :]
        fetch(hbm, refs[:5], refs[5])
        src_ref, dst_ref, proj_ref, att_src_ref, att_dst_ref = refs[:5]
        w = take_cols(proj_ref, lax.axis_index("feat"), width)
        outs[0][...] = project(dst_ref[...], w)
        outs[1][...] = LOG2E * head_rows(att_dst_ref[...], heads, width, up8(heads))
        outs[2][...] = LOG2E * head_rows(att_src_ref[...], heads, width, hp)
        for ch in range(n_chunk):
            outs[3 + ch][...] = project(src_ref[ch * part_rows : (ch + 1) * part_rows], w)

    dst_own, dst_att, src_att, *src_own = fetching(
        own_kernel,
        [
            pltpu.VMEM((own_rows, width), F32),
            pltpu.VMEM((up8(heads), width), F32),
            pltpu.VMEM((hp, width), F32),
        ]
        + [pltpu.VMEM((part_rows, width), F32)] * n_chunk,
        src_feats,
        dst_feats,
        proj,
        att_src2,
        att_dst2,
    )
    dst_parts, src_own = lax.optimization_barrier((dst_parts, src_own))

    tiles = row_tiles * col_tiles
    whole = lambda shape: pl.BlockSpec(shape, lambda s: (0,) * len(shape))

    def dst_kernel(own_ref, att_ref, *rest):
        got, (z_ref, s_ref) = rest[: n_feat - 1], rest[n_feat - 1 :]
        z = own_ref[...]
        for part in got:
            z = z + part[...]
        z_ref[...] = z
        s_ref[...] = contract(att_ref[...], z, ((1,), (1,)))

    zdst, s_dst = call(
        dst_kernel,
        [
            jax.ShapeDtypeStruct((own_rows, width), F32),
            jax.ShapeDtypeStruct((up8(heads), own_rows), F32),
        ],
        dst_own,
        dst_att,
        *dst_parts,
    )
    rows_of = up8(heads)
    if is_pow2(n_col) and n_col > 1:
        targets, d = [s_dst], 1
        while d < n_col:
            targets = [targets[0], hop(targets[0], "col", d)]
            d *= 2
            if d < n_col:

                def join_kernel(low_ref, high_ref, out_ref):
                    out_ref[...] = jnp.concatenate([low_ref[...], high_ref[...]], axis=0)

                shape = (d * rows_of, own_rows)
                targets = [call(join_kernel, pltpu.VMEM(shape, F32), *targets)]
    else:
        targets = [s_dst] + [hop(s_dst, "col", d) for d in range(1, n_col)]
    size = n_col // len(targets)

    pack_rows = part_rows + chunk_tiles * hp

    def z_kernel(own_ref, att_ref, *rest):
        got, out_ref = rest[: n_feat - 1], rest[n_feat - 1]
        z = own_ref[...]
        for part in got:
            z = z + part[...]
        if width < lanes:
            out_ref[...] = jnp.zeros_like(out_ref)
        out_ref[:part_rows, :width] = z
        s = contract(att_ref[...], z, ((1,), (1,)))
        low = lax.broadcasted_iota(jnp.int32, s.shape, 0) < heads
        s = jnp.where(low, s, SLOPE * s)
        for t in range(chunk_tiles):
            at = part_rows + t * hp
            out_ref[at : at + hp, :TILE] = s[:, t * TILE : (t + 1) * TILE]

    parts, far_first = {}, n_row // 2
    for ch in range(n_chunk):
        own = call(z_kernel, pltpu.VMEM((pack_rows, lanes), F32), src_own[ch], src_att, *src_parts[ch])
        parts[far_first, ch] = hop(own, "row", far_first)
        parts[0, ch] = own

    def spread(first, ch):
        d = n_row // 4
        while d:
            for k in [k for k, c in parts if c == ch and k ^ first < far_first]:
                parts[k ^ d, ch] = hop(parts[k, ch], "row", d)
            d //= 2

    for ch in range(n_chunk):
        spread(0, ch)

    units = n_row * n_chunk
    period = min(slots, tiles) if slots % min(slots, tiles) == 0 else slots
    reps = slots // period
    group = 8
    groups = period // group

    def weight_kernel(rows_hbm, cols_hbm, count_ref, w_hbm, panel_ref, *scratch):
        rows_ref, cols_ref, w_ref, index_sems, w_sems = scratch
        row = lax.axis_index("row")
        indices = [
            pltpu.make_async_copy(rows_hbm, rows_ref, index_sems.at[0]),
            pltpu.make_async_copy(cols_hbm, cols_ref, index_sems.at[1]),
        ]
        blocks = [
            pltpu.make_async_copy(
                w_hbm.at[k, pl.ds(g * group, group)],
                w_ref.at[k, pl.ds(g * group, group)],
                w_sems.at[g, k],
            )
            for g in range(groups)
            for k in range(reps)
        ]
        for copy in indices + blocks:
            copy.start()

        @pl.loop(0, units)
        def _(u):
            @pl.loop(0, row_tiles)
            def _(r):
                panel_ref[u, r] = jnp.zeros((chunk_tiles, TILE, TILE), F32)

        for copy in indices:
            copy.wait()
        count = count_ref[0, 0]
        for g in range(groups):
            for copy in blocks[g * reps : (g + 1) * reps]:
                copy.wait()
            base = g * group

            @pl.loop(base, jnp.clip(count, base, base + group))
            def _(u):
                r, c = rows_ref[0, 0, u], cols_ref[0, 0, u]
                unit = ((c // piece_tiles) ^ row) * n_chunk + c % piece_tiles // chunk_tiles
                t = c % chunk_tiles
                total = w_ref[0, u].astype(F32)
                for k in range(1, reps):
                    live = (u + k * period < count).astype(F32)
                    total = total + w_ref[k, u].astype(F32) * live
                panel_ref[unit, r, t] = panel_ref[unit, r, t] + total

    panel = call(
        weight_kernel,
        pltpu.VMEM((units, row_tiles, chunk_tiles, TILE, TILE), F32),
        in_hbm(tile_rows),
        in_hbm(tile_cols),
        tile_count,
        in_hbm(edge_weight.reshape(reps, period, TILE, TILE)),
        in_specs=[HBM, HBM, SMEM, HBM],
        scratch_shapes=[
            pltpu.SMEM(tile_rows.shape, jnp.int32),
            pltpu.SMEM(tile_cols.shape, jnp.int32),
            pltpu.VMEM((reps, period, TILE, TILE), edge_weight.dtype),
            pltpu.SemaphoreType.DMA((2,)),
            pltpu.SemaphoreType.DMA((groups, reps)),
        ],
        flops=slots * TILE * TILE,
        bytes_accessed=slots * TILE * TILE * 2,
        grant=12 << 20,
    )

    block = 64
    blocks = TILE // block
    unroll = 2 if row_tiles % 2 == 0 else 1
    steps = row_tiles // unroll
    chunk_rows = own_rows + mdp
    group_rows = unroll * TILE
    all_rows = row_tiles * TILE
    tiny, huge = 2.0**-60, 2.0**60
    lane_w = lambda: lax.broadcasted_iota(jnp.int32, (block, width), 1) // dims
    lane_t = lambda: lax.broadcasted_iota(jnp.int32, (block, TILE), 1)

    def score_rows(part_ref, t, h):
        at = part_rows + t * hp + h
        return part_ref[at : at + 1, :TILE], part_ref[at + heads : at + heads + 1, :TILE]

    def split(x):
        hi = x.astype(BF16)
        return hi, (x - hi.astype(F32)).astype(BF16)

    def split_z(part_refs):
        return jnp.concatenate(
            [jnp.concatenate(split(p[:part_rows, :width]), axis=1) for p in part_refs], axis=0
        )

    def stack(pairs):
        return jnp.concatenate(
            [jnp.concatenate([p[k] for p in row], axis=1) for row in pairs for k in range(2)], axis=0
        )

    def weighted(probs, z):
        both = lax.dot_general(probs, z, (((1,), (0,)), ((), ())), preferred_element_type=F32)
        num = jnp.zeros((block, width), F32)
        for h in range(heads):
            hi = both[2 * h * block : (2 * h + 1) * block]
            lo = both[(2 * h + 1) * block : (2 * h + 2) * block]
            num = jnp.where(lane_w() == h, hi[:, :width] + (hi[:, width:] + lo[:, :width]), num)
        return num

    def attend(part_refs, w_refs, posneg, den_in, num_in, den_out, num_out):
        base = pl.program_id(0) * group_rows
        z_cat = split_z(part_refs)
        for b in range(unroll * blocks):
            at = pl.ds(pl.multiple_of(base + b * block, block), block)
            rt, i0 = divmod(b * block, TILE)
            pairs = []
            for h in range(heads):
                pairs.append([])
                pn = posneg[at, :]
                pos = jnp.broadcast_to(pn[:, h : h + 1], (block, TILE))
                neg = jnp.broadcast_to(pn[:, heads + h : heads + h + 1], (block, TILE))
                den = jnp.zeros((block, TILE), F32) if den_in is None else den_in[h, at, :]
                for k, part_ref in enumerate(part_refs):
                    for t in range(chunk_tiles):
                        s, s_low = score_rows(part_ref, t, h)
                        x = jnp.maximum(pos + s, neg + s_low)
                        p = w_refs[k][0, rt, t, i0 : i0 + block, :] * jnp.exp2(x)
                        den = den + p
                        pairs[h].append(split(p))
                den_out[h, at, :] = den
            num = weighted(stack(pairs), z_cat)
            num_out[at, :] = num if num_in is None else num_in[at, :] + num

    shape_t, shape_w, shape_d = (all_rows, TILE), (all_rows, width), (heads, all_rows, TILE)
    part_spec = whole((pack_rows, lanes))

    def unit_spec(k, ch):
        return pl.BlockSpec(
            (1, unroll, chunk_tiles, TILE, TILE), lambda s: (k * n_chunk + ch, s, 0, 0, 0)
        )

    def stage(kernel, keys, before, before_shapes, outs, extra=(), scratch=()):
        n = len(keys)
        return pl.pallas_call(
            kernel,
            out_shape=[pltpu.VMEM(s, F32) for s in outs],
            grid=(steps,),
            in_specs=[whole(s) for s in before_shapes]
            + [part_spec] * (n + len(extra))
            + [unit_spec(*key) for key in (*keys, *extra)],
            out_specs=[whole(s) for s in outs],
            scratch_shapes=scratch,
            cost_estimate=pl.CostEstimate(
                flops=all_rows * n * part_rows * width * heads * 8,
                bytes_accessed=n * part_rows * width * 4,
                transcendentals=all_rows * n * part_rows * heads,
            ),
            compiler_params=pltpu.CompilerParams(vmem_limit_bytes=limit(16, 4 * tiles * TILE * TILE)),
        )(*before, *(parts[key] for key in (*keys, *extra)), *[panel] * (n + len(extra)))

    near_keys = [(k, ch) for ch in range(n_chunk) for k in range(far_first)]

    def near_kernel(*refs):
        n = len(near_keys)
        n_tgt = len(targets)
        tgt_refs, part_refs, w_refs = refs[:n_tgt], refs[n_tgt : n_tgt + n], refs[n_tgt + n :][:n]
        posneg, tgt_m, den_out, num_out = refs[n_tgt + 2 * n :]
        col = lax.axis_index("col")

        @pl.when(pl.program_id(0) == 0)
        def _():
            shape = (up8(heads), TILE)
            eye = (
                lax.broadcasted_iota(jnp.int32, shape, 0)
                == lax.broadcasted_iota(jnp.int32, shape, 1) % heads
            ).astype(F32)
            lane = lax.broadcasted_iota(jnp.int32, (1, TILE), 1)
            bound = jnp.zeros((1, TILE), F32)
            for h in range(heads):
                rows = [score_rows(r, t, h)[0] for r in part_refs for t in range(chunk_tiles)]
                top = rows[0]
                for other in rows[1:]:
                    top = jnp.maximum(top, other)
                top = jnp.max(top, axis=1, keepdims=True)
                bound = jnp.where(lane % heads == h, top, bound)
            for d in range(n_col):
                at = pl.ds(
                    pl.multiple_of(comes_from(col, d, n_col) * own_rows, own_rows), own_rows
                )
                k, g = divmod(d, size)
                a = contract(tgt_refs[k][g * rows_of : (g + 1) * rows_of], eye, ((0,), (0,)))
                m = leaky(a + bound)
                tgt_m[at, :] = jnp.where(lane < heads, a, m)
                posneg[at, :] = jnp.where(lane < heads, a, SLOPE * a) - m

        attend(part_refs, w_refs, posneg, None, None, den_out, num_out)

    def middle_kernel(*refs):
        n = len(middle_keys)
        (posneg, den_in, num_in), refs = refs[:3], refs[3:]
        part_refs, w_refs, (den_out, num_out) = refs[:n], refs[n : 2 * n], refs[2 * n :]
        attend(part_refs, w_refs, posneg, den_in, num_in, den_out, num_out)

    def last_kernel(*refs):
        n, n_all = len(last_keys), len(last_keys) + len(other_keys)
        (posneg, den_in, num_in, tgt_m), refs = refs[:4], refs[4:]
        part_refs, w_refs, refs = refs[:n_all], refs[n_all : 2 * n_all], refs[2 * n_all :]
        out_refs, (den_s, num_s, md_s) = refs[:n_col], refs[n_col:]
        col = lax.axis_index("col")
        step = pl.program_id(0)

        attend(part_refs[:n], w_refs[:n], posneg, den_in, num_in, den_s, num_s)
        base = step * group_rows
        low = high = None
        for b in range(unroll * blocks):
            at = pl.ds(pl.multiple_of(base + b * block, block), block)
            md = tgt_m[at, :]
            for h in range(heads):
                den = jnp.sum(den_s[h, at, :], axis=1, keepdims=True)
                low = den if low is None else jnp.minimum(low, den)
                high = den if high is None else jnp.maximum(high, den)
                md = jnp.where(lane_t() == h, den, md)
            md_s[at, :] = md
        fine = jnp.logical_and(jnp.min(low) >= tiny, jnp.max(high) <= huge)

        @pl.when(jnp.logical_not(fine))
        def _():
            @pl.loop(0, unroll * blocks)
            def _(b):
                at = pl.ds(pl.multiple_of(base + b * block, block), block)
                rt = b // blocks
                rows = pl.ds(pl.multiple_of((b % blocks) * block, block), block)
                md = tgt_m[at, :]
                posnegs, dens = [], []
                for h in range(heads):
                    best = jnp.full((block, TILE), NEG, F32)
                    for part_ref, w_ref in zip(part_refs, w_refs):
                        for t in range(chunk_tiles):
                            edge = w_ref[0, rt, t, rows, :] > 0
                            s = score_rows(part_ref, t, h)[0]
                            best = jnp.maximum(best, jnp.where(edge, s, NEG))
                    a = tgt_m[at, :][:, h : h + 1]
                    m = leaky(a + jnp.max(best, axis=1, keepdims=True))
                    md = jnp.where(lane_t() == heads + h, m, md)
                    posnegs.append((a - m, SLOPE * a - m))
                    dens.append(jnp.zeros((block, TILE), F32))
                num_s[at, :] = jnp.zeros((block, width), F32)
                for part_ref, w_ref in zip(part_refs, w_refs):
                    pairs = []
                    for h in range(heads):
                        pairs.append([])
                        pos, neg = posnegs[h]
                        for t in range(chunk_tiles):
                            s, s_low = score_rows(part_ref, t, h)
                            x = jnp.minimum(jnp.maximum(pos + s, neg + s_low), 0.0)
                            p = w_ref[0, rt, t, rows, :] * jnp.exp2(x)
                            dens[h] = dens[h] + p
                            pairs[h].append(split(p))
                    num_s[at, :] = num_s[at, :] + weighted(stack(pairs), split_z([part_ref]))
                for h in range(heads):
                    md = jnp.where(lane_t() == h, jnp.sum(dens[h], axis=1, keepdims=True), md)
                md_s[at, :] = md

        @pl.when(step == steps - 1)
        def _():
            for d in range(n_col):
                at = pl.ds(
                    pl.multiple_of(goes_to(col, d, n_col) * own_rows, own_rows), own_rows
                )
                if width < lanes:
                    out_refs[d][...] = jnp.zeros_like(out_refs[d])
                out_refs[d][:own_rows, :width] = num_s[at, :]
                out_refs[d][own_rows:, :own_rows] = md_s[at, :].T[:mdp]

    posneg, tgt_m, den, num = stage(
        near_kernel,
        near_keys,
        targets,
        [(size * rows_of, own_rows)] * len(targets),
        [shape_t, shape_t, shape_d, shape_w],
    )
    arrived = [parts[far_first, ch] for ch in range(n_chunk)]
    arrived, den = lax.optimization_barrier((arrived, den))
    for ch in range(n_chunk):
        parts[far_first, ch] = arrived[ch]
        spread(far_first, ch)
    far_keys = [(k, ch) for k in range(far_first, n_row) for ch in range(n_chunk)]
    middle_keys = far_keys[:n_chunk] if n_row > 2 else []
    if middle_keys:
        den, num = stage(
            middle_kernel,
            middle_keys,
            (posneg, den, num),
            [shape_t, shape_d, shape_w],
            [shape_d, shape_w],
        )
    last_keys = far_keys[len(middle_keys) :]
    other_keys = near_keys + middle_keys
    chunks = stage(
        last_kernel,
        last_keys,
        (posneg, den, num, tgt_m),
        [shape_t, shape_d, shape_w, shape_t],
        [(chunk_rows, lanes)] * n_col,
        extra=other_keys,
        scratch=[
            pltpu.VMEM(shape_d, F32),
            pltpu.VMEM(shape_w, F32),
            pltpu.VMEM(shape_t, F32),
        ],
    )
    gathered = [hop(chunks[d], "col", d) for d in range(n_col - 1, 0, -1)]
    gathered = [chunks[0]] + gathered[::-1]

    def out_kernel(zdst_ref, src_ref, dst_ref, bias_ref, *rest):
        parts, out_ref = rest[:n_col], rest[n_col]
        same = (
            lax.broadcasted_iota(jnp.int32, (width, width), 0) // dims
            == lax.broadcasted_iota(jnp.int32, (width, width), 1) // dims
        ).astype(F32)
        z = zdst_ref[...]
        pair = contract(z * (dst_ref[...] + src_ref[...]), same, ((1,), (0,)))
        e_self = leaky(LOG2E * pair)
        which = lax.broadcasted_iota(jnp.int32, (mdp, width), 0)
        head = lax.broadcasted_iota(jnp.int32, (mdp, width), 1) // dims
        den_of, m_of = (which == head).astype(F32), (which == head + heads).astype(F32)
        mds = [part[own_rows:, :own_rows] for part in parts]
        ms = [contract(md, m_of, ((0,), (0,))) for md in mds]
        dens = [contract(md, den_of, ((0,), (0,))) for md in mds]
        top = e_self
        for m in ms:
            top = jnp.maximum(top, m)
        den = jnp.exp2(e_self - top)
        num = den * z
        for part, m, own_den in zip(parts, ms, dens):
            factor = jnp.exp2(m - top)
            den = den + factor * own_den
            num = num + factor * part[:own_rows, :width]
        x = num / den + bias_ref[...]
        out_ref[...] = jnp.where(x > 0, x, jnp.exp(jnp.minimum(x, 0.0)) - 1.0).astype(BF16)

    return call(
        out_kernel,
        jax.ShapeDtypeStruct((own_rows, width), BF16),
        zdst,
        att_src2,
        att_dst2,
        bias2,
        *gathered,
    )


def solution(mesh):
    return jax.shard_map(
        on_device,
        mesh=mesh,
        in_specs=(
            P(("row", "col"), "feat"),
            P(("row", "col"), "feat"),
            P("feat", None),
            P("feat"),
            P("feat"),
            P("feat"),
            P("row", "col", None),
            P("row", "col", None),
            P("row", "col"),
            P("row", "col", None, None, None),
        ),
        out_specs=P(("row", "col"), "feat"),
        check_vma=False,
    )
```

```python
import jax
import jax.numpy as jnp
from jax import lax
from jax.experimental import pallas as pl
from jax.experimental.pallas import tpu as pltpu
from jax.sharding import PartitionSpec as P

HEADS = 8
TILE = 128
SLOPE = 0.2
LOG2E = 1.4426950408889634
NEG = -1e30
F32 = jnp.float32
BF16 = jnp.bfloat16
HIGHEST = lax.Precision.HIGHEST
VMEM = pl.BlockSpec(memory_space=pltpu.VMEM)
SMEM = pl.BlockSpec(memory_space=pltpu.SMEM)
HBM = pl.BlockSpec(memory_space=pltpu.HBM)


def is_pow2(n):
    return n & (n - 1) == 0


def goes_to(i, d, n):
    return i ^ d if is_pow2(n) else lax.rem(i + d, n)


def comes_from(i, d, n):
    return i ^ d if is_pow2(n) else lax.rem(i + n - d, n)


def hop(x, axis, d):
    n = lax.axis_size(axis)
    pairs = [(i, i ^ d if is_pow2(n) else (i + d) % n) for i in range(n)]
    return lax.ppermute(x, axis, pairs)


def call(kernel, out_shape, *args, in_specs=None, flops=0, bytes_accessed=0, grant=8 << 20, **kw):
    return pl.pallas_call(
        kernel,
        out_shape=out_shape,
        in_specs=in_specs or [VMEM] * len(args),
        cost_estimate=pl.CostEstimate(
            flops=flops, bytes_accessed=bytes_accessed, transcendentals=0
        ),
        compiler_params=pltpu.CompilerParams(vmem_limit_bytes=grant),
        **kw,
    )(*args)


def limit(mib, least):
    return min(max(mib << 20, least), 60 << 20)


def in_hbm(x):
    return pltpu.with_memory_space_constraint(x, pltpu.HBM)


def up8(n):
    return -(-n // 8) * 8


def head_rows(vector, heads, width, height):
    dims = width // heads
    shape = (height, width)
    row = lax.broadcasted_iota(jnp.int32, shape, 0) % heads
    lane = lax.broadcasted_iota(jnp.int32, shape, 1)
    return jnp.where(lane // dims == row, jnp.broadcast_to(vector, shape), 0.0)


def contract(lhs, rhs, dims, precision=HIGHEST):
    return lax.dot_general(
        lhs, rhs, (dims, ((), ())), preferred_element_type=F32, precision=precision
    )


def take_cols(proj_ref, which, width):
    if width % TILE == 0:
        return proj_ref[:, pl.ds(pl.multiple_of(which * width, width), width)]
    full = proj_ref[...]
    out = full[:, :width]
    for k in range(1, full.shape[1] // width):
        out = jnp.where(which == k, full[:, k * width : (k + 1) * width], out)
    return out


def project(x, w):
    return lax.dot_general(x, w, (((1,), (0,)), ((), ())), preferred_element_type=F32)


def leaky(x):
    return jnp.maximum(x, SLOPE * x)


def on_device(
    src_feats, dst_feats, proj, att_src, att_dst, bias, tile_rows, tile_cols, tile_count, edge_weight
):
    n_row, n_col, n_feat = (lax.axis_size(a) for a in ("row", "col", "feat"))
    width = proj.shape[1] // n_feat
    heads = HEADS // n_feat
    dims = width // heads
    lanes = -(-width // TILE) * TILE
    src_rows, own_rows = src_feats.shape[0], dst_feats.shape[0]
    slots = tile_rows.shape[2]
    row_tiles = own_rows * n_col // TILE
    piece_tiles = src_rows // TILE
    n_chunk = 2 if piece_tiles % 2 == 0 else 1
    chunk_tiles = piece_tiles // n_chunk
    part_rows = src_rows // n_chunk
    col_tiles = piece_tiles * n_row
    hp = up8(2 * heads)
    mdp = up8(2 * heads)
    att_src2, att_dst2, bias2 = (v.reshape(1, width) for v in (att_src, att_dst, bias))

    def fetch(hbm, vmem, sems):
        copies = [pltpu.make_async_copy(h, v, sems.at[k]) for k, (h, v) in enumerate(zip(hbm, vmem))]
        for copy in copies:
            copy.start()
        for copy in copies:
            copy.wait()

    def fetching(kernel, outs, *args):
        return call(
            kernel,
            outs,
            *map(in_hbm, args),
            in_specs=[HBM] * len(args),
            scratch_shapes=[
                *(pltpu.VMEM(v.shape, v.dtype) for v in args),
                pltpu.SemaphoreType.DMA((len(args),)),
            ],
        )

    def send_kernel(*refs):
        hbm, outs, refs = refs[:4], refs[4:-5], refs[-5:]
        fetch(hbm, refs[:4], refs[4])
        src_ref, dst_ref, proj_ref, att_ref = refs[:4]
        me = lax.axis_index("feat")
        outs[0][...] = project(dst_ref[...], take_cols(proj_ref, me, width))
        outs[1][...] = LOG2E * head_rows(att_ref[...], heads, width, up8(heads))
        for d in range(1, n_feat):
            w = take_cols(proj_ref, goes_to(me, d, n_feat), width)
            own_outs = outs[2 + (d - 1) * (n_chunk + 1) : 2 + d * (n_chunk + 1)]
            own_outs[0][...] = project(dst_ref[...], w)
            for ch in range(n_chunk):
                own_outs[ch + 1][...] = project(src_ref[ch * part_rows : (ch + 1) * part_rows], w)

    dst_own, dst_att, *sent = fetching(
        send_kernel,
        [pltpu.VMEM((own_rows, width), F32), pltpu.VMEM((up8(heads), width), F32)]
        + [
            pltpu.VMEM((n, width), F32)
            for _ in range(1, n_feat)
            for n in [own_rows] + [part_rows] * n_chunk
        ],
        src_feats,
        dst_feats,
        proj,
        att_dst2,
    )
    sent = [sent[k :: n_chunk + 1] for k in range(n_chunk + 1)]
    dst_parts = [hop(sent[0][d - 1], "feat", d) for d in range(1, n_feat)]
    src_parts = [[hop(part[d - 1], "feat", d) for d in range(1, n_feat)] for part in sent[1:]]

    tiles = row_tiles * col_tiles
    whole = lambda shape: pl.BlockSpec(shape, lambda s: (0,) * len(shape))

    def dst_kernel(own_ref, att_ref, *rest):
        got, (z_ref, s_ref) = rest[: n_feat - 1], rest[n_feat - 1 :]
        z = own_ref[...]
        for part in got:
            z = z + part[...]
        z_ref[...] = z
        s_ref[...] = contract(att_ref[...], z, ((1,), (1,)))

    zdst, s_dst = call(
        dst_kernel,
        [
            jax.ShapeDtypeStruct((own_rows, width), F32),
            jax.ShapeDtypeStruct((up8(heads), own_rows), F32),
        ],
        dst_own,
        dst_att,
        *dst_parts,
    )
    rows_of = up8(heads)
    if is_pow2(n_col) and n_col > 1:
        bits = n_col.bit_length() - 1
        place = lambda d: sum(((d >> k) & 1) << (bits - 1 - k) for k in range(bits))
        targets, d = [s_dst], n_col // 2
        while d:
            targets = [targets[0], hop(targets[0], "col", d)]
            d //= 2
            if d:

                def join_kernel(low_ref, high_ref, out_ref):
                    out_ref[...] = jnp.concatenate([low_ref[...], high_ref[...]], axis=0)

                shape = (2 * targets[0].shape[0], own_rows)
                targets = [call(join_kernel, pltpu.VMEM(shape, F32), *targets)]
    else:
        place = lambda d: d
        targets = [s_dst] + [hop(s_dst, "col", d) for d in range(1, n_col)]
    size = n_col // len(targets)

    units = n_row * n_chunk
    period = min(slots, tiles) if slots % min(slots, tiles) == 0 else slots
    reps = slots // period
    group = 8
    groups = period // group

    def local_kernel(*refs):
        hbm, count_ref, refs = refs[:6], refs[6], refs[7:]
        outs, panel_ref, refs = refs[: 1 + n_chunk], refs[1 + n_chunk], refs[2 + n_chunk :]
        src_ref, proj_ref, att_ref, rows_ref, cols_ref, w_ref, sems, w_sems = refs
        small = [
            pltpu.make_async_copy(h, v, sems.at[k]) for k, (h, v) in enumerate(zip(hbm[:5], refs[:5]))
        ]
        large = [
            pltpu.make_async_copy(
                hbm[5].at[k, pl.ds(g * group, group)],
                w_ref.at[k, pl.ds(g * group, group)],
                w_sems.at[g, k],
            )
            for g in range(groups)
            for k in range(reps)
        ]
        for copy in small + large:
            copy.start()

        @pl.loop(0, units)
        def _(u):
            @pl.loop(0, row_tiles)
            def _(r):
                panel_ref[u, r] = jnp.zeros((chunk_tiles, TILE, TILE), F32)

        for copy in small:
            copy.wait()
        outs[0][...] = LOG2E * head_rows(att_ref[...], heads, width, hp)
        w = take_cols(proj_ref, lax.axis_index("feat"), width)
        for ch in range(n_chunk):
            outs[1 + ch][...] = project(src_ref[ch * part_rows : (ch + 1) * part_rows], w)

        row = lax.axis_index("row")
        count = count_ref[0, 0]
        for g in range(groups):
            for copy in large[g * reps : (g + 1) * reps]:
                copy.wait()
            base = g * group

            @pl.loop(base, jnp.clip(count, base, base + group))
            def _(u):
                r, c = rows_ref[0, 0, u], cols_ref[0, 0, u]
                unit = ((c // piece_tiles) ^ row) * n_chunk + c % piece_tiles // chunk_tiles
                t = c % chunk_tiles
                total = w_ref[0, u].astype(F32)
                for k in range(1, reps):
                    live = (u + k * period < count).astype(F32)
                    total = total + w_ref[k, u].astype(F32) * live
                panel_ref[unit, r, t] = panel_ref[unit, r, t] + total

    slot_weights = edge_weight.reshape(reps, period, TILE, TILE)
    inputs = (src_feats, proj, att_src2, tile_rows, tile_cols, slot_weights)
    src_att, *src_own, panel = call(
        local_kernel,
        [pltpu.VMEM((hp, width), F32)]
        + [pltpu.VMEM((part_rows, width), F32)] * n_chunk
        + [pltpu.VMEM((units, row_tiles, chunk_tiles, TILE, TILE), F32)],
        *map(in_hbm, inputs),
        tile_count,
        in_specs=[HBM] * len(inputs) + [SMEM],
        scratch_shapes=[
            *(
                (pltpu.SMEM if v.dtype == jnp.int32 else pltpu.VMEM)(v.shape, v.dtype)
                for v in inputs
            ),
            pltpu.SemaphoreType.DMA((5,)),
            pltpu.SemaphoreType.DMA((groups, reps)),
        ],
        grant=12 << 20,
    )

    pack_rows = part_rows + chunk_tiles * hp

    def z_kernel(own_ref, att_ref, *rest):
        got, out_ref = rest[: n_feat - 1], rest[n_feat - 1]
        z = own_ref[...]
        for part in got:
            z = z + part[...]
        if width < lanes:
            out_ref[...] = jnp.zeros_like(out_ref)
        out_ref[:part_rows, :width] = z
        s = contract(att_ref[...], z, ((1,), (1,)))
        low = lax.broadcasted_iota(jnp.int32, s.shape, 0) < heads
        s = jnp.where(low, s, SLOPE * s)
        for t in range(chunk_tiles):
            at = part_rows + t * hp
            out_ref[at : at + hp, :TILE] = s[:, t * TILE : (t + 1) * TILE]

    parts, far_first = {}, n_row // 2
    for ch in range(n_chunk):
        own = call(z_kernel, pltpu.VMEM((pack_rows, lanes), F32), src_own[ch], src_att, *src_parts[ch])
        parts[far_first, ch] = hop(own, "row", far_first)
        parts[0, ch] = own

    def spread(first, ch):
        d = n_row // 4
        while d:
            for k in [k for k, c in parts if c == ch and k ^ first < far_first]:
                parts[k ^ d, ch] = hop(parts[k, ch], "row", d)
            d //= 2

    for ch in range(n_chunk):
        spread(0, ch)

    block = 64
    blocks = TILE // block
    unroll = 2 if row_tiles % 2 == 0 else 1
    steps = row_tiles // unroll
    chunk_rows = own_rows + mdp
    group_rows = unroll * TILE
    all_rows = row_tiles * TILE
    tiny, huge = 2.0**-60, 2.0**60
    lane_w = lambda: lax.broadcasted_iota(jnp.int32, (block, width), 1) // dims
    lane_t = lambda: lax.broadcasted_iota(jnp.int32, (block, TILE), 1)

    def score_rows(part_ref, t, h):
        at = part_rows + t * hp + h
        return part_ref[at : at + 1, :TILE], part_ref[at + heads : at + heads + 1, :TILE]

    def split(x):
        hi = x.astype(BF16)
        return hi, (x - hi.astype(F32)).astype(BF16)

    def split_z(part_refs):
        return jnp.concatenate(
            [jnp.concatenate(split(p[:part_rows, :width]), axis=1) for p in part_refs], axis=0
        )

    def stack(pairs):
        return jnp.concatenate(
            [jnp.concatenate([p[k] for p in row], axis=1) for row in pairs for k in range(2)], axis=0
        )

    def weighted(probs, z):
        both = lax.dot_general(probs, z, (((1,), (0,)), ((), ())), preferred_element_type=F32)
        num = jnp.zeros((block, width), F32)
        for h in range(heads):
            hi = both[2 * h * block : (2 * h + 1) * block]
            lo = both[(2 * h + 1) * block : (2 * h + 2) * block]
            num = jnp.where(lane_w() == h, hi[:, :width] + (hi[:, width:] + lo[:, :width]), num)
        return num

    def attend(part_refs, w_refs, posneg, den_in, num_in, den_out, num_out):
        base = pl.program_id(0) * group_rows
        z_cat = split_z(part_refs)
        for b in range(unroll * blocks):
            at = pl.ds(pl.multiple_of(base + b * block, block), block)
            rt, i0 = divmod(b * block, TILE)
            pairs = []
            for h in range(heads):
                pairs.append([])
                pn = posneg[at, :]
                pos = jnp.broadcast_to(pn[:, h : h + 1], (block, TILE))
                neg = jnp.broadcast_to(pn[:, heads + h : heads + h + 1], (block, TILE))
                den = jnp.zeros((block, TILE), F32) if den_in is None else den_in[h, at, :]
                for k, part_ref in enumerate(part_refs):
                    for t in range(chunk_tiles):
                        s, s_low = score_rows(part_ref, t, h)
                        x = jnp.maximum(pos + s, neg + s_low)
                        p = w_refs[k][0, rt, t, i0 : i0 + block, :] * jnp.exp2(x)
                        den = den + p
                        pairs[h].append(split(p))
                den_out[h, at, :] = den
            num = weighted(stack(pairs), z_cat)
            num_out[at, :] = num if num_in is None else num_in[at, :] + num

    shape_t, shape_w, shape_d = (all_rows, TILE), (all_rows, width), (heads, all_rows, TILE)
    part_spec = whole((pack_rows, lanes))

    def unit_spec(k, ch):
        return pl.BlockSpec(
            (1, unroll, chunk_tiles, TILE, TILE), lambda s: (k * n_chunk + ch, s, 0, 0, 0)
        )

    def stage(kernel, keys, before, before_shapes, outs, extra=(), scratch=()):
        n = len(keys)
        return pl.pallas_call(
            kernel,
            out_shape=[pltpu.VMEM(s, F32) for s in outs],
            grid=(steps,),
            in_specs=[whole(s) for s in before_shapes]
            + [part_spec] * (n + len(extra))
            + [unit_spec(*key) for key in (*keys, *extra)],
            out_specs=[whole(s) for s in outs],
            scratch_shapes=scratch,
            cost_estimate=pl.CostEstimate(
                flops=all_rows * n * part_rows * width * heads * 8,
                bytes_accessed=n * part_rows * width * 4,
                transcendentals=all_rows * n * part_rows * heads,
            ),
            compiler_params=pltpu.CompilerParams(vmem_limit_bytes=limit(16, 4 * tiles * TILE * TILE)),
        )(*before, *(parts[key] for key in (*keys, *extra)), *[panel] * (n + len(extra)))

    near_keys = [(k, ch) for ch in range(n_chunk) for k in range(far_first)]

    def near_kernel(*refs):
        n = len(near_keys)
        n_tgt = len(targets)
        tgt_refs, part_refs, w_refs = refs[:n_tgt], refs[n_tgt : n_tgt + n], refs[n_tgt + n :][:n]
        posneg, tgt_m, den_out, num_out = refs[n_tgt + 2 * n :]
        col = lax.axis_index("col")

        @pl.when(pl.program_id(0) == 0)
        def _():
            shape = (up8(heads), TILE)
            eye = (
                lax.broadcasted_iota(jnp.int32, shape, 0)
                == lax.broadcasted_iota(jnp.int32, shape, 1) % heads
            ).astype(F32)
            lane = lax.broadcasted_iota(jnp.int32, (1, TILE), 1)
            bound = jnp.zeros((1, TILE), F32)
            for h in range(heads):
                rows = [score_rows(r, t, h)[0] for r in part_refs for t in range(chunk_tiles)]
                top = rows[0]
                for other in rows[1:]:
                    top = jnp.maximum(top, other)
                top = jnp.max(top, axis=1, keepdims=True)
                bound = jnp.where(lane % heads == h, top, bound)
            for d in range(n_col):
                at = pl.ds(
                    pl.multiple_of(comes_from(col, d, n_col) * own_rows, own_rows), own_rows
                )
                k, g = divmod(place(d), size)
                a = contract(tgt_refs[k][g * rows_of : (g + 1) * rows_of], eye, ((0,), (0,)))
                m = leaky(a + bound)
                tgt_m[at, :] = jnp.where(lane < heads, a, m)
                posneg[at, :] = jnp.where(lane < heads, a, SLOPE * a) - m

        attend(part_refs, w_refs, posneg, None, None, den_out, num_out)

    def middle_kernel(*refs):
        n = len(middle_keys)
        (posneg, den_in, num_in), refs = refs[:3], refs[3:]
        part_refs, w_refs, (den_out, num_out) = refs[:n], refs[n : 2 * n], refs[2 * n :]
        attend(part_refs, w_refs, posneg, den_in, num_in, den_out, num_out)

    def last_kernel(*refs):
        n, n_all = len(last_keys), len(last_keys) + len(other_keys)
        (posneg, den_in, num_in, tgt_m), refs = refs[:4], refs[4:]
        part_refs, w_refs, refs = refs[:n_all], refs[n_all : 2 * n_all], refs[2 * n_all :]
        out_refs, (den_s, num_s, md_s) = refs[:n_col], refs[n_col:]
        col = lax.axis_index("col")
        step = pl.program_id(0)

        attend(part_refs[:n], w_refs[:n], posneg, den_in, num_in, den_s, num_s)
        base = step * group_rows
        low = high = None
        for b in range(unroll * blocks):
            at = pl.ds(pl.multiple_of(base + b * block, block), block)
            md = tgt_m[at, :]
            for h in range(heads):
                den = jnp.sum(den_s[h, at, :], axis=1, keepdims=True)
                low = den if low is None else jnp.minimum(low, den)
                high = den if high is None else jnp.maximum(high, den)
                md = jnp.where(lane_t() == h, den, md)
            md_s[at, :] = md
        fine = jnp.logical_and(jnp.min(low) >= tiny, jnp.max(high) <= huge)

        @pl.when(jnp.logical_not(fine))
        def _():
            @pl.loop(0, unroll * blocks)
            def _(b):
                at = pl.ds(pl.multiple_of(base + b * block, block), block)
                rt = b // blocks
                rows = pl.ds(pl.multiple_of((b % blocks) * block, block), block)
                md = tgt_m[at, :]
                posnegs, dens = [], []
                for h in range(heads):
                    best = jnp.full((block, TILE), NEG, F32)
                    for part_ref, w_ref in zip(part_refs, w_refs):
                        for t in range(chunk_tiles):
                            edge = w_ref[0, rt, t, rows, :] > 0
                            s = score_rows(part_ref, t, h)[0]
                            best = jnp.maximum(best, jnp.where(edge, s, NEG))
                    a = tgt_m[at, :][:, h : h + 1]
                    m = leaky(a + jnp.max(best, axis=1, keepdims=True))
                    md = jnp.where(lane_t() == heads + h, m, md)
                    posnegs.append((a - m, SLOPE * a - m))
                    dens.append(jnp.zeros((block, TILE), F32))
                num_s[at, :] = jnp.zeros((block, width), F32)
                for part_ref, w_ref in zip(part_refs, w_refs):
                    pairs = []
                    for h in range(heads):
                        pairs.append([])
                        pos, neg = posnegs[h]
                        for t in range(chunk_tiles):
                            s, s_low = score_rows(part_ref, t, h)
                            x = jnp.minimum(jnp.maximum(pos + s, neg + s_low), 0.0)
                            p = w_ref[0, rt, t, rows, :] * jnp.exp2(x)
                            dens[h] = dens[h] + p
                            pairs[h].append(split(p))
                    num_s[at, :] = num_s[at, :] + weighted(stack(pairs), split_z([part_ref]))
                for h in range(heads):
                    md = jnp.where(lane_t() == h, jnp.sum(dens[h], axis=1, keepdims=True), md)
                md_s[at, :] = md

        @pl.when(step == steps - 1)
        def _():
            for d in range(n_col):
                at = pl.ds(
                    pl.multiple_of(goes_to(col, d, n_col) * own_rows, own_rows), own_rows
                )
                if width < lanes:
                    out_refs[d][...] = jnp.zeros_like(out_refs[d])
                out_refs[d][:own_rows, :width] = num_s[at, :]
                out_refs[d][own_rows:, :own_rows] = md_s[at, :].T[:mdp]

    posneg, tgt_m, den, num = stage(
        near_kernel,
        near_keys,
        targets,
        [(size * rows_of, own_rows)] * len(targets),
        [shape_t, shape_t, shape_d, shape_w],
    )
    arrived = [parts[far_first, ch] for ch in range(n_chunk)]
    arrived, den = lax.optimization_barrier((arrived, den))
    for ch in range(n_chunk):
        parts[far_first, ch] = arrived[ch]
        spread(far_first, ch)
    far_keys = [(k, ch) for k in range(far_first, n_row) for ch in range(n_chunk)]
    middle_keys = far_keys[:n_chunk] if n_row > 2 else []
    if middle_keys:
        den, num = stage(
            middle_kernel,
            middle_keys,
            (posneg, den, num),
            [shape_t, shape_d, shape_w],
            [shape_d, shape_w],
        )
    last_keys = far_keys[len(middle_keys) :]
    other_keys = near_keys + middle_keys
    chunks = stage(
        last_kernel,
        last_keys,
        (posneg, den, num, tgt_m),
        [shape_t, shape_d, shape_w, shape_t],
        [(chunk_rows, lanes)] * n_col,
        extra=other_keys,
        scratch=[
            pltpu.VMEM(shape_d, F32),
            pltpu.VMEM(shape_w, F32),
            pltpu.VMEM(shape_t, F32),
        ],
    )
    gathered = [hop(chunks[d], "col", d) for d in range(n_col - 1, 0, -1)]
    gathered = [chunks[0]] + gathered[::-1]

    def out_kernel(zdst_ref, src_ref, dst_ref, bias_ref, *rest):
        parts, out_ref = rest[:n_col], rest[n_col]
        same = (
            lax.broadcasted_iota(jnp.int32, (width, width), 0) // dims
            == lax.broadcasted_iota(jnp.int32, (width, width), 1) // dims
        ).astype(F32)
        z = zdst_ref[...]
        pair = contract(z * (dst_ref[...] + src_ref[...]), same, ((1,), (0,)))
        e_self = leaky(LOG2E * pair)
        which = lax.broadcasted_iota(jnp.int32, (mdp, width), 0)
        head = lax.broadcasted_iota(jnp.int32, (mdp, width), 1) // dims
        den_of, m_of = (which == head).astype(F32), (which == head + heads).astype(F32)
        mds = [part[own_rows:, :own_rows] for part in parts]
        ms = [contract(md, m_of, ((0,), (0,))) for md in mds]
        dens = [contract(md, den_of, ((0,), (0,))) for md in mds]
        top = e_self
        for m in ms:
            top = jnp.maximum(top, m)
        den = jnp.exp2(e_self - top)
        num = den * z
        for part, m, own_den in zip(parts, ms, dens):
            factor = jnp.exp2(m - top)
            den = den + factor * own_den
            num = num + factor * part[:own_rows, :width]
        x = num / den + bias_ref[...]
        out_ref[...] = jnp.where(x > 0, x, jnp.exp(jnp.minimum(x, 0.0)) - 1.0).astype(BF16)

    return call(
        out_kernel,
        jax.ShapeDtypeStruct((own_rows, width), BF16),
        zdst,
        att_src2,
        att_dst2,
        bias2,
        *gathered,
    )


def solution(mesh):
    return jax.shard_map(
        on_device,
        mesh=mesh,
        in_specs=(
            P(("row", "col"), "feat"),
            P(("row", "col"), "feat"),
            P("feat", None),
            P("feat"),
            P("feat"),
            P("feat"),
            P("row", "col", None),
            P("row", "col", None),
            P("row", "col"),
            P("row", "col", None, None, None),
        ),
        out_specs=P(("row", "col"), "feat"),
        check_vma=False,
    )
```

```python
import jax
import jax.numpy as jnp
from jax import lax
from jax.experimental import pallas as pl
from jax.experimental.pallas import tpu as pltpu
from jax.sharding import PartitionSpec as P

HEADS = 8
TILE = 128
SLOPE = 0.2
LOG2E = 1.4426950408889634
NEG = -1e30
F32 = jnp.float32
BF16 = jnp.bfloat16
HIGHEST = lax.Precision.HIGHEST
VMEM = pl.BlockSpec(memory_space=pltpu.VMEM)
SMEM = pl.BlockSpec(memory_space=pltpu.SMEM)
HBM = pl.BlockSpec(memory_space=pltpu.HBM)


def is_pow2(n):
    return n & (n - 1) == 0


def goes_to(i, d, n):
    return i ^ d if is_pow2(n) else lax.rem(i + d, n)


def comes_from(i, d, n):
    return i ^ d if is_pow2(n) else lax.rem(i + n - d, n)


def hop(x, axis, d):
    n = lax.axis_size(axis)
    pairs = [(i, i ^ d if is_pow2(n) else (i + d) % n) for i in range(n)]
    return lax.ppermute(x, axis, pairs)


def call(kernel, out_shape, *args, in_specs=None, flops=0, bytes_accessed=0, grant=8 << 20, **kw):
    return pl.pallas_call(
        kernel,
        out_shape=out_shape,
        in_specs=in_specs or [VMEM] * len(args),
        cost_estimate=pl.CostEstimate(
            flops=flops, bytes_accessed=bytes_accessed, transcendentals=0
        ),
        compiler_params=pltpu.CompilerParams(vmem_limit_bytes=grant),
        **kw,
    )(*args)


def limit(mib, least):
    return min(max(mib << 20, least), 60 << 20)


def in_hbm(x):
    return pltpu.with_memory_space_constraint(x, pltpu.HBM)


def up8(n):
    return -(-n // 8) * 8


def head_rows(vector, heads, width, height):
    dims = width // heads
    shape = (height, width)
    row = lax.broadcasted_iota(jnp.int32, shape, 0) % heads
    lane = lax.broadcasted_iota(jnp.int32, shape, 1)
    return jnp.where(lane // dims == row, jnp.broadcast_to(vector, shape), 0.0)


def contract(lhs, rhs, dims, precision=HIGHEST):
    return lax.dot_general(
        lhs, rhs, (dims, ((), ())), preferred_element_type=F32, precision=precision
    )


def take_cols(proj_ref, which, width):
    if width % TILE == 0:
        return proj_ref[:, pl.ds(pl.multiple_of(which * width, width), width)]
    full = proj_ref[...]
    out = full[:, :width]
    for k in range(1, full.shape[1] // width):
        out = jnp.where(which == k, full[:, k * width : (k + 1) * width], out)
    return out


def project(x, w):
    return lax.dot_general(x, w, (((1,), (0,)), ((), ())), preferred_element_type=F32)


def leaky(x):
    return jnp.maximum(x, SLOPE * x)


def on_device(
    src_feats, dst_feats, proj, att_src, att_dst, bias, tile_rows, tile_cols, tile_count, edge_weight
):
    n_row, n_col, n_feat = (lax.axis_size(a) for a in ("row", "col", "feat"))
    width = proj.shape[1] // n_feat
    heads = HEADS // n_feat
    dims = width // heads
    lanes = -(-width // TILE) * TILE
    src_rows, own_rows = src_feats.shape[0], dst_feats.shape[0]
    slots = tile_rows.shape[2]
    row_tiles = own_rows * n_col // TILE
    piece_tiles = src_rows // TILE
    n_chunk = 2 if piece_tiles % 2 == 0 else 1
    chunk_tiles = piece_tiles // n_chunk
    part_rows = src_rows // n_chunk
    col_tiles = piece_tiles * n_row
    hp = up8(2 * heads)
    mdp = up8(2 * heads)
    att_src2, att_dst2, bias2 = (v.reshape(1, width) for v in (att_src, att_dst, bias))

    def fetch(hbm, vmem, sems):
        copies = [pltpu.make_async_copy(h, v, sems.at[k]) for k, (h, v) in enumerate(zip(hbm, vmem))]
        for copy in copies:
            copy.start()
        for copy in copies:
            copy.wait()

    def fetching(kernel, outs, *args):
        return call(
            kernel,
            outs,
            *map(in_hbm, args),
            in_specs=[HBM] * len(args),
            scratch_shapes=[
                *(pltpu.VMEM(v.shape, v.dtype) for v in args),
                pltpu.SemaphoreType.DMA((len(args),)),
            ],
        )

    def send_kernel(*refs):
        hbm, outs, refs = refs[:4], refs[4:-5], refs[-5:]
        fetch(hbm, refs[:4], refs[4])
        src_ref, dst_ref, proj_ref, att_ref = refs[:4]
        me = lax.axis_index("feat")
        outs[0][...] = project(dst_ref[...], take_cols(proj_ref, me, width))
        outs[1][...] = LOG2E * head_rows(att_ref[...], heads, width, up8(heads))
        for d in range(1, n_feat):
            w = take_cols(proj_ref, goes_to(me, d, n_feat), width)
            own_outs = outs[2 + (d - 1) * (n_chunk + 1) : 2 + d * (n_chunk + 1)]
            own_outs[0][...] = project(dst_ref[...], w)
            for ch in range(n_chunk):
                own_outs[ch + 1][...] = project(src_ref[ch * part_rows : (ch + 1) * part_rows], w)

    dst_own, dst_att, *sent = fetching(
        send_kernel,
        [pltpu.VMEM((own_rows, width), F32), pltpu.VMEM((up8(heads), width), F32)]
        + [
            pltpu.VMEM((n, width), F32)
            for _ in range(1, n_feat)
            for n in [own_rows] + [part_rows] * n_chunk
        ],
        src_feats,
        dst_feats,
        proj,
        att_dst2,
    )
    sent = [sent[k :: n_chunk + 1] for k in range(n_chunk + 1)]
    dst_parts = [hop(sent[0][d - 1], "feat", d) for d in range(1, n_feat)]
    src_parts = [[hop(part[d - 1], "feat", d) for d in range(1, n_feat)] for part in sent[1:]]

    tiles = row_tiles * col_tiles
    whole = lambda shape: pl.BlockSpec(shape, lambda s: (0,) * len(shape))

    def dst_kernel(own_ref, att_ref, *rest):
        got, (z_ref, s_ref) = rest[: n_feat - 1], rest[n_feat - 1 :]
        z = own_ref[...]
        for part in got:
            z = z + part[...]
        z_ref[...] = z
        s_ref[...] = contract(att_ref[...], z, ((1,), (1,)))

    zdst, s_dst = call(
        dst_kernel,
        [
            jax.ShapeDtypeStruct((own_rows, width), F32),
            jax.ShapeDtypeStruct((up8(heads), own_rows), F32),
        ],
        dst_own,
        dst_att,
        *dst_parts,
    )
    rows_of = up8(heads)
    if is_pow2(n_col) and n_col > 1:
        bits = n_col.bit_length() - 1
        place = lambda d: sum(((d >> k) & 1) << (bits - 1 - k) for k in range(bits))
        targets, d = [s_dst], n_col // 2
        while d:
            targets = [targets[0], hop(targets[0], "col", d)]
            d //= 2
            if d:

                def join_kernel(low_ref, high_ref, out_ref):
                    out_ref[...] = jnp.concatenate([low_ref[...], high_ref[...]], axis=0)

                shape = (2 * targets[0].shape[0], own_rows)
                targets = [call(join_kernel, pltpu.VMEM(shape, F32), *targets)]
    else:
        place = lambda d: d
        targets = [s_dst] + [hop(s_dst, "col", d) for d in range(1, n_col)]
    size = n_col // len(targets)

    units = n_row * n_chunk
    period = min(slots, tiles) if slots % min(slots, tiles) == 0 else slots
    reps = slots // period
    group = 8
    groups = period // group
    panel_bytes = 4 * tiles * TILE * TILE
    n_panel = 2 if groups % 2 == 0 and panel_bytes <= 4 << 20 else 1
    share = groups // n_panel

    def weight_sums(first, extra, hbm, small_refs, count_ref, panel_ref, w_ref, sems, w_sems):
        rows_ref, cols_ref = small_refs[-2:]
        small = [
            pltpu.make_async_copy(h, v, sems.at[k]) for k, (h, v) in enumerate(zip(hbm, small_refs))
        ]
        large = [
            pltpu.make_async_copy(
                hbm[-1].at[k, pl.ds((first + g) * group, group)],
                w_ref.at[k, pl.ds(g * group, group)],
                w_sems.at[g, k],
            )
            for g in range(share)
            for k in range(reps)
        ]
        for copy in small + large:
            copy.start()

        @pl.loop(0, units)
        def _(u):
            @pl.loop(0, row_tiles)
            def _(r):
                panel_ref[u, r] = jnp.zeros((chunk_tiles, TILE, TILE), F32)

        for copy in small:
            copy.wait()
        extra()
        row = lax.axis_index("row")
        count = count_ref[0, 0]
        for g in range(share):
            for copy in large[g * reps : (g + 1) * reps]:
                copy.wait()
            base = (first + g) * group

            @pl.loop(base, jnp.clip(count, base, base + group))
            def _(u):
                at = u - first * group
                r, c = rows_ref[0, 0, u], cols_ref[0, 0, u]
                unit = ((c // piece_tiles) ^ row) * n_chunk + c % piece_tiles // chunk_tiles
                t = c % chunk_tiles
                total = w_ref[0, at].astype(F32)
                for k in range(1, reps):
                    live = (u + k * period < count).astype(F32)
                    total = total + w_ref[k, at].astype(F32) * live
                panel_ref[unit, r, t] = panel_ref[unit, r, t] + total

    def local_kernel(*refs):
        hbm, count_ref, refs = refs[:6], refs[6], refs[7:]
        outs, panel_ref, refs = refs[: 1 + n_chunk], refs[1 + n_chunk], refs[2 + n_chunk :]
        src_ref, proj_ref, att_ref = refs[:3]

        def own():
            outs[0][...] = LOG2E * head_rows(att_ref[...], heads, width, hp)
            w = take_cols(proj_ref, lax.axis_index("feat"), width)
            for ch in range(n_chunk):
                outs[1 + ch][...] = project(src_ref[ch * part_rows : (ch + 1) * part_rows], w)

        weight_sums(0, own, hbm, refs[:5], count_ref, panel_ref, *refs[5:])

    def more_kernel(*refs):
        hbm, count_ref, panel_ref, refs = refs[:3], refs[3], refs[4], refs[5:]
        weight_sums(share, lambda: None, hbm, refs[:2], count_ref, panel_ref, *refs[2:])

    def weights(kernel, outs, *inputs):
        return call(
            kernel,
            outs + [pltpu.VMEM((units, row_tiles, chunk_tiles, TILE, TILE), F32)],
            *map(in_hbm, inputs),
            tile_count,
            in_specs=[HBM] * len(inputs) + [SMEM],
            scratch_shapes=[
                *(
                    (pltpu.SMEM if v.dtype == jnp.int32 else pltpu.VMEM)(v.shape, v.dtype)
                    for v in inputs[:-1]
                ),
                pltpu.VMEM((reps, share * group, TILE, TILE), edge_weight.dtype),
                pltpu.SemaphoreType.DMA((len(inputs) - 1,)),
                pltpu.SemaphoreType.DMA((share, reps)),
            ],
            grant=12 << 20,
        )

    slot_weights = edge_weight.reshape(reps, period, TILE, TILE)
    slot_inputs = (tile_rows, tile_cols, slot_weights)
    src_att, *src_own, panel = weights(
        local_kernel,
        [pltpu.VMEM((hp, width), F32)] + [pltpu.VMEM((part_rows, width), F32)] * n_chunk,
        src_feats,
        proj,
        att_src2,
        *slot_inputs,
    )
    panels = [panel]
    if n_panel > 1:
        panels += weights(more_kernel, [], *slot_inputs)

    pack_rows = part_rows + chunk_tiles * hp

    def z_kernel(own_ref, att_ref, *rest):
        got, out_ref = rest[: n_feat - 1], rest[n_feat - 1]
        z = own_ref[...]
        for part in got:
            z = z + part[...]
        if width < lanes:
            out_ref[...] = jnp.zeros_like(out_ref)
        out_ref[:part_rows, :width] = z
        s = contract(att_ref[...], z, ((1,), (1,)))
        low = lax.broadcasted_iota(jnp.int32, s.shape, 0) < heads
        s = jnp.where(low, s, SLOPE * s)
        for t in range(chunk_tiles):
            at = part_rows + t * hp
            out_ref[at : at + hp, :TILE] = s[:, t * TILE : (t + 1) * TILE]

    parts, far_first = {}, n_row // 2
    for ch in range(n_chunk):
        shape = pltpu.VMEM((pack_rows, lanes), F32)
        own = call(z_kernel, shape, src_own[ch], src_att, *src_parts[ch])
        parts[far_first, ch] = hop(own, "row", far_first)
        parts[0, ch] = own

    def spread(first, ch):
        d = n_row // 4
        while d:
            for k in [k for k, c in parts if c == ch and k ^ first < far_first]:
                parts[k ^ d, ch] = hop(parts[k, ch], "row", d)
            d //= 2

    for ch in range(n_chunk):
        spread(0, ch)

    block = 64
    blocks = TILE // block
    unroll = 2 if row_tiles % 2 == 0 else 1
    steps = row_tiles // unroll
    chunk_rows = own_rows + mdp
    group_rows = unroll * TILE
    all_rows = row_tiles * TILE
    tiny, huge = 2.0**-60, 2.0**60
    lane_w = lambda: lax.broadcasted_iota(jnp.int32, (block, width), 1) // dims
    lane_t = lambda: lax.broadcasted_iota(jnp.int32, (block, TILE), 1)

    def score_rows(part_ref, t, h):
        at = part_rows + t * hp + h
        return part_ref[at : at + 1, :TILE], part_ref[at + heads : at + heads + 1, :TILE]

    def panel_sum(refs, rt, t, rows):
        total = refs[0][0, rt, t, rows, :]
        for ref in refs[1:]:
            total = total + ref[0, rt, t, rows, :]
        return total

    def by_unit(refs):
        return [refs[k : k + n_panel] for k in range(0, len(refs), n_panel)]

    def split(x):
        hi = x.astype(BF16)
        return hi, (x - hi.astype(F32)).astype(BF16)

    def split_z(part_refs):
        return jnp.concatenate(
            [jnp.concatenate(split(p[:part_rows, :width]), axis=1) for p in part_refs], axis=0
        )

    def stack(pairs):
        return jnp.concatenate(
            [jnp.concatenate([p[k] for p in row], axis=1) for row in pairs for k in range(2)], axis=0
        )

    def weighted(probs, z):
        both = lax.dot_general(probs, z, (((1,), (0,)), ((), ())), preferred_element_type=F32)
        num = jnp.zeros((block, width), F32)
        for h in range(heads):
            hi = both[2 * h * block : (2 * h + 1) * block]
            lo = both[(2 * h + 1) * block : (2 * h + 2) * block]
            num = jnp.where(lane_w() == h, hi[:, :width] + (hi[:, width:] + lo[:, :width]), num)
        return num

    def attend(part_refs, w_refs, posneg, den_in, num_in, den_out, num_out):
        base = pl.program_id(0) * group_rows
        z_cat = split_z(part_refs)
        for b in range(unroll * blocks):
            at = pl.ds(pl.multiple_of(base + b * block, block), block)
            rt, i0 = divmod(b * block, TILE)
            pairs = []
            for h in range(heads):
                pairs.append([])
                pn = posneg[at, :]
                pos = jnp.broadcast_to(pn[:, h : h + 1], (block, TILE))
                neg = jnp.broadcast_to(pn[:, heads + h : heads + h + 1], (block, TILE))
                den = jnp.zeros((block, TILE), F32) if den_in is None else den_in[h, at, :]
                for k, part_ref in enumerate(part_refs):
                    for t in range(chunk_tiles):
                        s, s_low = score_rows(part_ref, t, h)
                        x = jnp.maximum(pos + s, neg + s_low)
                        p = panel_sum(w_refs[k], rt, t, slice(i0, i0 + block)) * jnp.exp2(x)
                        den = den + p
                        pairs[h].append(split(p))
                den_out[h, at, :] = den
            num = weighted(stack(pairs), z_cat)
            num_out[at, :] = num if num_in is None else num_in[at, :] + num

    shape_t, shape_w, shape_d = (all_rows, TILE), (all_rows, width), (heads, all_rows, TILE)
    part_spec = whole((pack_rows, lanes))

    def unit_spec(k, ch):
        return pl.BlockSpec(
            (1, unroll, chunk_tiles, TILE, TILE), lambda s: (k * n_chunk + ch, s, 0, 0, 0)
        )

    def stage(kernel, keys, before, before_shapes, outs, extra=(), scratch=()):
        n = len(keys)
        return pl.pallas_call(
            kernel,
            out_shape=[pltpu.VMEM(s, F32) for s in outs],
            grid=(steps,),
            in_specs=[whole(s) for s in before_shapes]
            + [part_spec] * (n + len(extra))
            + [unit_spec(*key) for key in (*keys, *extra) for _ in panels],
            out_specs=[whole(s) for s in outs],
            scratch_shapes=scratch,
            cost_estimate=pl.CostEstimate(
                flops=all_rows * n * part_rows * width * heads * 8,
                bytes_accessed=n * part_rows * width * 4,
                transcendentals=all_rows * n * part_rows * heads,
            ),
            compiler_params=pltpu.CompilerParams(vmem_limit_bytes=limit(16, 4 * tiles * TILE * TILE)),
        )(*before, *(parts[key] for key in (*keys, *extra)), *panels * (n + len(extra)))

    near_keys = [(k, ch) for ch in range(n_chunk) for k in range(far_first)]

    def near_kernel(*refs):
        n = len(near_keys)
        n_tgt = len(targets)
        tgt_refs, part_refs, refs = refs[:n_tgt], refs[n_tgt : n_tgt + n], refs[n_tgt + n :]
        w_refs, refs = by_unit(refs[: n * n_panel]), refs[n * n_panel :]
        posneg, tgt_m, den_out, num_out = refs
        col = lax.axis_index("col")

        @pl.when(pl.program_id(0) == 0)
        def _():
            shape = (up8(heads), TILE)
            eye = (
                lax.broadcasted_iota(jnp.int32, shape, 0)
                == lax.broadcasted_iota(jnp.int32, shape, 1) % heads
            ).astype(F32)
            lane = lax.broadcasted_iota(jnp.int32, (1, TILE), 1)
            bound = jnp.zeros((1, TILE), F32)
            for h in range(heads):
                rows = [score_rows(r, t, h)[0] for r in part_refs for t in range(chunk_tiles)]
                top = rows[0]
                for other in rows[1:]:
                    top = jnp.maximum(top, other)
                top = jnp.max(top, axis=1, keepdims=True)
                bound = jnp.where(lane % heads == h, top, bound)
            for d in range(n_col):
                at = pl.ds(
                    pl.multiple_of(comes_from(col, d, n_col) * own_rows, own_rows), own_rows
                )
                k, g = divmod(place(d), size)
                a = contract(tgt_refs[k][g * rows_of : (g + 1) * rows_of], eye, ((0,), (0,)))
                m = leaky(a + bound)
                tgt_m[at, :] = jnp.where(lane < heads, a, m)
                posneg[at, :] = jnp.where(lane < heads, a, SLOPE * a) - m

        attend(part_refs, w_refs, posneg, None, None, den_out, num_out)

    def middle_kernel(*refs):
        n = len(middle_keys)
        (posneg, den_in, num_in), refs = refs[:3], refs[3:]
        part_refs, refs = refs[:n], refs[n:]
        w_refs, (den_out, num_out) = by_unit(refs[: n * n_panel]), refs[n * n_panel :]
        attend(part_refs, w_refs, posneg, den_in, num_in, den_out, num_out)

    def last_kernel(*refs):
        n, n_all = len(last_keys), len(last_keys) + len(other_keys)
        (posneg, den_in, num_in, tgt_m), refs = refs[:4], refs[4:]
        part_refs, refs = refs[:n_all], refs[n_all:]
        w_refs, refs = by_unit(refs[: n_all * n_panel]), refs[n_all * n_panel :]
        out_refs, (den_s, num_s, md_s) = refs[:n_col], refs[n_col:]
        col = lax.axis_index("col")
        step = pl.program_id(0)

        attend(part_refs[:n], w_refs[:n], posneg, den_in, num_in, den_s, num_s)
        base = step * group_rows
        low = high = None
        for b in range(unroll * blocks):
            at = pl.ds(pl.multiple_of(base + b * block, block), block)
            md = tgt_m[at, :]
            for h in range(heads):
                den = jnp.sum(den_s[h, at, :], axis=1, keepdims=True)
                low = den if low is None else jnp.minimum(low, den)
                high = den if high is None else jnp.maximum(high, den)
                md = jnp.where(lane_t() == h, den, md)
            md_s[at, :] = md
        fine = jnp.logical_and(jnp.min(low) >= tiny, jnp.max(high) <= huge)

        @pl.when(jnp.logical_not(fine))
        def _():
            @pl.loop(0, unroll * blocks)
            def _(b):
                at = pl.ds(pl.multiple_of(base + b * block, block), block)
                rt = b // blocks
                rows = pl.ds(pl.multiple_of((b % blocks) * block, block), block)
                md = tgt_m[at, :]
                posnegs, dens = [], []
                for h in range(heads):
                    best = jnp.full((block, TILE), NEG, F32)
                    for part_ref, w_ref in zip(part_refs, w_refs):
                        for t in range(chunk_tiles):
                            edge = panel_sum(w_ref, rt, t, rows) > 0
                            s = score_rows(part_ref, t, h)[0]
                            best = jnp.maximum(best, jnp.where(edge, s, NEG))
                    a = tgt_m[at, :][:, h : h + 1]
                    m = leaky(a + jnp.max(best, axis=1, keepdims=True))
                    md = jnp.where(lane_t() == heads + h, m, md)
                    posnegs.append((a - m, SLOPE * a - m))
                    dens.append(jnp.zeros((block, TILE), F32))
                num_s[at, :] = jnp.zeros((block, width), F32)
                for part_ref, w_ref in zip(part_refs, w_refs):
                    pairs = []
                    for h in range(heads):
                        pairs.append([])
                        pos, neg = posnegs[h]
                        for t in range(chunk_tiles):
                            s, s_low = score_rows(part_ref, t, h)
                            x = jnp.minimum(jnp.maximum(pos + s, neg + s_low), 0.0)
                            p = panel_sum(w_ref, rt, t, rows) * jnp.exp2(x)
                            dens[h] = dens[h] + p
                            pairs[h].append(split(p))
                    num_s[at, :] = num_s[at, :] + weighted(stack(pairs), split_z([part_ref]))
                for h in range(heads):
                    md = jnp.where(lane_t() == h, jnp.sum(dens[h], axis=1, keepdims=True), md)
                md_s[at, :] = md

        @pl.when(step == steps - 1)
        def _():
            for d in range(n_col):
                at = pl.ds(
                    pl.multiple_of(goes_to(col, d, n_col) * own_rows, own_rows), own_rows
                )
                if width < lanes:
                    out_refs[d][...] = jnp.zeros_like(out_refs[d])
                out_refs[d][:own_rows, :width] = num_s[at, :]
                out_refs[d][own_rows:, :own_rows] = md_s[at, :].T[:mdp]

    posneg, tgt_m, den, num = stage(
        near_kernel,
        near_keys,
        targets,
        [(size * rows_of, own_rows)] * len(targets),
        [shape_t, shape_t, shape_d, shape_w],
    )
    arrived = [parts[far_first, ch] for ch in range(n_chunk)]
    arrived, den = lax.optimization_barrier((arrived, den))
    for ch in range(n_chunk):
        parts[far_first, ch] = arrived[ch]
        spread(far_first, ch)
    far_keys = [(k, ch) for k in range(far_first, n_row) for ch in range(n_chunk)]
    middle_keys = far_keys[:n_chunk] if n_row > 2 else []
    if middle_keys:
        den, num = stage(
            middle_kernel,
            middle_keys,
            (posneg, den, num),
            [shape_t, shape_d, shape_w],
            [shape_d, shape_w],
        )
    last_keys = far_keys[len(middle_keys) :]
    other_keys = near_keys + middle_keys
    chunks = stage(
        last_kernel,
        last_keys,
        (posneg, den, num, tgt_m),
        [shape_t, shape_d, shape_w, shape_t],
        [(chunk_rows, lanes)] * n_col,
        extra=other_keys,
        scratch=[
            pltpu.VMEM(shape_d, F32),
            pltpu.VMEM(shape_w, F32),
            pltpu.VMEM(shape_t, F32),
        ],
    )
    gathered = [hop(chunks[d], "col", d) for d in range(n_col - 1, 0, -1)]
    gathered = [chunks[0]] + gathered[::-1]

    def out_kernel(zdst_ref, src_ref, dst_ref, bias_ref, *rest):
        parts, out_ref = rest[:n_col], rest[n_col]
        same = (
            lax.broadcasted_iota(jnp.int32, (width, width), 0) // dims
            == lax.broadcasted_iota(jnp.int32, (width, width), 1) // dims
        ).astype(F32)
        z = zdst_ref[...]
        pair = contract(z * (dst_ref[...] + src_ref[...]), same, ((1,), (0,)))
        e_self = leaky(LOG2E * pair)
        which = lax.broadcasted_iota(jnp.int32, (mdp, width), 0)
        head = lax.broadcasted_iota(jnp.int32, (mdp, width), 1) // dims
        den_of, m_of = (which == head).astype(F32), (which == head + heads).astype(F32)
        mds = [part[own_rows:, :own_rows] for part in parts]
        ms = [contract(md, m_of, ((0,), (0,))) for md in mds]
        dens = [contract(md, den_of, ((0,), (0,))) for md in mds]
        top = e_self
        for m in ms:
            top = jnp.maximum(top, m)
        den = jnp.exp2(e_self - top)
        num = den * z
        for part, m, own_den in zip(parts, ms, dens):
            factor = jnp.exp2(m - top)
            den = den + factor * own_den
            num = num + factor * part[:own_rows, :width]
        x = num / den + bias_ref[...]
        out_ref[...] = jnp.where(x > 0, x, jnp.exp(jnp.minimum(x, 0.0)) - 1.0).astype(BF16)

    return call(
        out_kernel,
        jax.ShapeDtypeStruct((own_rows, width), BF16),
        zdst,
        att_src2,
        att_dst2,
        bias2,
        *gathered,
    )


def solution(mesh):
    return jax.shard_map(
        on_device,
        mesh=mesh,
        in_specs=(
            P(("row", "col"), "feat"),
            P(("row", "col"), "feat"),
            P("feat", None),
            P("feat"),
            P("feat"),
            P("feat"),
            P("row", "col", None),
            P("row", "col", None),
            P("row", "col"),
            P("row", "col", None, None, None),
        ),
        out_specs=P(("row", "col"), "feat"),
        check_vma=False,
    )
```

```python
import jax
import jax.numpy as jnp
from jax import lax
from jax.experimental import pallas as pl
from jax.experimental.pallas import tpu as pltpu
from jax.sharding import PartitionSpec as P

HEADS = 8
TILE = 128
SLOPE = 0.2
LOG2E = 1.4426950408889634
NEG = -1e30
F32 = jnp.float32
BF16 = jnp.bfloat16
HIGHEST = lax.Precision.HIGHEST
VMEM = pl.BlockSpec(memory_space=pltpu.VMEM)
SMEM = pl.BlockSpec(memory_space=pltpu.SMEM)
HBM = pl.BlockSpec(memory_space=pltpu.HBM)


def is_pow2(n):
    return n & (n - 1) == 0


def goes_to(i, d, n):
    return i ^ d if is_pow2(n) else lax.rem(i + d, n)


def comes_from(i, d, n):
    return i ^ d if is_pow2(n) else lax.rem(i + n - d, n)


def hop(x, axis, d):
    n = lax.axis_size(axis)
    pairs = [(i, i ^ d if is_pow2(n) else (i + d) % n) for i in range(n)]
    return lax.ppermute(x, axis, pairs)


def call(kernel, out_shape, *args, in_specs=None, flops=0, bytes_accessed=0, grant=8 << 20, **kw):
    return pl.pallas_call(
        kernel,
        out_shape=out_shape,
        in_specs=in_specs or [VMEM] * len(args),
        cost_estimate=pl.CostEstimate(
            flops=flops, bytes_accessed=bytes_accessed, transcendentals=0
        ),
        compiler_params=pltpu.CompilerParams(vmem_limit_bytes=grant),
        **kw,
    )(*args)


def limit(mib, least):
    return min(max(mib << 20, least), 60 << 20)


def in_hbm(x):
    return pltpu.with_memory_space_constraint(x, pltpu.HBM)


def up8(n):
    return -(-n // 8) * 8


def head_rows(vector, heads, width, height):
    dims = width // heads
    shape = (height, width)
    row = lax.broadcasted_iota(jnp.int32, shape, 0) % heads
    lane = lax.broadcasted_iota(jnp.int32, shape, 1)
    return jnp.where(lane // dims == row, jnp.broadcast_to(vector, shape), 0.0)


def contract(lhs, rhs, dims, precision=HIGHEST):
    return lax.dot_general(
        lhs, rhs, (dims, ((), ())), preferred_element_type=F32, precision=precision
    )


def take_cols(proj_ref, which, width):
    if width % TILE == 0:
        return proj_ref[:, pl.ds(pl.multiple_of(which * width, width), width)]
    full = proj_ref[...]
    out = full[:, :width]
    for k in range(1, full.shape[1] // width):
        out = jnp.where(which == k, full[:, k * width : (k + 1) * width], out)
    return out


def project(x, w):
    return lax.dot_general(x, w, (((1,), (0,)), ((), ())), preferred_element_type=F32)


def leaky(x):
    return jnp.maximum(x, SLOPE * x)


def on_device(
    src_feats, dst_feats, proj, att_src, att_dst, bias, tile_rows, tile_cols, tile_count, edge_weight
):
    n_row, n_col, n_feat = (lax.axis_size(a) for a in ("row", "col", "feat"))
    width = proj.shape[1] // n_feat
    heads = HEADS // n_feat
    dims = width // heads
    lanes = -(-width // TILE) * TILE
    src_rows, own_rows = src_feats.shape[0], dst_feats.shape[0]
    slots = tile_rows.shape[2]
    row_tiles = own_rows * n_col // TILE
    piece_tiles = src_rows // TILE
    n_chunk = 2 if piece_tiles % 2 == 0 else 1
    chunk_tiles = piece_tiles // n_chunk
    part_rows = src_rows // n_chunk
    col_tiles = piece_tiles * n_row
    hp = up8(2 * heads)
    mdp = up8(2 * heads)
    att_src2, att_dst2, bias2 = (v.reshape(1, width) for v in (att_src, att_dst, bias))

    def fetch(hbm, vmem, sems):
        copies = [pltpu.make_async_copy(h, v, sems.at[k]) for k, (h, v) in enumerate(zip(hbm, vmem))]
        for copy in copies:
            copy.start()
        for copy in copies:
            copy.wait()

    def fetching(kernel, outs, *args):
        return call(
            kernel,
            outs,
            *map(in_hbm, args),
            in_specs=[HBM] * len(args),
            scratch_shapes=[
                *(pltpu.VMEM(v.shape, v.dtype) for v in args),
                pltpu.SemaphoreType.DMA((len(args),)),
            ],
        )

    def send_kernel(*refs):
        hbm, outs, refs = refs[:4], refs[4:-5], refs[-5:]
        fetch(hbm, refs[:4], refs[4])
        src_ref, dst_ref, proj_ref, att_ref = refs[:4]
        me = lax.axis_index("feat")
        outs[0][...] = project(dst_ref[...], take_cols(proj_ref, me, width))
        outs[1][...] = LOG2E * head_rows(att_ref[...], heads, width, up8(heads))
        for d in range(1, n_feat):
            w = take_cols(proj_ref, goes_to(me, d, n_feat), width)
            own_outs = outs[2 + (d - 1) * (n_chunk + 1) : 2 + d * (n_chunk + 1)]
            own_outs[0][...] = project(dst_ref[...], w)
            for ch in range(n_chunk):
                own_outs[ch + 1][...] = project(src_ref[ch * part_rows : (ch + 1) * part_rows], w)

    dst_own, dst_att, *sent = fetching(
        send_kernel,
        [pltpu.VMEM((own_rows, width), F32), pltpu.VMEM((up8(heads), width), F32)]
        + [
            pltpu.VMEM((n, width), F32)
            for _ in range(1, n_feat)
            for n in [own_rows] + [part_rows] * n_chunk
        ],
        src_feats,
        dst_feats,
        proj,
        att_dst2,
    )
    sent = [sent[k :: n_chunk + 1] for k in range(n_chunk + 1)]
    dst_parts = [hop(sent[0][d - 1], "feat", d) for d in range(1, n_feat)]
    src_parts = [[hop(part[d - 1], "feat", d) for d in range(1, n_feat)] for part in sent[1:]]

    tiles = row_tiles * col_tiles
    whole = lambda shape: pl.BlockSpec(shape, lambda s: (0,) * len(shape))

    def dst_kernel(own_ref, att_ref, _, *rest):
        got, (z_ref, s_ref) = rest[: n_feat - 1], rest[n_feat - 1 :]
        z = own_ref[...]
        for part in got:
            z = z + part[...]
        z_ref[...] = z
        s_ref[...] = contract(att_ref[...], z, ((1,), (1,)))

    zdst, s_dst = call(
        dst_kernel,
        [
            jax.ShapeDtypeStruct((own_rows, width), F32),
            jax.ShapeDtypeStruct((up8(heads), own_rows), F32),
        ],
        dst_own,
        dst_att,
        tile_count,
        *dst_parts,
        in_specs=[VMEM, VMEM, SMEM] + [VMEM] * len(dst_parts),
    )
    rows_of = up8(heads)
    if is_pow2(n_col) and n_col > 1:
        bits = n_col.bit_length() - 1
        place = lambda d: sum(((d >> k) & 1) << (bits - 1 - k) for k in range(bits))
        targets, d = [s_dst], n_col // 2
        while d:
            targets = [targets[0], hop(targets[0], "col", d)]
            d //= 2
            if d:

                def join_kernel(low_ref, high_ref, out_ref):
                    out_ref[...] = jnp.concatenate([low_ref[...], high_ref[...]], axis=0)

                shape = (2 * targets[0].shape[0], own_rows)
                targets = [call(join_kernel, pltpu.VMEM(shape, F32), *targets)]
    else:
        place = lambda d: d
        targets = [s_dst] + [hop(s_dst, "col", d) for d in range(1, n_col)]
    size = n_col // len(targets)

    units = n_row * n_chunk
    period = min(slots, tiles) if slots % min(slots, tiles) == 0 else slots
    reps = slots // period
    group = 8
    groups = period // group
    panel_bytes = 4 * tiles * TILE * TILE
    n_panel = 2 if groups % 2 == 0 and panel_bytes <= 4 << 20 else 1
    share = groups // n_panel

    def weight_sums(first, extra, hbm, small_refs, count_ref, panel_ref, w_ref, sems, w_sems):
        rows_ref, cols_ref = small_refs[-2:]
        small = [
            pltpu.make_async_copy(h, v, sems.at[k]) for k, (h, v) in enumerate(zip(hbm, small_refs))
        ]
        large = [
            pltpu.make_async_copy(
                hbm[-1].at[k, pl.ds((first + g) * group, group)],
                w_ref.at[k, pl.ds(g * group, group)],
                w_sems.at[g, k],
            )
            for g in range(share)
            for k in range(reps)
        ]
        for copy in small + large:
            copy.start()

        @pl.loop(0, units)
        def _(u):
            @pl.loop(0, row_tiles)
            def _(r):
                panel_ref[u, r] = jnp.zeros((chunk_tiles, TILE, TILE), F32)

        for copy in small:
            copy.wait()
        extra()
        row = lax.axis_index("row")
        count = count_ref[0, 0]
        for g in range(share):
            for copy in large[g * reps : (g + 1) * reps]:
                copy.wait()
            base = (first + g) * group

            @pl.loop(base, jnp.clip(count, base, base + group))
            def _(u):
                at = u - first * group
                r, c = rows_ref[0, 0, u], cols_ref[0, 0, u]
                unit = ((c // piece_tiles) ^ row) * n_chunk + c % piece_tiles // chunk_tiles
                t = c % chunk_tiles
                total = w_ref[0, at].astype(F32)
                for k in range(1, reps):
                    live = (u + k * period < count).astype(F32)
                    total = total + w_ref[k, at].astype(F32) * live
                panel_ref[unit, r, t] = panel_ref[unit, r, t] + total

    def local_kernel(*refs):
        hbm, count_ref, refs = refs[:6], refs[6], refs[7:]
        outs, panel_ref, refs = refs[: 1 + n_chunk], refs[1 + n_chunk], refs[2 + n_chunk :]
        src_ref, proj_ref, att_ref = refs[:3]

        def own():
            outs[0][...] = LOG2E * head_rows(att_ref[...], heads, width, hp)
            w = take_cols(proj_ref, lax.axis_index("feat"), width)
            for ch in range(n_chunk):
                outs[1 + ch][...] = project(src_ref[ch * part_rows : (ch + 1) * part_rows], w)

        weight_sums(0, own, hbm, refs[:5], count_ref, panel_ref, *refs[5:])

    def more_kernel(*refs):
        hbm, count_ref, panel_ref, refs = refs[:3], refs[3], refs[4], refs[5:]
        weight_sums(share, lambda: None, hbm, refs[:2], count_ref, panel_ref, *refs[2:])

    def weights(kernel, outs, *inputs):
        return call(
            kernel,
            outs + [pltpu.VMEM((units, row_tiles, chunk_tiles, TILE, TILE), F32)],
            *map(in_hbm, inputs),
            tile_count,
            in_specs=[HBM] * len(inputs) + [SMEM],
            scratch_shapes=[
                *(
                    (pltpu.SMEM if v.dtype == jnp.int32 else pltpu.VMEM)(v.shape, v.dtype)
                    for v in inputs[:-1]
                ),
                pltpu.VMEM((reps, share * group, TILE, TILE), edge_weight.dtype),
                pltpu.SemaphoreType.DMA((len(inputs) - 1,)),
                pltpu.SemaphoreType.DMA((share, reps)),
            ],
            grant=12 << 20,
        )

    slot_weights = edge_weight.reshape(reps, period, TILE, TILE)
    slot_inputs = (tile_rows, tile_cols, slot_weights)
    src_att, *src_own, panel = weights(
        local_kernel,
        [pltpu.VMEM((hp, width), F32)] + [pltpu.VMEM((part_rows, width), F32)] * n_chunk,
        src_feats,
        proj,
        att_src2,
        *slot_inputs,
    )
    panels = [panel]
    if n_panel > 1:
        panels += weights(more_kernel, [], *slot_inputs)

    pack_rows = part_rows + chunk_tiles * hp

    def z_kernel(own_ref, att_ref, *rest):
        got, out_ref = rest[: n_feat - 1], rest[n_feat - 1]
        z = own_ref[...]
        for part in got:
            z = z + part[...]
        if width < lanes:
            out_ref[...] = jnp.zeros_like(out_ref)
        out_ref[:part_rows, :width] = z
        s = contract(att_ref[...], z, ((1,), (1,)))
        low = lax.broadcasted_iota(jnp.int32, s.shape, 0) < heads
        s = jnp.where(low, s, SLOPE * s)
        for t in range(chunk_tiles):
            at = part_rows + t * hp
            out_ref[at : at + hp, :TILE] = s[:, t * TILE : (t + 1) * TILE]

    parts, far_first = {}, n_row // 2
    for ch in range(n_chunk):
        shape = pltpu.VMEM((pack_rows, lanes), F32)
        own = call(z_kernel, shape, src_own[ch], src_att, *src_parts[ch])
        parts[far_first, ch] = hop(own, "row", far_first)
        parts[0, ch] = own

    def spread(first, ch):
        d = n_row // 4
        while d:
            for k in [k for k, c in parts if c == ch and k ^ first < far_first]:
                parts[k ^ d, ch] = hop(parts[k, ch], "row", d)
            d //= 2

    for ch in range(n_chunk):
        spread(0, ch)

    block = 64
    blocks = TILE // block
    unroll = 2 if row_tiles % 2 == 0 else 1
    steps = row_tiles // unroll
    chunk_rows = own_rows + mdp
    group_rows = unroll * TILE
    all_rows = row_tiles * TILE
    tiny, huge = 2.0**-60, 2.0**60
    lane_w = lambda: lax.broadcasted_iota(jnp.int32, (block, width), 1) // dims
    lane_t = lambda: lax.broadcasted_iota(jnp.int32, (block, TILE), 1)

    def score_rows(part_ref, t, h):
        at = part_rows + t * hp + h
        return part_ref[at : at + 1, :TILE], part_ref[at + heads : at + heads + 1, :TILE]

    def panel_sum(refs, rt, t, rows):
        total = refs[0][0, rt, t, rows, :]
        for ref in refs[1:]:
            total = total + ref[0, rt, t, rows, :]
        return total

    def by_unit(refs):
        return [refs[k : k + n_panel] for k in range(0, len(refs), n_panel)]

    def split(x):
        hi = x.astype(BF16)
        return hi, (x - hi.astype(F32)).astype(BF16)

    def split_z(part_refs):
        return jnp.concatenate(
            [jnp.concatenate(split(p[:part_rows, :width]), axis=1) for p in part_refs], axis=0
        )

    def stack(pairs):
        return jnp.concatenate(
            [jnp.concatenate([p[k] for p in row], axis=1) for row in pairs for k in range(2)], axis=0
        )

    def weighted(probs, z):
        both = lax.dot_general(probs, z, (((1,), (0,)), ((), ())), preferred_element_type=F32)
        num = jnp.zeros((block, width), F32)
        for h in range(heads):
            hi = both[2 * h * block : (2 * h + 1) * block]
            lo = both[(2 * h + 1) * block : (2 * h + 2) * block]
            num = jnp.where(lane_w() == h, hi[:, :width] + (hi[:, width:] + lo[:, :width]), num)
        return num

    def attend(part_refs, w_refs, posneg, den_in, num_in, den_out, num_out):
        base = pl.program_id(0) * group_rows
        z_cat = split_z(part_refs)
        for b in range(unroll * blocks):
            at = pl.ds(pl.multiple_of(base + b * block, block), block)
            rt, i0 = divmod(b * block, TILE)
            pairs = []
            for h in range(heads):
                pairs.append([])
                pn = posneg[at, :]
                pos = jnp.broadcast_to(pn[:, h : h + 1], (block, TILE))
                neg = jnp.broadcast_to(pn[:, heads + h : heads + h + 1], (block, TILE))
                den = jnp.zeros((block, TILE), F32) if den_in is None else den_in[h, at, :]
                for k, part_ref in enumerate(part_refs):
                    for t in range(chunk_tiles):
                        s, s_low = score_rows(part_ref, t, h)
                        x = jnp.maximum(pos + s, neg + s_low)
                        p = panel_sum(w_refs[k], rt, t, slice(i0, i0 + block)) * jnp.exp2(x)
                        den = den + p
                        pairs[h].append(split(p))
                den_out[h, at, :] = den
            num = weighted(stack(pairs), z_cat)
            num_out[at, :] = num if num_in is None else num_in[at, :] + num

    shape_t, shape_w, shape_d = (all_rows, TILE), (all_rows, width), (heads, all_rows, TILE)
    part_spec = whole((pack_rows, lanes))

    def unit_spec(k, ch):
        return pl.BlockSpec(
            (1, unroll, chunk_tiles, TILE, TILE), lambda s: (k * n_chunk + ch, s, 0, 0, 0)
        )

    def stage(kernel, keys, before, before_shapes, outs, extra=(), scratch=()):
        n = len(keys)
        return pl.pallas_call(
            kernel,
            out_shape=[pltpu.VMEM(s, F32) for s in outs],
            grid=(steps,),
            in_specs=[whole(s) for s in before_shapes]
            + [part_spec] * (n + len(extra))
            + [unit_spec(*key) for key in (*keys, *extra) for _ in panels],
            out_specs=[whole(s) for s in outs],
            scratch_shapes=scratch,
            cost_estimate=pl.CostEstimate(
                flops=all_rows * n * part_rows * width * heads * 8,
                bytes_accessed=n * part_rows * width * 4,
                transcendentals=all_rows * n * part_rows * heads,
            ),
            compiler_params=pltpu.CompilerParams(vmem_limit_bytes=limit(16, 4 * tiles * TILE * TILE)),
        )(*before, *(parts[key] for key in (*keys, *extra)), *panels * (n + len(extra)))

    near_keys = [(k, ch) for ch in range(n_chunk) for k in range(far_first)]

    def near_kernel(*refs):
        n = len(near_keys)
        n_tgt = len(targets)
        tgt_refs, part_refs, refs = refs[:n_tgt], refs[n_tgt : n_tgt + n], refs[n_tgt + n :]
        w_refs, refs = by_unit(refs[: n * n_panel]), refs[n * n_panel :]
        posneg, tgt_m, den_out, num_out = refs
        col = lax.axis_index("col")

        @pl.when(pl.program_id(0) == 0)
        def _():
            shape = (up8(heads), TILE)
            eye = (
                lax.broadcasted_iota(jnp.int32, shape, 0)
                == lax.broadcasted_iota(jnp.int32, shape, 1) % heads
            ).astype(F32)
            lane = lax.broadcasted_iota(jnp.int32, (1, TILE), 1)
            bound = jnp.zeros((1, TILE), F32)
            for h in range(heads):
                rows = [score_rows(r, t, h)[0] for r in part_refs for t in range(chunk_tiles)]
                top = rows[0]
                for other in rows[1:]:
                    top = jnp.maximum(top, other)
                top = jnp.max(top, axis=1, keepdims=True)
                bound = jnp.where(lane % heads == h, top, bound)
            for d in range(n_col):
                at = pl.ds(
                    pl.multiple_of(comes_from(col, d, n_col) * own_rows, own_rows), own_rows
                )
                k, g = divmod(place(d), size)
                a = contract(tgt_refs[k][g * rows_of : (g + 1) * rows_of], eye, ((0,), (0,)))
                m = leaky(a + bound)
                tgt_m[at, :] = jnp.where(lane < heads, a, m)
                posneg[at, :] = jnp.where(lane < heads, a, SLOPE * a) - m

        attend(part_refs, w_refs, posneg, None, None, den_out, num_out)

    def middle_kernel(*refs):
        n = len(middle_keys)
        (posneg, den_in, num_in), refs = refs[:3], refs[3:]
        part_refs, refs = refs[:n], refs[n:]
        w_refs, (den_out, num_out) = by_unit(refs[: n * n_panel]), refs[n * n_panel :]
        attend(part_refs, w_refs, posneg, den_in, num_in, den_out, num_out)

    def last_kernel(*refs):
        n, n_all = len(last_keys), len(last_keys) + len(other_keys)
        (posneg, den_in, num_in, tgt_m), refs = refs[:4], refs[4:]
        part_refs, refs = refs[:n_all], refs[n_all:]
        w_refs, refs = by_unit(refs[: n_all * n_panel]), refs[n_all * n_panel :]
        out_refs, (den_s, num_s, md_s) = refs[:n_col], refs[n_col:]
        col = lax.axis_index("col")
        step = pl.program_id(0)

        attend(part_refs[:n], w_refs[:n], posneg, den_in, num_in, den_s, num_s)
        base = step * group_rows
        low = high = None
        for b in range(unroll * blocks):
            at = pl.ds(pl.multiple_of(base + b * block, block), block)
            md = tgt_m[at, :]
            for h in range(heads):
                den = jnp.sum(den_s[h, at, :], axis=1, keepdims=True)
                low = den if low is None else jnp.minimum(low, den)
                high = den if high is None else jnp.maximum(high, den)
                md = jnp.where(lane_t() == h, den, md)
            md_s[at, :] = md
        fine = jnp.logical_and(jnp.min(low) >= tiny, jnp.max(high) <= huge)

        @pl.when(jnp.logical_not(fine))
        def _():
            @pl.loop(0, unroll * blocks)
            def _(b):
                at = pl.ds(pl.multiple_of(base + b * block, block), block)
                rt = b // blocks
                rows = pl.ds(pl.multiple_of((b % blocks) * block, block), block)
                md = tgt_m[at, :]
                posnegs, dens = [], []
                for h in range(heads):
                    best = jnp.full((block, TILE), NEG, F32)
                    for part_ref, w_ref in zip(part_refs, w_refs):
                        for t in range(chunk_tiles):
                            edge = panel_sum(w_ref, rt, t, rows) > 0
                            s = score_rows(part_ref, t, h)[0]
                            best = jnp.maximum(best, jnp.where(edge, s, NEG))
                    a = tgt_m[at, :][:, h : h + 1]
                    m = leaky(a + jnp.max(best, axis=1, keepdims=True))
                    md = jnp.where(lane_t() == heads + h, m, md)
                    posnegs.append((a - m, SLOPE * a - m))
                    dens.append(jnp.zeros((block, TILE), F32))
                num_s[at, :] = jnp.zeros((block, width), F32)
                for part_ref, w_ref in zip(part_refs, w_refs):
                    pairs = []
                    for h in range(heads):
                        pairs.append([])
                        pos, neg = posnegs[h]
                        for t in range(chunk_tiles):
                            s, s_low = score_rows(part_ref, t, h)
                            x = jnp.minimum(jnp.maximum(pos + s, neg + s_low), 0.0)
                            p = panel_sum(w_ref, rt, t, rows) * jnp.exp2(x)
                            dens[h] = dens[h] + p
                            pairs[h].append(split(p))
                    num_s[at, :] = num_s[at, :] + weighted(stack(pairs), split_z([part_ref]))
                for h in range(heads):
                    md = jnp.where(lane_t() == h, jnp.sum(dens[h], axis=1, keepdims=True), md)
                md_s[at, :] = md

        @pl.when(step == steps - 1)
        def _():
            for d in range(n_col):
                at = pl.ds(
                    pl.multiple_of(goes_to(col, d, n_col) * own_rows, own_rows), own_rows
                )
                if width < lanes:
                    out_refs[d][...] = jnp.zeros_like(out_refs[d])
                out_refs[d][:own_rows, :width] = num_s[at, :]
                out_refs[d][own_rows:, :own_rows] = md_s[at, :].T[:mdp]

    posneg, tgt_m, den, num = stage(
        near_kernel,
        near_keys,
        targets,
        [(size * rows_of, own_rows)] * len(targets),
        [shape_t, shape_t, shape_d, shape_w],
    )
    arrived = [parts[far_first, ch] for ch in range(n_chunk)]
    arrived, den = lax.optimization_barrier((arrived, den))
    for ch in range(n_chunk):
        parts[far_first, ch] = arrived[ch]
        spread(far_first, ch)
    far_keys = [(k, ch) for k in range(far_first, n_row) for ch in range(n_chunk)]
    middle_keys = far_keys[:n_chunk] if n_row > 2 else []
    if middle_keys:
        den, num = stage(
            middle_kernel,
            middle_keys,
            (posneg, den, num),
            [shape_t, shape_d, shape_w],
            [shape_d, shape_w],
        )
    last_keys = far_keys[len(middle_keys) :]
    other_keys = near_keys + middle_keys
    chunks = stage(
        last_kernel,
        last_keys,
        (posneg, den, num, tgt_m),
        [shape_t, shape_d, shape_w, shape_t],
        [(chunk_rows, lanes)] * n_col,
        extra=other_keys,
        scratch=[
            pltpu.VMEM(shape_d, F32),
            pltpu.VMEM(shape_w, F32),
            pltpu.VMEM(shape_t, F32),
        ],
    )
    gathered = [hop(chunks[d], "col", d) for d in range(n_col - 1, 0, -1)]
    gathered = [chunks[0]] + gathered[::-1]

    def out_kernel(zdst_ref, src_ref, dst_ref, bias_ref, *rest):
        parts, out_ref = rest[:n_col], rest[n_col]
        same = (
            lax.broadcasted_iota(jnp.int32, (width, width), 0) // dims
            == lax.broadcasted_iota(jnp.int32, (width, width), 1) // dims
        ).astype(F32)
        z = zdst_ref[...]
        pair = contract(z * (dst_ref[...] + src_ref[...]), same, ((1,), (0,)))
        e_self = leaky(LOG2E * pair)
        which = lax.broadcasted_iota(jnp.int32, (mdp, 2 * width), 0)
        lane = lax.broadcasted_iota(jnp.int32, (mdp, 2 * width), 1)
        pick = (which == jnp.where(lane < width, heads + lane // dims, (lane - width) // dims)).astype(F32)
        mds = [part[own_rows:, :own_rows] for part in parts]
        both = [contract(md, pick, ((0,), (0,))) for md in mds]
        ms, dens = [b[:, :width] for b in both], [b[:, width:] for b in both]
        top = e_self
        for m in ms:
            top = jnp.maximum(top, m)
        den = jnp.exp2(e_self - top)
        num = den * z
        for part, m, own_den in zip(parts, ms, dens):
            factor = jnp.exp2(m - top)
            den = den + factor * own_den
            num = num + factor * part[:own_rows, :width]
        x = num / den + bias_ref[...]
        out_ref[...] = jnp.where(x > 0, x, jnp.exp(jnp.minimum(x, 0.0)) - 1.0).astype(BF16)

    return call(
        out_kernel,
        jax.ShapeDtypeStruct((own_rows, width), BF16),
        zdst,
        att_src2,
        att_dst2,
        bias2,
        *gathered,
    )


def solution(mesh):
    return jax.shard_map(
        on_device,
        mesh=mesh,
        in_specs=(
            P(("row", "col"), "feat"),
            P(("row", "col"), "feat"),
            P("feat", None),
            P("feat"),
            P("feat"),
            P("feat"),
            P("row", "col", None),
            P("row", "col", None),
            P("row", "col"),
            P("row", "col", None, None, None),
        ),
        out_specs=P(("row", "col"), "feat"),
        check_vma=False,
    )
```
